32 devices in a mesh: dp: 16 (over z, y, x), tensor: 2 (over core).
Axes of the slice: x: 2, y: 2, z: 4, core: 2. Of those that a mesh axis runs over, the one named last changes fastest.
Arguments:
- tokens: bfloat16 [2048, 768], P('dp'), may hold values from -6 to 6
- seq_ids: int32 [2048], P('dp'), may hold values from 0 to 127, as said below
- routes: int32 [2048, 2], P('dp'), may hold values from 0 to 3, all different within a row; in each aligned block of 128 rows (0 to 127, 128 to 255, ...) at most 80 rows name the same one
- gain_attn: float32 [768], replicated, may hold values from 0.25 to 1.75
- w_query: bfloat16 [768, 768], P(None, 'tensor'), may hold values from -0.21875 to 0.21875
- w_key: bfloat16 [768, 768], P(None, 'tensor'), may hold values from -0.21875 to 0.21875
- w_value: bfloat16 [768, 768], P(None, 'tensor'), may hold values from -0.21875 to 0.21875
- w_attn_out: bfloat16 [768, 768], P('tensor'), may hold values from -0.625 to 0.625
- rel_bias: float32 [12, 32], P('tensor'), may hold values from -2.5 to 2.5
- gain_ffn: float32 [768], replicated, may hold values from 0.25 to 1.75
- w_router: bfloat16 [768, 4], replicated, may hold values from -0.145 to 0.145
- expert_in: bfloat16 [16, 768, 768], P('dp', None, 'tensor'), may hold values from -0.21875 to 0.21875
- expert_out: bfloat16 [16, 768, 768], P('dp', 'tensor'), may hold values from -1.75 to 1.75
- cotangent: bfloat16 [2048, 768], P('dp'), may hold values from -6 to 6
Outputs:
- output: bfloat16 [2048, 768], P('dp')
- grad_tokens: float32 [2048, 768], P('dp')
- grad_gain_attn: float32 [768], replicated
- grad_w_query: float32 [768, 768], P(None, 'tensor')
- grad_w_key: float32 [768, 768], P(None, 'tensor')
- grad_w_value: float32 [768, 768], P(None, 'tensor')
- grad_w_attn_out: float32 [768, 768], P('tensor')
- grad_rel_bias: float32 [12, 32], P('tensor')
- grad_gain_ffn: float32 [768], replicated
- grad_w_router: float32 [768, 4], replicated
- grad_expert_in: float32 [16, 768, 768], P('dp', None, 'tensor')
- grad_expert_out: float32 [16, 768, 768], P('dp', 'tensor')
The draws below stay inside these ranges and needn't reach their ends.
Inputs may be any that keep to these rules, and one draw needn't show every extreme that they name: `seq_ids`: in each device's 128 rows the sequence number starts at 0 and rises by 0 or 1 from row to row; equal numbers form one sequence; in every draw some device holds a single sequence of 128 rows, and some device holds 128 sequences of one row. `routes`: the 2 experts of a row differ; within the 128 rows of one device no expert is named more than 80 times, and in every draw some expert is named exactly 80 times there.
All inputs are finite; a program needn't handle non-finite values.
Results may differ from the reference program's by a relative error of at most 0.017.
Values may be sent and summed in bfloat16 or wider, within the bound.
No kernel may reach another device: no remote copies, remote signals or barrier semaphores. Data moves between devices by JAX's collectives and lax.ppermute only.
A program may use at most 128 MiB of HBM per device.

```python
import math
import jax
import jax.numpy as jnp
import numpy as np
from jax import lax

D = 768
HEADS = 12
HEAD_DIM = 64
FF = 3072
TOP = 2
BUCKETS = 32
REACH = 64
TOK_DEV = 128
TOKENS = 2048
EXPERTS = 4
CAP = 80
UNITS = 384
N_DP = 16
N_TENSOR = 2


def draw_tokens(key, part):
    own_key = jax.random.fold_in(key, 101)
    base_key = jax.random.fold_in(own_key, 0)
    values = jnp.clip(jax.random.normal(base_key, (TOKENS, D)), -6.0, 6.0)
    return values.astype(jnp.float32).astype(jnp.bfloat16)


def draw_seq_ids(key, part):
    own_key = jax.random.fold_in(key, 401)
    rate_key, flag_key, whole_key = jax.random.split(own_key, 3)
    thresholds = jax.random.randint(rate_key, (N_DP, 1), 1, 41)
    rolled = jax.random.randint(flag_key, (N_DP, TOK_DEV), 0, 1000)
    column = jnp.arange(TOK_DEV)[None, :]
    single_device = jax.random.randint(whole_key, (), 0, N_DP)
    busy_device = (single_device + 1) % N_DP
    device_ids = jnp.arange(N_DP)[:, None]
    starts = ((rolled < thresholds) | (device_ids == busy_device)) & (column > 0) & (device_ids != single_device)
    return jnp.cumsum(starts.astype(jnp.int32), axis=1).astype(jnp.int32).reshape(-1)


def draw_rel_bias(key, part):
    own_key = jax.random.fold_in(key, 303)
    values = jax.random.uniform(own_key, (HEADS, BUCKETS), minval=-2.0, maxval=2.0)
    return values.astype(jnp.float32)


def draw_w_router(key, part):
    own_key = jax.random.fold_in(key, 202)
    limit = min(4.0, 0.145 * math.sqrt(D))
    values = jnp.clip(jax.random.normal(own_key, (D, EXPERTS)), -limit, limit) / math.sqrt(D)
    return values.astype(jnp.float32).astype(jnp.bfloat16)


def level_of(key, shape, cuts, smallest, high):
    factor_of = 1.0
    for position, blocks in cuts:
        steps = jax.random.uniform(jax.random.fold_in(jax.random.fold_in(key, 6), position), (blocks,), jnp.float32, smallest / len(cuts), high / len(cuts))
        factor_of = factor_of * jnp.repeat(jnp.exp(steps), shape[position] // blocks).reshape((-1,) + (1,) * (len(shape) - 1 - position))
    return factor_of


def routed_block(key, own, number, rows, number_of, top, most, skew):
    sequence = jax.random.permutation(key, number_of)
    heavy_load, common = load_shares(number_of, rows * top, most, skew, True), load_shares(number_of, rows * top, most, skew, False)
    places = jnp.arange(number_of)

    def named(sizes, rotation):
        used = int((sizes > 0).sum())
        fixed = max(1, used // 4)
        passed = fixed + (places - fixed + rotation * (used - fixed)) % max(1, number_of - fixed)
        return jnp.zeros((number_of,), jnp.int32).at[sequence[jnp.where(places < fixed, places, passed)]].set(jnp.asarray(sizes, jnp.int32))

    sizes = jnp.where(number % 4 == 0, named(heavy_load, number // 4), named(common, number - number // 4 - 1))
    mixed = jax.random.permutation(jax.random.fold_in(own, 3), number_of)
    giver, sink = mixed[0:number_of // 2 * 2:2], mixed[1:number_of // 2 * 2:2]
    room = jnp.minimum(sizes[giver] - 1, most - sizes[sink]) // 2
    room = jnp.where((giver == sequence[0]) | (sink == sequence[0]) | (sizes[sink] == 0), 0, jnp.maximum(room, 0))
    passed = jax.random.randint(jax.random.fold_in(own, 4), (number_of // 2,), 0, 1 << 20) % (room + 1)
    sizes = sizes.at[giver].add(-passed).at[sink].add(passed)
    labels = jnp.searchsorted(jnp.cumsum(sizes), jnp.arange(rows * top), side="right").astype(jnp.int32)
    table = labels.reshape(top, rows).T
    table = table[jax.random.permutation(jax.random.fold_in(own, 1), rows)]
    rotation = jax.random.randint(jax.random.fold_in(own, 2), (rows, 1), 0, top)
    return jnp.take_along_axis(table, (jnp.arange(top)[None, :] + rotation) % top, axis=1)


def load_shares(amount, total, most, slope, full):
    loads = [(1 << 20) // math.isqrt(standing ** slope) + 1 for standing in range(1, amount + 1)]
    largest = most if full else min(most, max(-(-total // amount), total * loads[0] // sum(loads)))
    least = 1 if total - largest >= amount - 1 else 0
    holding, rest = [largest] + [least] * (amount - 1), total - largest - least * (amount - 1)
    while rest > 0:
        free = [i for i in range(1, amount) if holding[i] < largest] or [i for i in range(1, amount) if holding[i] < most]
        whole, remaining = sum([loads[i] for i in free]), rest
        for i in free:
            more = min(most - holding[i], max(1, remaining * loads[i] // whole), rest)
            holding[i] = holding[i] + more
            rest = rest - more
    return np.array(holding)


def gaussian(key, dims, width, most, cuts=(), held_as=jnp.bfloat16):
    array = width * jax.random.normal(key, dims, jnp.float32)
    if cuts:
        array = array * level_of(key, dims, cuts, -0.22, 0.18)
    return jnp.clip(array, -most, most).astype(held_as)


def setup_inputs(seed: int = 0) -> dict:
    arg_keys = jax.random.split(jax.random.key(seed), 15)
    tokens = draw_tokens(jax.random.fold_in(arg_keys[14], 71), 0)
    seq_ids = draw_seq_ids(jax.random.fold_in(arg_keys[14], 71), 0)
    routes_keys = jax.random.split(jax.random.fold_in(arg_keys[2], 1), TOKENS // TOK_DEV)
    routes_turns = jax.random.permutation(jax.random.fold_in(arg_keys[2], 3), TOKENS // TOK_DEV)
    routes = jax.vmap(lambda own, number: routed_block(jax.random.fold_in(arg_keys[2], 2), own, number, TOK_DEV, EXPERTS, TOP, CAP, 2))(routes_keys, routes_turns).reshape((TOKENS, TOP))
    gain_attn = jnp.clip(1.0 + 0.15 * jax.random.normal(arg_keys[3], (D,), jnp.float32), 0.25, 1.75)
    w_query = gaussian(arg_keys[4], (D, HEADS * HEAD_DIM), D ** -0.5, 0.21875, ((1, 2),))
    w_key = gaussian(arg_keys[5], (D, HEADS * HEAD_DIM), D ** -0.5, 0.21875, ((1, 2),))
    w_value = gaussian(arg_keys[6], (D, HEADS * HEAD_DIM), D ** -0.5, 0.21875, ((1, 2),))
    w_attn_out = gaussian(arg_keys[7], (HEADS * HEAD_DIM, D), (HEADS * HEAD_DIM // 8) ** -0.5, 0.625, ((0, 2),))
    rel_bias = draw_rel_bias(jax.random.fold_in(arg_keys[14], 71), 0)
    gain_ffn = jnp.clip(1.0 + 0.15 * jax.random.normal(arg_keys[9], (D,), jnp.float32), 0.25, 1.75)
    w_router = draw_w_router(jax.random.fold_in(arg_keys[14], 71), 0)
    expert_in = gaussian(arg_keys[11], (4 * EXPERTS, D, FF // 4), D ** -0.5, 0.21875, ((0, 16), (2, 2)))
    expert_out = gaussian(arg_keys[12], (4 * EXPERTS, FF // 4, D), (FF // 256) ** -0.5, 1.75, ((0, 16), (1, 2)))
    cotangent = gaussian(arg_keys[13], (TOKENS, D), 1.0, 6.0, ((0, 16),))
    return dict(tokens=tokens, seq_ids=seq_ids, routes=routes, gain_attn=gain_attn, w_query=w_query, w_key=w_key, w_value=w_value, w_attn_out=w_attn_out, rel_bias=rel_bias, gain_ffn=gain_ffn, w_router=w_router, expert_in=expert_in, expert_out=expert_out, cotangent=cotangent)


eps_norm = 1e-06

def bucket_matrix(length, buckets, max_reach):
    exact_span = buckets // 2
    distance = np.arange(length)
    log_ratio = np.log(np.maximum(distance, exact_span) / exact_span) / np.log(max_reach / exact_span)
    coarse = exact_span + np.floor(log_ratio * (buckets - exact_span)).astype(np.int64)
    bucket_of = np.where(distance < exact_span, distance, np.minimum(coarse, buckets - 1))
    offset = np.maximum(distance[:, None] - distance[None, :], 0)
    return bucket_of[offset].astype(np.int32)

def rounded(values):
    return lax.optimization_barrier(values.astype(jnp.bfloat16))

def gelu_tanh(values):
    return jax.nn.gelu(values, approximate=True)

def rms_forward(values, gain_vec):
    inv_rms = lax.rsqrt(lax.optimization_barrier(jnp.mean(values * values, axis=-1, keepdims=True)) + eps_norm)
    return (values * inv_rms * gain_vec, inv_rms)

def rms_backward(grad_normed, values, inv_rms, gain_vec):
    scaled = grad_normed * gain_vec
    inv_cubed = inv_rms * inv_rms * inv_rms
    grad_values = inv_rms * scaled - values * inv_cubed * lax.optimization_barrier(jnp.mean(scaled * values, axis=-1, keepdims=True))
    grad_gain = lax.optimization_barrier(jnp.sum(grad_normed * values * inv_rms, axis=0))
    return (grad_values, grad_gain)

def slot_of(route_ids, experts, capacity):
    count_all = route_ids.shape[0] * route_ids.shape[1]
    flat_ids = route_ids.reshape(-1).astype(jnp.int32)
    expert_hot = (flat_ids[:, None] == jnp.arange(experts, dtype=jnp.int32)[None, :]).astype(jnp.float32)
    order_ids = jnp.arange(count_all, dtype=jnp.int32)
    earlier = (order_ids[:, None] > order_ids[None, :]).astype(jnp.float32)
    before = jnp.dot(earlier, expert_hot, preferred_element_type=jnp.float32)
    rank_in = lax.optimization_barrier(jnp.sum(before * expert_hot, axis=1)).astype(jnp.int32)
    return (flat_ids * capacity + rank_in).reshape(route_ids.shape)

def split_heads(matrix):
    return matrix.reshape(matrix.shape[0], -1, HEAD_DIM).astype(jnp.float32)

def attention_scores(queries, key_rows, score_bias, allowed):
    raw_scores = jnp.einsum('qhd,khd->hqk', split_heads(queries), split_heads(key_rows))
    return jnp.where(allowed[None], raw_scores * HEAD_DIM ** (-0.5) + score_bias, -jnp.inf)

def reference(tokens, seq_ids, routes, gain_attn, w_query, w_key, w_value, w_attn_out, rel_bias, gain_ffn, w_router, expert_in, expert_out, cotangent):
    slot_count = EXPERTS * CAP
    quarters = 4 * N_TENSOR
    bucket_hot = (jnp.asarray(bucket_matrix(TOK_DEV, BUCKETS, REACH))[None] == jnp.arange(BUCKETS, dtype=jnp.int32)[:, None, None]).astype(jnp.float32)
    positions = jnp.arange(TOK_DEV)
    score_bias = jnp.einsum('hb,bij->hij', rel_bias, bucket_hot, precision=lax.Precision.HIGHEST)

    def pick_rows(slot_index):
        return (slot_index[:, :, None] == jnp.arange(slot_count, dtype=jnp.int32)[None, None, :]).astype(jnp.float32)

    def device_forward(inputs):
        token_block, seq_block, route_block = inputs
        inputs_wide = token_block.astype(jnp.float32)
        normed_one, inv_one = rms_forward(inputs_wide, gain_attn)
        normed_one = rounded(normed_one)
        queries = rounded(jnp.dot(normed_one, w_query, preferred_element_type=jnp.float32))
        key_rows = rounded(jnp.dot(normed_one, w_key, preferred_element_type=jnp.float32))
        value_rows = rounded(jnp.dot(normed_one, w_value, preferred_element_type=jnp.float32))
        allowed = (seq_block[:, None] == seq_block[None, :]) & (positions[:, None] >= positions[None, :])
        scores = attention_scores(queries, key_rows, score_bias, allowed)
        row_max = lax.optimization_barrier(jnp.max(scores, axis=-1, keepdims=True))
        log_total = row_max + jnp.log(lax.optimization_barrier(jnp.sum(jnp.exp(scores - row_max), axis=-1, keepdims=True)))
        weights = rounded(jnp.exp(scores - log_total))
        mixed_heads = rounded(jnp.einsum('hqk,khd->qhd', weights.astype(jnp.float32), split_heads(value_rows))).reshape(TOK_DEV, -1)
        attended = jnp.dot(mixed_heads, w_attn_out, preferred_element_type=jnp.float32)
        residual_one = inputs_wide + attended
        normed_two, inv_two = rms_forward(residual_one, gain_ffn)
        normed_two = rounded(normed_two)
        logits = jnp.dot(normed_two, w_router, preferred_element_type=jnp.float32)
        router_max = lax.optimization_barrier(jnp.max(logits, axis=-1, keepdims=True))
        router_exp = jnp.exp(logits - router_max)
        router_probs = router_exp / lax.optimization_barrier(jnp.sum(router_exp, axis=-1, keepdims=True))
        route_hot = (route_block[:, :, None] == jnp.arange(EXPERTS, dtype=jnp.int32)[None, None, :]).astype(jnp.float32)
        gate_probs = lax.optimization_barrier(jnp.sum(router_probs[:, None, :] * route_hot, axis=-1))
        slot_index = slot_of(route_block, EXPERTS, CAP)
        return {'inputs_wide': inputs_wide, 'inv_one': inv_one, 'normed_one': normed_one, 'queries': queries, 'key_rows': key_rows, 'value_rows': value_rows, 'allowed': allowed, 'log_total': log_total, 'mixed_heads': mixed_heads, 'residual_one': residual_one, 'inv_two': inv_two, 'normed_two': normed_two, 'router_probs': router_probs, 'route_hot': route_hot, 'gate_probs': gate_probs, 'slot_index': slot_index}

    def section_dispatch(inputs):
        kept = device_forward(inputs)
        dispatched = rounded(jnp.einsum('tks,td->sd', pick_rows(kept['slot_index']), kept['normed_two'].astype(jnp.float32)))
        return (kept['residual_one'], kept['gate_probs'], kept['slot_index'], dispatched)
    blocks = (tokens.reshape(N_DP, TOK_DEV, D), seq_ids.reshape(N_DP, TOK_DEV), routes.reshape(N_DP, TOK_DEV, TOP))
    residuals, gates_all, slots_all, dispatched_all = lax.map(section_dispatch, blocks)

    def by_expert(per_device):
        return per_device.reshape(N_DP, EXPERTS, CAP, D).transpose(1, 0, 2, 3).reshape(EXPERTS, N_DP * CAP, D)

    def by_device(per_expert):
        return per_expert.reshape(EXPERTS, N_DP, CAP, D).transpose(1, 0, 2, 3).reshape(N_DP, slot_count, D)
    w_in_full = expert_in.reshape(EXPERTS, 4, D, FF // 4).transpose(0, 2, 1, 3).reshape(EXPERTS, D, FF)
    w_out_full = expert_out.reshape(EXPERTS, FF, D)

    def quarter_sum(left_rows, right_blocks):
        pieces = jnp.einsum('rqf,qfd->qrd', left_rows.reshape(left_rows.shape[0], quarters, UNITS).astype(jnp.float32), right_blocks.astype(jnp.float32))
        return lax.optimization_barrier(jnp.sum(rounded(pieces).astype(jnp.float32), axis=0))

    def expert_forward(inputs):
        expert_rows, weight_in, weight_out = inputs
        pre_act = jnp.dot(expert_rows, weight_in, preferred_element_type=jnp.float32)
        activated = rounded(gelu_tanh(pre_act))
        return quarter_sum(activated, weight_out.reshape(quarters, UNITS, D))
    expert_inputs = by_expert(dispatched_all)
    results = by_device(lax.map(expert_forward, (expert_inputs, w_in_full, w_out_full)))

    def section_combine(inputs):
        residual_one, gate_probs, slot_index, device_results, grad_block = inputs
        chosen = jnp.take(device_results, slot_index, axis=0)
        mixture = lax.optimization_barrier(jnp.sum(gate_probs[:, :, None] * chosen, axis=1))
        output = (residual_one + mixture).astype(jnp.bfloat16)
        grad_wide = grad_block.astype(jnp.float32)
        routed_grad = rounded(gate_probs[:, :, None] * grad_wide[:, None, :])
        returned = rounded(jnp.einsum('tks,tkd->sd', pick_rows(slot_index), routed_grad.astype(jnp.float32)))
        return (output, returned)
    cot_blocks = cotangent.reshape(N_DP, TOK_DEV, D)
    outputs, returned_all = lax.map(section_combine, (residuals, gates_all, slots_all, results, cot_blocks))

    def expert_backward(inputs):
        expert_rows, grad_rows, weight_in, weight_out = inputs
        pre_act = jnp.dot(expert_rows, weight_in, preferred_element_type=jnp.float32)
        activated, gelu_back = jax.vjp(gelu_tanh, pre_act)
        activated = rounded(activated)
        grad_act = jnp.dot(grad_rows, weight_out.T, preferred_element_type=jnp.float32)
        grad_pre = rounded(gelu_back(grad_act)[0])
        grad_weight_out = jnp.dot(activated.T, grad_rows, preferred_element_type=jnp.float32)
        grad_weight_in = jnp.dot(expert_rows.T, grad_pre, preferred_element_type=jnp.float32)
        back_rows = quarter_sum(grad_pre, weight_in.reshape(D, quarters, UNITS).transpose(1, 2, 0))
        return (back_rows, grad_weight_in, grad_weight_out)
    back_all, grad_in_full, grad_out_full = lax.map(expert_backward, (expert_inputs, by_expert(returned_all), w_in_full, w_out_full))
    back_all = by_device(back_all)
    grad_expert_in = grad_in_full.reshape(EXPERTS, D, 4, FF // 4).transpose(0, 2, 1, 3).reshape(4 * EXPERTS, D, FF // 4)
    grad_expert_out = grad_out_full.reshape(4 * EXPERTS, FF // 4, D)

    def section_backward(totals, inputs):
        token_block, seq_block, route_block, grad_block, device_results, device_back = inputs
        kept = device_forward((token_block, seq_block, route_block))
        grad_wide = grad_block.astype(jnp.float32)
        slot_index = kept['slot_index']
        chosen = jnp.take(device_results, slot_index, axis=0)
        grad_gate = lax.optimization_barrier(jnp.sum(grad_wide[:, None, :] * chosen, axis=-1))
        back_tokens = lax.optimization_barrier(jnp.sum(jnp.take(device_back, slot_index, axis=0), axis=1))
        router_probs = kept['router_probs']
        grad_probs = lax.optimization_barrier(jnp.sum(grad_gate[:, :, None] * kept['route_hot'], axis=1))
        grad_logits = rounded(router_probs * (grad_probs - lax.optimization_barrier(jnp.sum(router_probs * grad_probs, axis=-1, keepdims=True))))
        grad_router = jnp.dot(kept['normed_two'].T, grad_logits, preferred_element_type=jnp.float32)
        grad_normed_two = back_tokens + jnp.dot(grad_logits, w_router.T, preferred_element_type=jnp.float32)
        grad_res_norm, grad_gain_ffn = rms_backward(grad_normed_two, kept['residual_one'], kept['inv_two'], gain_ffn)
        grad_residual = grad_wide + grad_res_norm
        grad_attended = rounded(grad_residual)
        mixed_heads = kept['mixed_heads']
        grad_attn_out = jnp.dot(mixed_heads.T, grad_attended, preferred_element_type=jnp.float32)
        grad_mixed = rounded(jnp.dot(grad_attended, w_attn_out.T, preferred_element_type=jnp.float32))
        scores = attention_scores(kept['queries'], kept['key_rows'], score_bias, kept['allowed'])
        probs_wide = jnp.exp(scores - kept['log_total'])
        grad_heads = split_heads(grad_mixed)
        grad_values = rounded(jnp.einsum('hqk,qhd->khd', rounded(probs_wide).astype(jnp.float32), grad_heads)).reshape(TOK_DEV, -1)
        grad_probs_attn = jnp.einsum('qhd,khd->hqk', grad_heads, split_heads(kept['value_rows']))
        delta_rows = lax.optimization_barrier(jnp.sum(grad_heads * split_heads(mixed_heads), axis=-1)).T[:, :, None]
        grad_scores = probs_wide * (grad_probs_attn - delta_rows)
        grad_bias = jnp.einsum('hij,bij->hb', grad_scores, bucket_hot, precision=lax.Precision.HIGHEST)
        scores_half = rounded(grad_scores).astype(jnp.float32)
        score_scale = HEAD_DIM ** (-0.5)
        grad_queries = rounded(jnp.einsum('hqk,khd->qhd', scores_half, split_heads(kept['key_rows'])) * score_scale).reshape(TOK_DEV, -1)
        grad_keys = rounded(jnp.einsum('hqk,qhd->khd', scores_half, split_heads(kept['queries'])) * score_scale).reshape(TOK_DEV, -1)
        normed_one = kept['normed_one']
        grad_query = jnp.dot(normed_one.T, grad_queries, preferred_element_type=jnp.float32)
        grad_key = jnp.dot(normed_one.T, grad_keys, preferred_element_type=jnp.float32)
        grad_value = jnp.dot(normed_one.T, grad_values, preferred_element_type=jnp.float32)
        grad_normed_one = jnp.dot(grad_queries, w_query.T, preferred_element_type=jnp.float32)
        grad_normed_one = grad_normed_one + jnp.dot(grad_keys, w_key.T, preferred_element_type=jnp.float32)
        grad_normed_one = grad_normed_one + jnp.dot(grad_values, w_value.T, preferred_element_type=jnp.float32)
        grad_in_norm, grad_gain_attn = rms_backward(grad_normed_one, kept['inputs_wide'], kept['inv_one'], gain_attn)
        grad_tokens = grad_residual + grad_in_norm
        updates = (grad_gain_attn, grad_query, grad_key, grad_value, grad_attn_out, grad_bias, grad_gain_ffn, grad_router)
        return (jax.tree.map(jnp.add, totals, updates), grad_tokens)
    initial = (jnp.zeros((D,), jnp.float32), jnp.zeros((D, HEADS * HEAD_DIM), jnp.float32), jnp.zeros((D, HEADS * HEAD_DIM), jnp.float32), jnp.zeros((D, HEADS * HEAD_DIM), jnp.float32), jnp.zeros((HEADS * HEAD_DIM, D), jnp.float32), jnp.zeros((HEADS, BUCKETS), jnp.float32), jnp.zeros((D,), jnp.float32), jnp.zeros((D, EXPERTS), jnp.float32))
    totals, grad_blocks = lax.scan(section_backward, initial, (blocks[0], blocks[1], blocks[2], cot_blocks, results, back_all))
    return (outputs.reshape(TOKENS, D), grad_blocks.reshape(TOKENS, D), totals[0], totals[1], totals[2], totals[3], totals[4], totals[5], totals[6], totals[7], grad_expert_in, grad_expert_out)
```

```python
import functools

import jax
import jax.numpy as jnp
import numpy as np
from jax import lax
from jax.sharding import PartitionSpec as P

HEAD_DIM = 64
TOP = 2
REACH = 64


eps_norm = 1e-06


def bucket_matrix(length, buckets, max_reach):
    exact_span = buckets // 2
    distance = np.arange(length)
    log_ratio = np.log(np.maximum(distance, exact_span) / exact_span) / np.log(
        max_reach / exact_span
    )
    coarse = exact_span + np.floor(log_ratio * (buckets - exact_span)).astype(np.int64)
    bucket_of = np.where(distance < exact_span, distance, np.minimum(coarse, buckets - 1))
    offset = np.maximum(distance[:, None] - distance[None, :], 0)
    return bucket_of[offset].astype(np.int32)


def gelu_tanh(values):
    return jax.nn.gelu(values, approximate=True)


def rms_forward(values, gain_vec):
    inv_rms = lax.rsqrt(jnp.mean(values * values, axis=-1, keepdims=True) + eps_norm)
    return (values * inv_rms * gain_vec, inv_rms)


def rms_backward(grad_normed, values, inv_rms, gain_vec):
    scaled = grad_normed * gain_vec
    inv_cubed = inv_rms * inv_rms * inv_rms
    grad_values = inv_rms * scaled - values * inv_cubed * jnp.mean(
        scaled * values, axis=-1, keepdims=True
    )
    grad_gain = jnp.sum(grad_normed * values * inv_rms, axis=0)
    return (grad_values, grad_gain)


def slot_of(route_ids, group_id, experts, capacity):
    count_all = route_ids.shape[0] * route_ids.shape[1]
    flat_ids = route_ids.reshape(-1)
    expert_hot = (flat_ids[:, None] == jnp.arange(experts, dtype=jnp.int32)[None, :]).astype(
        jnp.bfloat16
    )
    order_ids = jnp.arange(count_all, dtype=jnp.int32)
    earlier = (order_ids[:, None] > order_ids[None, :]).astype(jnp.bfloat16)
    before = jnp.dot(earlier, expert_hot, preferred_element_type=jnp.float32)
    rank_in = jnp.sum(before * expert_hot.astype(jnp.float32), axis=1).astype(jnp.int32)
    return ((flat_ids ^ group_id) * capacity + rank_in).reshape(route_ids.shape)


def head_split(matrix):
    return matrix.reshape(matrix.shape[0], -1, HEAD_DIM)


def attention_scores(queries, key_rows, score_bias, allowed):
    raw_scores = jnp.einsum(
        "qhd,khd->hqk",
        head_split(queries),
        head_split(key_rows),
        preferred_element_type=jnp.float32,
    )
    return jnp.where(allowed[None], raw_scores * HEAD_DIM ** (-0.5) + score_bias, -jnp.inf)


def make_comm(n_dp, n_tensor):
    groups = n_dp // 4

    def send(array, target):
        pairs = []
        for dp_id in range(n_dp):
            for t_id in range(n_tensor):
                e_to, q_to, t_to = target(dp_id // 4, dp_id % 4, t_id)
                pairs.append((dp_id * n_tensor + t_id, (e_to * 4 + q_to) * n_tensor + t_to))
        return lax.ppermute(array, ("dp", "tensor"), pairs)

    return groups, send


def swap_pair(send, array):
    return send(array, lambda e, q, t: (e, q, 1 - t))


def plane_gather(send, array, t):
    first = send(array, lambda e, q, t: (e, q ^ (1 if t == 0 else 2), t))
    both = jnp.concatenate([array, first], axis=0)
    second = send(both, lambda e, q, t: (e, q ^ (2 if t == 0 else 1), t))
    rows = array.shape[0]
    even = t == 0
    near = jnp.where(even, first, second[:rows])
    far = jnp.where(even, second[:rows], first)
    return jnp.concatenate([array, near, far, second[rows:]], axis=0)


def plane_scatter(send, array, t):
    rows = array.shape[0] // 4
    even = t == 0
    blocks = array.reshape(4, rows, array.shape[1])
    near = jnp.where(even, blocks[1], blocks[2])
    far = jnp.where(even, blocks[2], blocks[1])
    moved = send(
        jnp.concatenate([near, blocks[3]], axis=0),
        lambda e, q, t: (e, q ^ (1 if t == 0 else 2), t),
    )
    kept = jnp.concatenate([blocks[0], far], axis=0).astype(jnp.float32) + moved.astype(jnp.float32)
    moved_two = send(
        kept[rows:].astype(jnp.bfloat16), lambda e, q, t: (e, q ^ (2 if t == 0 else 1), t)
    )
    return (kept[:rows] + moved_two.astype(jnp.float32)).astype(jnp.bfloat16)


def group_exchange(send, chunks):
    received = [chunks[0]]
    for step in range(1, len(chunks)):
        received.append(send(chunks[step], lambda e, q, t, step=step: (e ^ step, q, t)))
    return received


def own_half(array, t):
    width = array.shape[1] // 2
    return lax.dynamic_slice_in_dim(array, t * width, width, axis=1)


def join_halves(mine, other, t):
    even = t == 0
    return jnp.concatenate([jnp.where(even, mine, other), jnp.where(even, other, mine)], axis=1)


def on_device(
    n_dp,
    n_tensor,
    tokens,
    seq_ids,
    routes,
    gain_attn,
    w_query,
    w_key,
    w_value,
    w_attn_out,
    rel_bias,
    gain_ffn,
    w_router,
    expert_in,
    expert_out,
    cotangent,
):
    tok_rows = tokens.shape[0]
    experts = w_router.shape[1]
    bucket_count = rel_bias.shape[1]
    capacity = 4 * ((5 * TOP * tok_rows + 16 * experts - 1) // (16 * experts))
    groups, send = make_comm(n_dp, n_tensor)
    dp_id = lax.axis_index("dp")
    t_id = lax.axis_index("tensor")
    e_id = dp_id // 4
    q_id = dp_id % 4

    slot_index = slot_of(routes, e_id, experts, capacity)
    pick_table = (
        slot_index[:, :, None] == jnp.arange(experts * capacity, dtype=jnp.int32)[None, None, :]
    ).astype(jnp.bfloat16)
    pick_any = pick_table[:, 0] + pick_table[:, 1]

    def dispatch(rows, extra=None):
        width = rows.shape[1]
        picked = lax.dot_general(
            pick_any, rows, (((0,), (0,)), ((), ())), preferred_element_type=jnp.float32
        ).astype(jnp.bfloat16)
        chunks = [picked[s * capacity : (s + 1) * capacity] for s in range(experts)]
        arrived = group_exchange(send, chunks)
        if extra is not None:
            arrived = arrived + [extra]
        block = jnp.concatenate(arrived, axis=0)
        gathered = plane_gather(send, block, t_id)
        return join_halves(gathered, swap_pair(send, gathered), t_id)

    def give_back(rows):
        mine = own_half(rows, t_id)
        other = swap_pair(send, own_half(rows, 1 - t_id))
        summed = (mine.astype(jnp.float32) + other.astype(jnp.float32)).astype(jnp.bfloat16)
        block = plane_scatter(send, summed, t_id)
        chunks = [block[s * capacity : (s + 1) * capacity] for s in range(experts)]
        return jnp.concatenate(group_exchange(send, chunks), axis=0)

    inputs_wide = tokens.astype(jnp.float32)
    normed_one, inv_one = rms_forward(inputs_wide, gain_attn)
    normed_one = normed_one.astype(jnp.bfloat16)
    slots = experts * capacity
    early = dispatch(own_half(cotangent, t_id), own_half(normed_one, t_id))
    early = early.reshape(4, slots + tok_rows, -1)
    cot_rows = early[:, :slots].reshape(4 * slots, -1)
    normed_all = early[:, slots:].reshape(4 * tok_rows, -1)
    queries = jnp.dot(normed_one, w_query, preferred_element_type=jnp.float32).astype(jnp.bfloat16)
    key_rows = jnp.dot(normed_one, w_key, preferred_element_type=jnp.float32).astype(jnp.bfloat16)
    value_rows = jnp.dot(normed_one, w_value, preferred_element_type=jnp.float32).astype(
        jnp.bfloat16
    )
    positions = jnp.arange(tok_rows)
    allowed = (seq_ids[:, None] == seq_ids[None, :]) & (positions[:, None] >= positions[None, :])
    bucket_hot = (
        jnp.asarray(bucket_matrix(tok_rows, bucket_count, REACH))[None]
        == jnp.arange(bucket_count, dtype=jnp.int32)[:, None, None]
    ).astype(jnp.float32)
    score_bias = jnp.einsum("hb,bij->hij", rel_bias, bucket_hot, precision=lax.Precision.HIGHEST)
    scores = attention_scores(queries, key_rows, score_bias, allowed)
    row_max = jnp.max(scores, axis=-1, keepdims=True)
    log_total = row_max + jnp.log(jnp.sum(jnp.exp(scores - row_max), axis=-1, keepdims=True))
    weights = jnp.exp(scores - log_total).astype(jnp.bfloat16)
    mixed_heads = (
        jnp.einsum(
            "hqk,khd->qhd", weights, head_split(value_rows), preferred_element_type=jnp.float32
        )
        .astype(jnp.bfloat16)
        .reshape(tok_rows, -1)
    )
    attended_part = jnp.dot(mixed_heads, w_attn_out, preferred_element_type=jnp.float32)
    attended = attended_part + swap_pair(send, attended_part)
    residual_one = inputs_wide + attended
    normed_two, inv_two = rms_forward(residual_one, gain_ffn)
    normed_two = normed_two.astype(jnp.bfloat16)
    logits = jnp.dot(normed_two, w_router, preferred_element_type=jnp.float32)
    router_max = jnp.max(logits, axis=-1, keepdims=True)
    router_exp = jnp.exp(logits - router_max)
    router_probs = router_exp / jnp.sum(router_exp, axis=-1, keepdims=True)
    route_hot = (routes[:, :, None] == jnp.arange(experts, dtype=jnp.int32)[None, None, :]).astype(
        jnp.float32
    )
    gate_probs = jnp.sum(router_probs[:, None, :] * route_hot, axis=-1)
    received = dispatch(own_half(normed_two, t_id))
    row_logits = jnp.dot(received, w_router, preferred_element_type=jnp.float32)
    row_exp = jnp.exp(row_logits - jnp.max(row_logits, axis=-1, keepdims=True))
    own_expert = (jnp.arange(experts, dtype=jnp.int32) == e_id).astype(jnp.float32)
    row_gate = jnp.sum(row_exp * own_expert, axis=-1, keepdims=True) / jnp.sum(
        row_exp, axis=-1, keepdims=True
    )
    grad_rows = (row_gate * cot_rows.astype(jnp.float32)).astype(jnp.bfloat16)
    weight_in = expert_in[0]
    weight_out = expert_out[0]
    pre_act = jnp.dot(received, weight_in, preferred_element_type=jnp.float32)
    activated, gelu_back = jax.vjp(gelu_tanh, pre_act)
    activated = activated.astype(jnp.bfloat16)
    expert_part = jnp.dot(activated, weight_out, preferred_element_type=jnp.float32).astype(
        jnp.bfloat16
    )
    grad_act = jnp.dot(grad_rows, weight_out.T, preferred_element_type=jnp.float32)
    grad_pre = gelu_back(grad_act)[0].astype(jnp.bfloat16)
    grad_weight_out = jnp.dot(activated.T, grad_rows, preferred_element_type=jnp.float32)
    grad_weight_in = jnp.dot(received.T, grad_pre, preferred_element_type=jnp.float32)
    back_part = jnp.dot(grad_pre, weight_in.T, preferred_element_type=jnp.float32).astype(
        jnp.bfloat16
    )
    expert_rows = give_back(expert_part)
    back_rows = give_back(back_part)
    grad_wide = cotangent.astype(jnp.float32)
    chosen = jnp.einsum("tks,sd->tkd", pick_table, expert_rows, preferred_element_type=jnp.float32)
    back_half = jnp.dot(pick_any, back_rows, preferred_element_type=jnp.float32)
    mixture_half = jnp.sum(gate_probs[:, :, None] * chosen, axis=1)
    gate_half = jnp.sum(own_half(grad_wide, t_id)[:, None, :] * chosen, axis=-1)
    output_half = (own_half(residual_one, t_id) + mixture_half).astype(jnp.bfloat16)
    output = join_halves(output_half, swap_pair(send, output_half), t_id)
    packed = jnp.concatenate([back_half, jnp.pad(gate_half, ((0, 0), (0, 126)))], axis=1)
    packed_other = swap_pair(send, packed)
    width = back_half.shape[1]
    back_tokens = join_halves(back_half, packed_other[:, :width], t_id)
    grad_gate = gate_half + packed_other[:, width : width + TOP]
    grad_probs = jnp.sum(grad_gate[:, :, None] * route_hot, axis=1)
    grad_logits = (
        router_probs * (grad_probs - jnp.sum(router_probs * grad_probs, axis=-1, keepdims=True))
    ).astype(jnp.bfloat16)
    grad_router = jnp.dot(normed_two.T, grad_logits, preferred_element_type=jnp.float32)
    grad_normed_two = back_tokens + jnp.dot(
        grad_logits, w_router.T, preferred_element_type=jnp.float32
    )
    grad_res_norm, grad_gain_ffn = rms_backward(grad_normed_two, residual_one, inv_two, gain_ffn)
    grad_residual = grad_wide + grad_res_norm
    grad_attended = grad_residual.astype(jnp.bfloat16)
    att_gathered = plane_gather(send, own_half(grad_attended, t_id), t_id)
    attended_all = join_halves(att_gathered, swap_pair(send, att_gathered), t_id)
    grad_mixed = jnp.dot(grad_attended, w_attn_out.T, preferred_element_type=jnp.float32).astype(
        jnp.bfloat16
    )
    scores_again = attention_scores(queries, key_rows, score_bias, allowed)
    probs_wide = jnp.exp(scores_again - log_total)
    grad_heads = head_split(grad_mixed)
    grad_values = (
        jnp.einsum(
            "hqk,qhd->khd",
            probs_wide.astype(jnp.bfloat16),
            grad_heads,
            preferred_element_type=jnp.float32,
        )
        .astype(jnp.bfloat16)
        .reshape(tok_rows, -1)
    )
    grad_probs_attn = jnp.einsum(
        "qhd,khd->hqk", grad_heads, head_split(value_rows), preferred_element_type=jnp.float32
    )
    delta_rows = jnp.sum(
        grad_heads.astype(jnp.float32) * head_split(mixed_heads).astype(jnp.float32), axis=-1
    ).T[:, :, None]
    grad_scores = probs_wide * (grad_probs_attn - delta_rows)
    grad_bias = jnp.einsum("hij,bij->hb", grad_scores, bucket_hot, precision=lax.Precision.HIGHEST)
    scores_half = grad_scores.astype(jnp.bfloat16)
    score_scale = HEAD_DIM ** (-0.5)
    grad_queries = (
        (
            jnp.einsum(
                "hqk,khd->qhd",
                scores_half,
                head_split(key_rows),
                preferred_element_type=jnp.float32,
            )
            * score_scale
        )
        .astype(jnp.bfloat16)
        .reshape(tok_rows, -1)
    )
    grad_keys = (
        (
            jnp.einsum(
                "hqk,qhd->khd", scores_half, head_split(queries), preferred_element_type=jnp.float32
            )
            * score_scale
        )
        .astype(jnp.bfloat16)
        .reshape(tok_rows, -1)
    )
    grad_normed_part = jnp.dot(grad_queries, w_query.T, preferred_element_type=jnp.float32)
    grad_normed_part = grad_normed_part + jnp.dot(
        grad_keys, w_key.T, preferred_element_type=jnp.float32
    )
    grad_normed_part = grad_normed_part + jnp.dot(
        grad_values, w_value.T, preferred_element_type=jnp.float32
    )
    normed_part = grad_normed_part.astype(jnp.bfloat16)
    grad_normed_one = normed_part.astype(jnp.float32) + swap_pair(send, normed_part).astype(
        jnp.float32
    )
    grad_in_norm, grad_gain_attn = rms_backward(grad_normed_one, inputs_wide, inv_one, gain_attn)
    grad_tokens = grad_residual + grad_in_norm
    right_sides = jnp.stack([grad_queries, grad_keys, grad_values, mixed_heads])
    right_all = [lax.dynamic_index_in_dim(right_sides, q_id, 0, keepdims=False)]
    for step in (1, 2, 3):
        right_all.append(
            send(
                lax.dynamic_index_in_dim(right_sides, q_id ^ step, 0, keepdims=False),
                lambda e, q, t, step=step: (e, q ^ step, t),
            )
        )
    right_all = jnp.concatenate(right_all, axis=0)
    left_all = jnp.where(q_id == 3, attended_all, normed_all)
    partial = lax.dot_general(
        left_all, right_all, (((0,), (0,)), ((), ())), preferred_element_type=jnp.float32
    ).astype(jnp.bfloat16)
    depth = partial.shape[0] // groups
    blocks = [
        lax.dynamic_slice_in_dim(partial, (e_id ^ s) * depth, depth, axis=0) for s in range(groups)
    ]
    arrived = group_exchange(send, blocks)
    reduced = arrived[0].astype(jnp.float32)
    for block in arrived[1:]:
        reduced = reduced + block.astype(jnp.float32)
    reduced = reduced.astype(jnp.bfloat16)
    spread = jnp.stack(group_exchange(send, [reduced] * groups))
    order = jnp.arange(groups, dtype=jnp.int32) ^ e_id
    matrix = jnp.take(spread, order, axis=0).reshape(partial.shape)
    rows = matrix.shape[0] // 2
    from_x = send(matrix, lambda e, q, t: (e, q ^ 1, t))
    from_y = send(matrix, lambda e, q, t: (e, q ^ 2, t))
    cross_top = send(from_x[:rows], lambda e, q, t: (e, q ^ 2, t))
    cross_low = send(from_y[rows:], lambda e, q, t: (e, q ^ 1, t))
    cross = jnp.concatenate([cross_top, cross_low], axis=0)
    matrices = jnp.stack([matrix, from_x, from_y, cross])
    grads = [
        lax.dynamic_index_in_dim(matrices, q_id ^ m, 0, keepdims=False).astype(jnp.float32)
        for m in range(4)
    ]
    small_parts = (grad_gain_attn, grad_bias, grad_gain_ffn, grad_router)
    small = jnp.concatenate([part.reshape(-1) for part in small_parts])
    small = jnp.pad(small, (0, -small.shape[0] % 1024)).reshape(-1, 128)
    small = small + send(small, lambda e, q, t: (e, q ^ 1, t))
    small = small + send(small, lambda e, q, t: (e, q ^ 2, t))
    step = 1
    while step < groups:
        small = small + send(small, lambda e, q, t, step=step: (e ^ step, q, t))
        step *= 2
    small = small.reshape(-1)
    totals = []
    start = 0
    for part in small_parts:
        totals.append(small[start : start + part.size].reshape(part.shape))
        start += part.size
    return (
        output,
        grad_tokens,
        totals[0],
        grads[0],
        grads[1],
        grads[2],
        grads[3].T,
        totals[1],
        totals[2],
        totals[3],
        grad_weight_in[None],
        grad_weight_out[None],
    )


def solution(mesh):
    in_specs = (
        P("dp", None),
        P("dp"),
        P("dp", None),
        P(),
        P(None, "tensor"),
        P(None, "tensor"),
        P(None, "tensor"),
        P("tensor", None),
        P("tensor", None),
        P(),
        P(),
        P("dp", None, "tensor"),
        P("dp", "tensor", None),
        P("dp", None),
    )
    out_specs = (
        P("dp", None),
        P("dp", None),
        P(),
        P(None, "tensor"),
        P(None, "tensor"),
        P(None, "tensor"),
        P("tensor", None),
        P("tensor", None),
        P(),
        P(),
        P("dp", None, "tensor"),
        P("dp", "tensor", None),
    )
    return jax.shard_map(
        functools.partial(on_device, mesh.shape["dp"], mesh.shape["tensor"]),
        mesh=mesh, in_specs=in_specs, out_specs=out_specs, check_vma=False
    )
```

```python
import functools

import jax
import jax.numpy as jnp
import numpy as np
from jax import lax
from jax.experimental import pallas as pl
from jax.experimental.pallas import tpu as pltpu
from jax.sharding import PartitionSpec as P

HEAD_DIM = 64
TOP = 2
REACH = 64
LANES = 128

eps_norm = 1e-06
gelu_scale = float(np.sqrt(2.0 / np.pi))
microseconds = {"front": 5, "route": 1.9, "expert": 4.4, "expert_back": 5.4, "expert_grads": 4.0, "combine": 1.9, "attend_back": 2.5, "partial": 1.2, "final": 3.9, "tokens_back": 1.5, "small": 1.4}
f32 = jnp.float32
bf16 = jnp.bfloat16


def bucket_of_distance(length, buckets, max_reach):
    exact_span = buckets // 2
    distance = np.arange(length)
    log_ratio = np.log(np.maximum(distance, exact_span) / exact_span) / np.log(
        max_reach / exact_span
    )
    coarse = exact_span + np.floor(log_ratio * (buckets - exact_span)).astype(np.int64)
    return np.where(distance < exact_span, distance, np.minimum(coarse, buckets - 1))


def nn(left, right, precision=None):
    return lax.dot_general(
        left, right, (((1,), (0,)), ((), ())), precision=precision, preferred_element_type=f32
    )


def nt(left, right):
    return lax.dot_general(left, right, (((1,), (1,)), ((), ())), preferred_element_type=f32)


def tn(left, right):
    return lax.dot_general(left, right, (((0,), (0,)), ((), ())), preferred_element_type=f32)


def iota(shape, axis):
    return lax.broadcasted_iota(jnp.int32, shape, axis)


def call(body, name, ids, outs, *args, scratch=(), limit=24, far=()):
    shapes = [jax.ShapeDtypeStruct(shape, dtype) for shape, dtype in outs]
    return pl.pallas_call(
        body,
        out_shape=shapes,
        in_specs=[pl.BlockSpec(memory_space=pltpu.SMEM)]
        + [
            pl.BlockSpec(memory_space=pltpu.HBM if i in far else pltpu.VMEM)
            for i in range(len(args))
        ],
        out_specs=[pl.BlockSpec(memory_space=pltpu.VMEM)] * len(outs),
        scratch_shapes=list(scratch),
        compiler_params=pltpu.CompilerParams(vmem_limit_bytes=limit << 20),
        cost_estimate=pl.CostEstimate(
            flops=0, transcendentals=0, bytes_accessed=int(microseconds.get(name, 0.8) * 3.6e6)
        ),
        name=name,
    )(
        ids,
        *[
            pltpu.with_memory_space_constraint(a, pltpu.HBM) if i in far else a
            for i, a in enumerate(args)
        ],
    )


def halves(value, t):
    width = value.shape[1] // 2
    low, high = value[:, :width], value[:, width:]
    even = t == 0
    return jnp.where(even, low, high), jnp.where(even, high, low)


def row_halves(value, t):
    width = value.shape[0] // 2
    low, high = value[:width], value[width:]
    even = t == 0
    return jnp.where(even, low, high), jnp.where(even, high, low)


def columns_of(row):
    length = row.shape[1]
    return jnp.broadcast_to(row.astype(f32), (length, length)).T


def sums_by_distance(square):
    length = square.shape[0]
    rows = length // 2
    while rows >= 1:
        square = square[:rows] + pltpu.roll(square[rows:], length - rows, 1)
        rows //= 2
    return square


def fetch(sources, targets, sems):
    copies = [
        pltpu.make_async_copy(source, target, sems.at[i])
        for i, (source, target) in enumerate(zip(sources, targets))
    ]
    for copy in copies:
        copy.start()
    return copies


def route_body(experts, stride, ids, routes_far, cot_far, slots, *refs):
    chunks, (routes, cot, sems) = refs[:experts], refs[experts:]
    copies = fetch((routes_far, cot_far), (routes, cot), sems)
    copies[0].wait()
    e, t = ids[0], ids[2]
    length = routes.shape[1]
    expert_row = iota((experts, length), 0)
    first = (expert_row == routes[0:1, :]).astype(f32)
    second = (expert_row == routes[1:2, :]).astype(f32)
    earlier = (iota((length, length), 0) < iota((length, length), 1)).astype(bf16)
    before = nn((first + second).astype(bf16), earlier)
    rank0 = jnp.sum(before * first, axis=0, keepdims=True).astype(jnp.int32)
    rank1 = jnp.sum(before * second, axis=0, keepdims=True).astype(jnp.int32)
    slot0 = (routes[0:1, :] ^ e) * stride + rank0
    slot1 = (routes[1:2, :] ^ e) * stride + rank1
    slots[0:1, :] = slot0
    slots[1:2, :] = slot1
    copies[1].wait()
    mine, _ = halves(cot[...], t)
    for s in range(experts):
        place = iota((stride, length), 0) + s * stride
        pick = ((place == slot0) | (place == slot1)).astype(bf16)
        chunks[s][...] = nn(pick, mine).astype(bf16)


def front_body(ids, *refs):
    sources = refs[:9]
    early, part, q_out, k_out, v_out, probs = refs[9:15]
    targets, sems = refs[15:-1], refs[-1]
    tokens, gain, wq, wk, wv, rel, hot, seq, wo = targets
    copies = fetch(sources, targets, sems)
    t = ids[2]
    length = tokens.shape[0]
    mixed_out = early.at[pl.ds(length, length), :]
    copies[0].wait()
    copies[1].wait()
    wide = tokens[...].astype(f32)
    inv = lax.rsqrt(jnp.mean(wide * wide, axis=-1, keepdims=True) + eps_norm)
    value = (wide * inv * gain[...][None, :]).astype(bf16)
    early[pl.ds(0, length), :] = halves(value, t)[0]
    rows = length
    copies[2].wait()
    queries = nn(value, wq[...]).astype(bf16)
    copies[3].wait()
    keys = nn(value, wk[...]).astype(bf16)
    copies[4].wait()
    values = nn(value, wv[...]).astype(bf16)
    q_out[...] = queries
    k_out[...] = keys
    v_out[...] = values
    for copy in copies[5:8]:
        copy.wait()
    seq_cols = jnp.broadcast_to(seq[...].astype(f32), (rows, rows))
    allowed = (seq_cols == seq_cols.T) & (iota((rows, rows), 0) >= iota((rows, rows), 1))
    table = nn(rel[...], hot[...], lax.Precision.HIGHEST)
    lane = iota((rows, LANES), 1)
    for pair in range(queries.shape[1] // LANES):
        span = slice(pair * LANES, (pair + 1) * LANES)
        q, k, v = queries[:, span], keys[:, span], values[:, span]
        mixed = []
        for side in range(2):
            head = pair * 2 + side
            mine = (lane < HEAD_DIM) if side == 0 else (lane >= HEAD_DIM)
            raw = nt(jnp.where(mine, q, jnp.zeros_like(q)), k)
            bias = pltpu.roll(
                jnp.broadcast_to(table[head : head + 1, :], (rows, rows)),
                0,
                1,
                stride=1,
                stride_axis=0,
            )
            scores = jnp.where(allowed, raw * HEAD_DIM ** (-0.5) + bias, -1e30)
            top = jnp.max(scores, axis=-1, keepdims=True)
            raised = jnp.exp(scores - top)
            weight = raised / jnp.sum(raised, axis=-1, keepdims=True)
            probs[head] = weight
            mixed.append(nn(weight.astype(bf16), v))
        mixed_out[:, span] = jnp.where(lane < HEAD_DIM, mixed[0], mixed[1]).astype(bf16)
    copies[8].wait()
    part[...] = nn(mixed_out[...], wo[...])


def router_of(normed, weights_row):
    logits = nt(normed, weights_row)
    raised = jnp.exp(logits - jnp.max(logits, axis=-1, keepdims=True))
    return raised / jnp.sum(raised, axis=-1, keepdims=True)


def middle_body(experts, stride, ids, own, other, tokens, gain, router, slots, residual, normed, probs, *chunks):
    t = ids[2]
    wide = tokens[...].astype(f32) + (own[...] + other[...])
    residual[...] = wide
    inv = lax.rsqrt(jnp.mean(wide * wide, axis=-1, keepdims=True) + eps_norm)
    value = (wide * inv * gain[...][None, :]).astype(bf16)
    normed[...] = value
    mine, _ = halves(value, t)
    length = slots.shape[1]
    for s in range(experts):
        place = iota((stride, length), 0) + s * stride
        pick = ((place == slots[0:1, :]) | (place == slots[1:2, :])).astype(bf16)
        chunks[s][...] = nn(pick, mine).astype(bf16)
    probs[...] = router_of(value, router[...])


def join_body(ids, *refs):
    out = refs[-1]
    start = 0
    for ref in refs[:-1]:
        out[pl.ds(start, ref.shape[0]), :] = ref[...]
        start += ref.shape[0]


def expert_body(rows, ids, *refs):
    own, other = refs[:4], refs[4:8]
    w_in, w_out, act, slope, part_mine, part_other = refs[8:]
    t = ids[2]
    in_mine, in_other = row_halves(w_in[0], t)
    out_mine, out_other = halves(w_out[0], t)
    for p in range(4):
        span = pl.ds(p * rows, rows)
        pre = nn(own[p][...], in_mine) + nn(other[p][...], in_other)
        square = pre * pre
        bent = jnp.tanh(gelu_scale * (pre + 0.044715 * pre * square))
        half = 0.5 * (1.0 + bent)
        value = (pre * half).astype(bf16)
        act[span, :] = value
        slope[span, :] = half + 0.5 * pre * (1.0 - bent * bent) * (
            gelu_scale * (1.0 + 3 * 0.044715 * square)
        )
        part_mine[span, :] = nn(value, out_mine).astype(bf16)
        part_other[span, :] = nn(value, out_other).astype(bf16)


def expert_back_body(rows, experts, ids, *refs):
    own, other, cot_own, cot_other = refs[:4], refs[4:8], refs[8:12], refs[12:16]
    w_in, w_out, router, slope, grad_pre, grad_mine, grad_other, back_mine, back_other = refs[16:]
    e, t = ids[0], ids[2]
    in_mine, in_other = row_halves(w_in[0], t)
    out_mine, out_other = halves(w_out[0], t)
    router_mine, router_other = halves(router[...], t)
    for p in range(4):
        span = pl.ds(p * rows, rows)
        logits = nt(own[p][...], router_mine) + nt(other[p][...], router_other)
        raised = jnp.exp(logits - jnp.max(logits, axis=-1, keepdims=True))
        chosen = jnp.where(iota(raised.shape, 1) == e, raised, 0.0)
        gate = jnp.sum(chosen, axis=-1, keepdims=True) / jnp.sum(raised, axis=-1, keepdims=True)
        first = (gate * cot_own[p][pl.ds(0, rows), :].astype(f32)).astype(bf16)
        second = (gate * cot_other[p][pl.ds(0, rows), :].astype(f32)).astype(bf16)
        grad_mine[span, :] = first
        grad_other[span, :] = second
        grad_act = nt(first, out_mine) + nt(second, out_other)
        value = (grad_act * slope[span, :]).astype(bf16)
        grad_pre[span, :] = value
        back_mine[span, :] = nt(value, in_mine).astype(bf16)
        back_other[span, :] = nt(value, in_other).astype(bf16)


def expert_grads_body(rows, ids, *refs):
    own, other = refs[:4], refs[4:8]
    act, grad_pre, grad_mine, grad_other, out_in, out_out = refs[8:]
    even = ids[2] == 0
    low = jnp.where(even, grad_mine[...], grad_other[...])
    high = jnp.where(even, grad_other[...], grad_mine[...])
    width = low.shape[1]
    left = act[...]
    out_out[0, :, :width] = tn(left, low)
    out_out[0, :, width:] = tn(left, high)
    first = jnp.concatenate([jnp.where(even, own[p][...], other[p][...]) for p in range(4)], axis=0)
    second = jnp.concatenate([jnp.where(even, other[p][...], own[p][...]) for p in range(4)], axis=0)
    right = grad_pre[...]
    out_in[0, :width, :] = tn(first, right)
    out_in[0, width:, :] = tn(second, right)


def pair_sum_body(ids, mine, received, keep, send):
    rows = mine.shape[0] // 4

    def block(p):
        q = (0, 2, 1, 3)[p]
        left = mine[pl.ds(p * rows, rows), :].astype(f32)
        return (left + received[pl.ds(q * rows, rows), :].astype(f32)).astype(bf16)

    keep[pl.ds(0, rows), :] = block(0)
    keep[pl.ds(rows, rows), :] = block(2)
    send[pl.ds(0, rows), :] = block(1)
    send[pl.ds(rows, rows), :] = block(3)


def plane_sum_body(ids, keep, received, kept, send):
    rows = keep.shape[0] // 2
    total = keep[...].astype(f32) + received[...].astype(f32)
    kept[...] = total[:rows]
    send[...] = total[rows:].astype(bf16)


def last_sum_body(experts, stride, ids, kept, received, kept_back, received_back, *chunks):
    first = (kept[...] + received[...].astype(f32)).astype(bf16)
    second = (kept_back[...] + received_back[...].astype(f32)).astype(bf16)
    for s in range(experts):
        chunks[s][pl.ds(0, stride), :] = first[s * stride : (s + 1) * stride]
        chunks[s][pl.ds(stride, stride), :] = second[s * stride : (s + 1) * stride]


def combine_body(experts, stride, ids, *refs):
    chunks = refs[:experts]
    slots, routes, probs, cot, residual, packed = refs[experts:]
    t = ids[2]
    length = slots.shape[1]
    probs_all = probs[...]
    choice = iota(probs_all.shape, 1)
    cot_mine = halves(cot[...], t)[0].astype(f32)
    mixture = None
    back = None
    lanes = iota((length, LANES), 1)
    dots = jnp.zeros((length, LANES), f32)
    for k in range(TOP):
        slot = columns_of(slots[k : k + 1, :])
        route = columns_of(routes[k : k + 1, :])[:, : probs_all.shape[1]]
        gate = jnp.sum(
            jnp.where(choice.astype(f32) == route, probs_all, 0.0), axis=-1, keepdims=True
        )
        chosen = None
        for s in range(experts):
            place = (iota((length, stride), 1) + s * stride).astype(f32)
            pick = (place == slot[:, :1]).astype(bf16)
            value = nn(pick, chunks[s][pl.ds(0, stride), :])
            grad = nn(pick, chunks[s][pl.ds(stride, stride), :])
            chosen = value if chosen is None else chosen + value
            back = grad if back is None else back + grad
        mixture = gate * chosen if mixture is None else mixture + gate * chosen
        dots = jnp.where(lanes == k, jnp.sum(cot_mine * chosen, axis=-1, keepdims=True), dots)
    width = back.shape[1]
    packed[:, :width] = back
    packed[:, width : 2 * width] = halves(residual[...], t)[0] + mixture
    packed[:, 2 * width :] = dots


def norm_back_body(
    experts, ids, own, other, normed, probs, residual, routes, cot, gain, router, output, grad_out, att, small
):
    even = ids[2] == 0
    width = residual.shape[1] // 2
    first, last = slice(0, width), slice(width, 2 * width)
    low = jnp.where(even, own[:, first], other[:, first])
    high = jnp.where(even, other[:, first], own[:, first])
    back = jnp.concatenate([low, high], axis=1)
    output[:, first] = jnp.where(even, own[:, last], other[:, last]).astype(bf16)
    output[:, last] = jnp.where(even, other[:, last], own[:, last]).astype(bf16)
    dots = own[:, 2 * width :] + other[:, 2 * width :]
    probs_all = probs[...]
    choice = iota(probs_all.shape, 1).astype(f32)
    grad_probs = jnp.zeros_like(probs_all)
    for k in range(TOP):
        route = columns_of(routes[k : k + 1, :])[:, : probs_all.shape[1]]
        grad_probs = grad_probs + jnp.where(choice == route, dots[:, k : k + 1], 0.0)
    inner = jnp.sum(probs_all * grad_probs, axis=-1, keepdims=True)
    grad_logits = (probs_all * (grad_probs - inner)).astype(bf16)
    grad_normed = back + nn(grad_logits, router[...])
    wide = residual[...]
    inv = lax.rsqrt(jnp.mean(wide * wide, axis=-1, keepdims=True) + eps_norm)
    scaled = grad_normed * gain[...][None, :]
    grad = (
        cot[...].astype(f32)
        + inv * scaled
        - wide * (inv * inv * inv) * jnp.mean(scaled * wide, axis=-1, keepdims=True)
    )
    grad_out[...] = grad
    att[...] = grad.astype(bf16)
    small[0:1, :] = jnp.sum(grad_normed * wide * inv, axis=0, keepdims=True)
    small[pl.ds(1, experts), :] = tn(grad_logits, normed[...])


def attend_back_body(
    ids, att, wo, q_in, k_in, v_in, mixed_in, probs, wq, wk, wv, r0, r1, r2, r3, normed_part, bias, stack
):
    q_id, t = ids[1], ids[2]
    grad = att[...]
    rows = grad.shape[0]
    lane = iota((rows, LANES), 1)
    scale = HEAD_DIM ** (-0.5)
    for pair in range(q_in.shape[1] // LANES):
        span = slice(pair * LANES, (pair + 1) * LANES)
        grad_mixed = nt(grad, wo[span, :]).astype(bf16)
        q, k, v = q_in[:, span], k_in[:, span], v_in[:, span]
        mixed = mixed_in[pl.ds(rows, rows), span].astype(f32)
        dq, dk, dv = [], [], []
        for side in range(2):
            head = pair * 2 + side
            mine = (lane < HEAD_DIM) if side == 0 else (lane >= HEAD_DIM)
            part = jnp.where(mine, grad_mixed, jnp.zeros_like(grad_mixed))
            weight = probs[head]
            dv.append(tn(weight.astype(bf16), grad_mixed))
            delta = jnp.sum(part.astype(f32) * mixed, axis=-1, keepdims=True)
            scores = weight * (nt(part, v) - delta)
            bias[0:1, head * rows : (head + 1) * rows] = sums_by_distance(scores)
            scores = scores.astype(bf16)
            dq.append(nn(scores, k))
            dk.append(tn(scores, q))
        first = lane < HEAD_DIM
        stack[0, :, span] = (jnp.where(first, dq[0], dq[1]) * scale).astype(bf16)
        stack[1, :, span] = (jnp.where(first, dk[0], dk[1]) * scale).astype(bf16)
        stack[2, :, span] = jnp.where(first, dv[0], dv[1]).astype(bf16)
    stack[3] = halves(grad, t)[0]
    r0[...] = stack[q_id]
    r1[...] = stack[q_id ^ (1 + t)]
    r2[...] = stack[q_id ^ (2 - t)]
    r3[...] = stack[q_id ^ 3]
    total = nt(stack[0], wq[...]) + nt(stack[1], wk[...]) + nt(stack[2], wv[...])
    normed_part[...] = total.astype(bf16)


def tokens_back_body(experts, ids, own, other, tokens, gain, grad_res, small_ffn, bias, out, small):
    wide = tokens[...].astype(f32)
    inv = lax.rsqrt(jnp.mean(wide * wide, axis=-1, keepdims=True) + eps_norm)
    grad_normed = own[...].astype(f32) + other[...].astype(f32)
    scaled = grad_normed * gain[...][None, :]
    out[...] = (
        grad_res[...]
        + inv * scaled
        - wide * (inv * inv * inv) * jnp.mean(scaled * wide, axis=-1, keepdims=True)
    )
    small[...] = jnp.zeros_like(small)
    small[0:1, :] = jnp.sum(grad_normed * wide * inv, axis=0, keepdims=True)
    small[1:2, :] = bias[...]
    small[pl.ds(2, 1 + experts), :] = small_ffn[...]


def encode(value):
    width = value.shape[1] // 2
    tall = jnp.concatenate([value[:, :width], value[:, width:]], axis=0)
    lead = tall.astype(bf16)
    return lead, (tall - lead.astype(f32)).astype(bf16)


def decode(ref, start, rows):
    lead = ref[pl.ds(start, 2 * rows), :].astype(f32)
    return lead + ref[pl.ds(start + 2 * rows, 2 * rows), :].astype(f32)


def widen(tall):
    rows = tall.shape[0] // 2
    return jnp.concatenate([tall[:rows], tall[rows:]], axis=1)


def partial_body(groups, ids, *refs):
    early_own, early_other = refs[:4], refs[4:8]
    right, right_pair, small = refs[8:12], refs[12:16], refs[16]
    blocks, total = refs[17:-1], refs[-1]
    e, q, t = ids[0], ids[1], ids[2]
    even = t == 0
    is_last = q == 3
    tokens = right[0].shape[0]
    rows = early_own[0].shape[0]
    width = early_own[0].shape[1]
    low, high, rights = [], [], []
    normed, mixed = pl.ds(rows - 2 * tokens, tokens), pl.ds(rows - tokens, tokens)
    for p in range(4):
        mine = jnp.where(is_last, right[p][...], early_own[p][normed, :])
        other = jnp.where(is_last, right_pair[p][...], early_other[p][normed, :])
        low.append(jnp.where(even, mine, other))
        high.append(jnp.where(even, other, mine))
        rights.append(jnp.where(is_last, early_own[p][mixed, :], right[p][...]))
    rights = jnp.concatenate(rights, axis=0)
    total[:width, :] = tn(jnp.concatenate(low, axis=0), rights)
    total[width:, :] = tn(jnp.concatenate(high, axis=0), rights)
    depth = total.shape[0] // groups
    lead, rest = encode(small[...])
    for s in range(groups):
        start = pl.multiple_of((e ^ s) * depth, 8)
        blocks[s][pl.ds(0, depth), :] = total[pl.ds(start, depth), :].astype(bf16)
        blocks[s][pl.ds(depth, lead.shape[0]), :] = lead
        blocks[s][pl.ds(depth + lead.shape[0], lead.shape[0]), :] = rest


def reduce_body(groups, rows, ids, *refs):
    arrived, outs = refs[:groups], refs[groups:]
    depth = outs[0].shape[0]
    total = arrived[0][pl.ds(0, depth), :].astype(f32)
    for ref in arrived[1:]:
        total = total + ref[pl.ds(0, depth), :].astype(f32)
    outs[0][...] = total.astype(bf16)
    code, stack = outs[1:]
    for s in range(groups):
        stack[s] = decode(arrived[s], depth, rows)
    small = stack[ids[0]]
    for k in range(1, groups):
        small = small + stack[ids[0] ^ k]
    lead = small.astype(bf16)
    code[pl.ds(0, 2 * rows), :] = lead
    code[pl.ds(2 * rows, 2 * rows), :] = (small - lead.astype(f32)).astype(bf16)


def final_body(groups, experts, rows, ids, *refs):
    pieces, hot, outs = refs[:8], refs[8], refs[9:13]
    gain_attn, bias, gain_ffn, router = refs[13:17]
    stack, square, small = refs[17:]
    e, q, t = ids[0], ids[1], ids[2]
    depth = stack.shape[2]
    per = groups // 2

    def place_of(chip):
        away = q ^ chip
        return jnp.where((t == 1) & ((away == 1) | (away == 2)), 3 - away, away)

    for p in range(4):
        for s in range(groups):
            piece = pieces[s // per * 4 + p]
            stack[p, s] = piece[pl.ds(s % per * depth, depth), :].astype(f32)
        small[p] = decode(pieces[p], per * depth, rows)
    for m in range(4):
        place = place_of(m)
        for k in range(groups):
            block = stack[place, k ^ e]
            span = pl.ds(k * depth, depth)
            if m < 3:
                outs[m][span, :] = block
            else:
                square[span, :] = block
    outs[3][...] = square[...].T
    total = widen(small[place_of(0)] + small[place_of(1)] + small[place_of(2)] + small[place_of(3)])
    gain_attn[...] = total[0]
    gain_ffn[...] = total[2]
    router[...] = total[3 : 3 + experts]
    length = hot.shape[1]
    for head in range(bias.shape[0]):
        line = jnp.broadcast_to(total[1:2, head * length : (head + 1) * length], (8, length))
        value = lax.dot_general(
            line,
            hot[...],
            (((1,), (1,)), ((), ())),
            precision=lax.Precision.HIGHEST,
            preferred_element_type=f32,
        )
        bias[head : head + 1, :] = value[0:1]


def on_device(
    n_dp,
    n_tensor,
    tokens,
    seq_ids,
    routes,
    gain_attn,
    w_query,
    w_key,
    w_value,
    w_attn_out,
    rel_bias,
    gain_ffn,
    w_router,
    expert_in,
    expert_out,
    cotangent,
):
    groups = n_dp // 4
    length, width = tokens.shape
    half = width // 2
    experts = w_router.shape[1]
    bucket_count = rel_bias.shape[1]
    heads = rel_bias.shape[0]
    local = w_query.shape[1]
    capacity = 4 * ((5 * TOP * length + 16 * experts - 1) // (16 * experts))
    stride = -(-capacity // 16) * 16
    slot_count = experts * stride
    dp_id = lax.axis_index("dp")
    t_id = lax.axis_index("tensor")
    ids = jnp.stack([dp_id // 4, dp_id % 4, t_id]).astype(jnp.int32)

    def send(array, target, only=None):
        pairs = []
        for dp in range(n_dp):
            for t in range(n_tensor):
                e_to, q_to, t_to = target(dp // 4, dp % 4, t)
                if only is None or q_to == only:
                    pairs.append((dp * n_tensor + t, (e_to * 4 + q_to) * n_tensor + t_to))
        return lax.ppermute(array, ("dp", "tensor"), pairs)

    def to_pair(e, q, t):
        return e, q, 1 - t

    def to_first(e, q, t):
        return e, q ^ (1 + t), t

    def to_second(e, q, t):
        return e, q ^ (2 - t), t

    def to_far(e, q, t):
        return e, q ^ 3, t

    def to_group(step):
        return lambda e, q, t: (e ^ step, q, t)

    def exchange(chunks):
        return [chunks[0]] + [send(chunks[s], to_group(s)) for s in range(1, len(chunks))]

    def join(arrays):
        rows = sum(a.shape[0] for a in arrays)
        return call(join_body, "join", ids, [((rows, arrays[0].shape[1]), arrays[0].dtype)], *arrays)[0]

    def spread_first(block):
        return block, send(block, to_first), send(block, to_second)

    def spread_rest(block, first, second):
        own = [block, first, second, send(first, to_second)]
        other = [send(piece, to_pair) for piece in own]
        return own, [other[0], other[2], other[1], other[3]]

    routes_t = routes.T
    gain_one, gain_two = gain_attn, gain_ffn
    router_t = w_router.T
    distance_bucket = bucket_of_distance(length, bucket_count, REACH)
    hot = (
        distance_bucket[(-np.arange(length)) % length][None, :] == np.arange(bucket_count)[:, None]
    ).astype(np.float32)
    hot = jnp.asarray(hot)

    chunk = ((stride, half), bf16)
    local_out = ((length, local), bf16)
    slots, *cot_chunks = call(
        functools.partial(route_body, experts, stride),
        "route",
        ids,
        [((TOP, length), jnp.int32)] + [chunk] * experts,
        routes_t,
        cotangent,
        scratch=[
            pltpu.VMEM((TOP, length), jnp.int32),
            pltpu.VMEM((length, width), bf16),
            pltpu.SemaphoreType.DMA((2,)),
        ],
        far=(0, 1),
    )
    cot_arrived = exchange(cot_chunks)
    early, att_part, queries, keys, values, probs = call(
        front_body,
        "front",
        ids,
        [((2 * length, half), bf16), ((length, width), f32)]
        + [local_out] * 3
        + [((heads, length, length), f32)],
        tokens,
        gain_one,
        w_query,
        w_key,
        w_value,
        rel_bias,
        hot,
        seq_ids.reshape(1, length),
        w_attn_out,
        scratch=[pltpu.VMEM((length, width), bf16), pltpu.VMEM((width,), f32)]
        + [pltpu.VMEM((width, local), bf16)] * 3
        + [
            pltpu.VMEM(rel_bias.shape, f32),
            pltpu.VMEM(hot.shape, f32),
            pltpu.VMEM((1, length), jnp.int32),
            pltpu.VMEM((local, width), bf16),
            pltpu.SemaphoreType.DMA((9,)),
        ],
        far=range(9),
    )
    att_part, *cot_arrived = lax.optimization_barrier((att_part, *cot_arrived))
    cot_near = spread_first(join(cot_arrived + [early]))
    att_other = send(att_part, to_pair)
    residual, normed_two, router_probs, *row_chunks = call(
        functools.partial(middle_body, experts, stride),
        "middle",
        ids,
        [((length, width), f32), ((length, width), bf16), ((length, experts), f32)]
        + [chunk] * experts,
        att_part,
        att_other,
        tokens,
        gain_two,
        router_t,
        slots,
    )
    *row_arrived, near, next_near = lax.optimization_barrier((*exchange(row_chunks), *cot_near[1:]))
    row_own, row_other = spread_rest(*spread_first(join(row_arrived)))
    cot_own, cot_other = spread_rest(cot_near[0], near, next_near)

    all_rows = 4 * slot_count
    rows_half = ((all_rows, half), bf16)
    units = expert_in.shape[2]
    act, slope, part_mine, part_other = call(
        functools.partial(expert_body, slot_count),
        "expert",
        ids,
        [((all_rows, units), bf16), ((all_rows, units), f32), rows_half, rows_half],
        *row_own,
        *row_other,
        expert_in,
        expert_out,
        limit=40,
    )
    two = ((2 * slot_count, half), bf16)
    one = ((slot_count, half), bf16)
    one_wide = ((slot_count, half), f32)

    keep, go = call(pair_sum_body, "pair_sum", ids, [two, two], part_mine, send(part_other, to_pair))
    part_kept, go = call(
        plane_sum_body, "plane_sum", ids, [one_wide, one], keep, send(go, to_first)
    )
    part_last = send(go, to_second)
    grad_pre, grad_mine, grad_other, back_mine, back_other = call(
        functools.partial(expert_back_body, slot_count, experts),
        "expert_back",
        ids,
        [((all_rows, units), bf16), rows_half, rows_half, rows_half, rows_half],
        *row_own,
        *row_other,
        *cot_own,
        *cot_other,
        expert_in,
        expert_out,
        router_t,
        slope,
        limit=40,
    )
    keep, go = call(pair_sum_body, "pair_sum", ids, [two, two], back_mine, send(back_other, to_pair))
    back_kept, go = call(
        plane_sum_body, "plane_sum", ids, [one_wide, one], keep, send(go, to_first)
    )
    back_last = send(go, to_second)
    grad_in, grad_out = call(
        functools.partial(expert_grads_body, slot_count),
        "expert_grads",
        ids,
        [(expert_in.shape, f32), (expert_out.shape, f32)],
        *row_own,
        *row_other,
        act,
        grad_pre,
        grad_mine,
        grad_other,
        limit=40,
    )
    part_last, back_last, grad_in, grad_out = lax.optimization_barrier(
        (part_last, back_last, grad_in, grad_out)
    )
    chunks = call(
        functools.partial(last_sum_body, experts, stride),
        "last_sum",
        ids,
        [((2 * stride, half), bf16)] * experts,
        part_kept,
        part_last,
        back_kept,
        back_last,
    )
    returned = exchange(chunks)
    packed = call(
        functools.partial(combine_body, experts, stride),
        "combine",
        ids,
        [((length, width + LANES), f32)],
        *returned,
        slots,
        routes_t,
        router_probs,
        cotangent,
        residual,
    )[0]
    output, grad_residual, grad_att, small_ffn = call(
        functools.partial(norm_back_body, experts),
        "norm_back",
        ids,
        [
            ((length, width), bf16),
            ((length, width), f32),
            ((length, width), bf16),
            ((1 + experts, width), f32),
        ],
        packed,
        send(packed, to_pair),
        normed_two,
        router_probs,
        residual,
        routes_t,
        cotangent,
        gain_two,
        router_t,
    )
    right0, right1, right2, right3, normed_part, bias = call(
        attend_back_body,
        "attend_back",
        ids,
        [local_out] * 4 + [((length, width), bf16), ((1, heads * length), f32)],
        grad_att,
        w_attn_out,
        queries,
        keys,
        values,
        early,
        probs,
        w_query,
        w_key,
        w_value,
        scratch=[pltpu.VMEM((4, length, local), bf16)],
    )
    right_all = [right0, send(right1, to_first), send(right2, to_second), send(right3, to_far)]
    small_rows = -(-(3 + experts) // 8) * 8
    grad_tokens, small = call(
        functools.partial(tokens_back_body, experts),
        "tokens_back",
        ids,
        [((length, width), f32), ((small_rows, width), f32)],
        normed_part,
        send(normed_part, to_pair),
        tokens,
        gain_one,
        grad_residual,
        small_ffn,
        bias,
    )
    right_all[1], small = lax.optimization_barrier((right_all[1], small))
    right_pair = [send(right_all[p], to_pair) for p in (0, 2, 1, 3)]
    depth = width // groups
    blocks = call(
        functools.partial(partial_body, groups),
        "partial",
        ids,
        [((depth + 4 * small_rows, local), bf16)] * groups,
        *cot_own,
        *cot_other,
        *right_all,
        *right_pair,
        small,
        scratch=[pltpu.VMEM((width, local), f32)],
    )
    reduced, code = call(
        functools.partial(reduce_body, groups, small_rows),
        "reduce",
        ids,
        [((depth, local), bf16), ((4 * small_rows, local), bf16)],
        *exchange(blocks),
        scratch=[pltpu.VMEM((groups, 2 * small_rows, local), f32)],
    )
    spread = exchange([reduced] * groups)
    near, rest = spread[: groups // 2], spread[groups // 2 :]
    matrix = join(near + [code])
    first, second = send(matrix, to_first), send(matrix, to_second)
    *rest, first, second = lax.optimization_barrier((*rest, first, second))
    far = send(first, to_second)
    matrix_two = join(list(rest))
    first_two, second_two = send(matrix_two, to_first), send(matrix_two, to_second)
    far_two = send(second_two, to_first)
    grads = call(
        functools.partial(final_body, groups, experts, small_rows),
        "final",
        ids,
        [((width, local), f32)] * 3
        + [((local, width), f32), ((width,), f32), ((heads, bucket_count), f32)]
        + [((width,), f32), ((experts, width), f32)],
        matrix,
        first,
        second,
        far,
        matrix_two,
        first_two,
        second_two,
        far_two,
        hot,
        scratch=[
            pltpu.VMEM((4, groups, depth, local), f32),
            pltpu.VMEM((width, local), f32),
            pltpu.VMEM((4, 2 * small_rows, local), f32),
        ],
        limit=40,
    )
    return (
        output,
        grad_tokens,
        grads[4],
        grads[0],
        grads[1],
        grads[2],
        grads[3],
        grads[5],
        grads[6],
        grads[7].T,
        grad_in,
        grad_out,
    )


def solution(mesh):
    in_specs = (
        P("dp", None),
        P("dp"),
        P("dp", None),
        P(),
        P(None, "tensor"),
        P(None, "tensor"),
        P(None, "tensor"),
        P("tensor", None),
        P("tensor", None),
        P(),
        P(),
        P("dp", None, "tensor"),
        P("dp", "tensor", None),
        P("dp", None),
    )
    out_specs = (
        P("dp", None),
        P("dp", None),
        P(),
        P(None, "tensor"),
        P(None, "tensor"),
        P(None, "tensor"),
        P("tensor", None),
        P("tensor", None),
        P(),
        P(),
        P("dp", None, "tensor"),
        P("dp", "tensor", None),
    )
    return jax.shard_map(
        functools.partial(on_device, mesh.shape["dp"], mesh.shape["tensor"]),
        mesh=mesh,
        in_specs=in_specs,
        out_specs=out_specs,
        check_vma=False,
    )
```

```python
import functools

import jax
import jax.numpy as jnp
import numpy as np
from jax import lax
from jax.experimental import pallas as pl
from jax.experimental.pallas import tpu as pltpu
from jax.sharding import PartitionSpec as P

HEAD_DIM = 64
TOP = 2
REACH = 64
LANES = 128

eps_norm = 1e-06
gelu_scale = float(np.sqrt(2.0 / np.pi))
microseconds = {"front": 5, "route": 1.9, "expert": 4.4, "expert_back": 5.4, "expert_grads": 4.0, "combine": 1.9, "attend_back": 2.5, "partial": 1.2, "final": 3.9, "tokens_back": 1.5, "small": 1.4}
f32 = jnp.float32
bf16 = jnp.bfloat16


def bucket_of_distance(length, buckets, max_reach):
    exact_span = buckets // 2
    distance = np.arange(length)
    log_ratio = np.log(np.maximum(distance, exact_span) / exact_span) / np.log(
        max_reach / exact_span
    )
    coarse = exact_span + np.floor(log_ratio * (buckets - exact_span)).astype(np.int64)
    return np.where(distance < exact_span, distance, np.minimum(coarse, buckets - 1))


def nn(left, right, precision=None):
    return lax.dot_general(
        left, right, (((1,), (0,)), ((), ())), precision=precision, preferred_element_type=f32
    )


def nt(left, right):
    return lax.dot_general(left, right, (((1,), (1,)), ((), ())), preferred_element_type=f32)


def tn(left, right):
    return lax.dot_general(left, right, (((0,), (0,)), ((), ())), preferred_element_type=f32)


def iota(shape, axis):
    return lax.broadcasted_iota(jnp.int32, shape, axis)


def call(body, name, ids, outs, *args, scratch=(), limit=24, far=()):
    shapes = [jax.ShapeDtypeStruct(shape, dtype) for shape, dtype in outs]
    return pl.pallas_call(
        body,
        out_shape=shapes,
        in_specs=[pl.BlockSpec(memory_space=pltpu.SMEM)]
        + [
            pl.BlockSpec(memory_space=pltpu.HBM if i in far else pltpu.VMEM)
            for i in range(len(args))
        ],
        out_specs=[pl.BlockSpec(memory_space=pltpu.VMEM)] * len(outs),
        scratch_shapes=list(scratch),
        compiler_params=pltpu.CompilerParams(vmem_limit_bytes=limit << 20),
        cost_estimate=pl.CostEstimate(
            flops=0, transcendentals=0, bytes_accessed=int(microseconds.get(name, 0.8) * 3.6e6)
        ),
        name=name,
    )(
        ids,
        *[
            pltpu.with_memory_space_constraint(a, pltpu.HBM) if i in far else a
            for i, a in enumerate(args)
        ],
    )


def halves(value, t):
    width = value.shape[1] // 2
    low, high = value[:, :width], value[:, width:]
    even = t == 0
    return jnp.where(even, low, high), jnp.where(even, high, low)


def row_halves(value, t):
    width = value.shape[0] // 2
    low, high = value[:width], value[width:]
    even = t == 0
    return jnp.where(even, low, high), jnp.where(even, high, low)


def columns_of(row):
    length = row.shape[1]
    return jnp.broadcast_to(row.astype(f32), (length, length)).T


def sums_by_distance(square):
    length = square.shape[0]
    rows = length // 2
    while rows >= 1:
        square = square[:rows] + pltpu.roll(square[rows:], length - rows, 1)
        rows //= 2
    return square


def fetch(sources, targets, sems):
    copies = [
        pltpu.make_async_copy(source, target, sems.at[i])
        for i, (source, target) in enumerate(zip(sources, targets))
    ]
    for copy in copies:
        copy.start()
    return copies


def route_body(experts, stride, ids, routes_far, cot_far, slots, *refs):
    chunks, (routes, cot, sems) = refs[:experts], refs[experts:]
    copies = fetch((routes_far, cot_far), (routes, cot), sems)
    copies[0].wait()
    e, t = ids[0], ids[2]
    length = routes.shape[1]
    expert_row = iota((experts, length), 0)
    first = (expert_row == routes[0:1, :]).astype(f32)
    second = (expert_row == routes[1:2, :]).astype(f32)
    earlier = (iota((length, length), 0) < iota((length, length), 1)).astype(bf16)
    before = nn((first + second).astype(bf16), earlier)
    rank0 = jnp.sum(before * first, axis=0, keepdims=True).astype(jnp.int32)
    rank1 = jnp.sum(before * second, axis=0, keepdims=True).astype(jnp.int32)
    slot0 = (routes[0:1, :] ^ e) * stride + rank0
    slot1 = (routes[1:2, :] ^ e) * stride + rank1
    slots[0:1, :] = slot0
    slots[1:2, :] = slot1
    copies[1].wait()
    mine, _ = halves(cot[...], t)
    for s in range(experts):
        place = iota((stride, length), 0) + s * stride
        pick = ((place == slot0) | (place == slot1)).astype(bf16)
        chunks[s][...] = nn(pick, mine).astype(bf16)


def front_body(ids, *refs):
    sources = refs[:9]
    early, part, q_out, k_out, v_out, probs = refs[9:15]
    targets, sems = refs[15:-1], refs[-1]
    tokens, gain, wq, wk, wv, rel, hot, seq, wo = targets
    copies = fetch(sources, targets, sems)
    t = ids[2]
    length = tokens.shape[0]
    mixed_out = early.at[pl.ds(length, length), :]
    copies[0].wait()
    copies[1].wait()
    wide = tokens[...].astype(f32)
    inv = lax.rsqrt(jnp.mean(wide * wide, axis=-1, keepdims=True) + eps_norm)
    value = (wide * inv * gain[...][None, :]).astype(bf16)
    early[pl.ds(0, length), :] = halves(value, t)[0]
    rows = length
    copies[2].wait()
    queries = nn(value, wq[...]).astype(bf16)
    copies[3].wait()
    keys = nn(value, wk[...]).astype(bf16)
    copies[4].wait()
    values = nn(value, wv[...]).astype(bf16)
    q_out[...] = queries
    k_out[...] = keys
    v_out[...] = values
    for copy in copies[5:8]:
        copy.wait()
    seq_cols = jnp.broadcast_to(seq[...].astype(f32), (rows, rows))
    allowed = (seq_cols == seq_cols.T) & (iota((rows, rows), 0) >= iota((rows, rows), 1))
    table = nn(rel[...], hot[...], lax.Precision.HIGHEST)
    lane = iota((rows, LANES), 1)
    for pair in range(queries.shape[1] // LANES):
        span = slice(pair * LANES, (pair + 1) * LANES)
        q, k, v = queries[:, span], keys[:, span], values[:, span]
        mixed = []
        for side in range(2):
            head = pair * 2 + side
            mine = (lane < HEAD_DIM) if side == 0 else (lane >= HEAD_DIM)
            raw = nt(jnp.where(mine, q, jnp.zeros_like(q)), k)
            bias = pltpu.roll(
                jnp.broadcast_to(table[head : head + 1, :], (rows, rows)),
                0,
                1,
                stride=1,
                stride_axis=0,
            )
            scores = jnp.where(allowed, raw * HEAD_DIM ** (-0.5) + bias, -1e30)
            top = jnp.max(scores, axis=-1, keepdims=True)
            raised = jnp.exp(scores - top)
            weight = raised / jnp.sum(raised, axis=-1, keepdims=True)
            probs[head] = weight
            mixed.append(nn(weight.astype(bf16), v))
        mixed_out[:, span] = jnp.where(lane < HEAD_DIM, mixed[0], mixed[1]).astype(bf16)
    copies[8].wait()
    part[...] = nn(mixed_out[...], wo[...])


def router_of(normed, weights_row):
    logits = nt(normed, weights_row)
    raised = jnp.exp(logits - jnp.max(logits, axis=-1, keepdims=True))
    return raised / jnp.sum(raised, axis=-1, keepdims=True)


def middle_body(experts, stride, ids, own, other, tokens, gain, router, slots, residual, normed, probs, *chunks):
    t = ids[2]
    wide = tokens[...].astype(f32) + (own[...] + other[...])
    residual[...] = wide
    inv = lax.rsqrt(jnp.mean(wide * wide, axis=-1, keepdims=True) + eps_norm)
    value = (wide * inv * gain[...][None, :]).astype(bf16)
    normed[...] = value
    mine, _ = halves(value, t)
    length = slots.shape[1]
    for s in range(experts):
        place = iota((stride, length), 0) + s * stride
        pick = ((place == slots[0:1, :]) | (place == slots[1:2, :])).astype(bf16)
        chunks[s][...] = nn(pick, mine).astype(bf16)
    probs[...] = router_of(value, router[...])


def join_body(ids, *refs):
    out = refs[-1]
    start = 0
    for ref in refs[:-1]:
        out[pl.ds(start, ref.shape[0]), :] = ref[...]
        start += ref.shape[0]


def in_order(own, other, even):
    return jnp.concatenate([jnp.where(even, own, other), jnp.where(even, other, own)], axis=1)


def expert_body(rows, ids, *refs):
    own, other = refs[:4], refs[4:8]
    w_in, w_out, act, slope, part_mine, part_other = refs[8:]
    t = ids[2]
    for p in range(4):
        span = pl.ds(p * rows, rows)
        pre = nn(in_order(own[p][...], other[p][...], t == 0), w_in[0])
        square = pre * pre
        bent = jnp.tanh(gelu_scale * (pre + 0.044715 * pre * square))
        half = 0.5 * (1.0 + bent)
        value = (pre * half).astype(bf16)
        act[span, :] = value
        slope[span, :] = half + 0.5 * pre * (1.0 - bent * bent) * (
            gelu_scale * (1.0 + 3 * 0.044715 * square)
        )
        mine, rest = halves(nn(value, w_out[0]).astype(bf16), t)
        part_mine[span, :] = mine
        part_other[span, :] = rest


def expert_back_body(rows, experts, ids, *refs):
    own, other, cot_own, cot_other = refs[:4], refs[4:8], refs[8:12], refs[12:16]
    w_in, w_out, router, slope, grad_pre, grads, back_mine, back_other = refs[16:]
    e, t = ids[0], ids[2]
    for p in range(4):
        span = pl.ds(p * rows, rows)
        cot_rows = pl.ds(0, rows)
        logits = nt(in_order(own[p][...], other[p][...], t == 0), router[...])
        raised = jnp.exp(logits - jnp.max(logits, axis=-1, keepdims=True))
        chosen = jnp.where(iota(raised.shape, 1) == e, raised, 0.0)
        gate = jnp.sum(chosen, axis=-1, keepdims=True) / jnp.sum(raised, axis=-1, keepdims=True)
        cot = in_order(cot_own[p][cot_rows, :], cot_other[p][cot_rows, :], t == 0)
        grad = (gate * cot.astype(f32)).astype(bf16)
        grads[span, :] = grad
        value = (nt(grad, w_out[0]) * slope[span, :]).astype(bf16)
        grad_pre[span, :] = value
        mine, rest = halves(nt(value, w_in[0]).astype(bf16), t)
        back_mine[span, :] = mine
        back_other[span, :] = rest


def expert_grads_body(rows, ids, *refs):
    own, other = refs[:4], refs[4:8]
    act, grad_pre, grads, out_in, out_out = refs[8:]
    even = ids[2] == 0
    out_out[0] = tn(act[...], grads[...])
    sent = jnp.concatenate([in_order(own[p][...], other[p][...], even) for p in range(4)], axis=0)
    out_in[0] = tn(sent, grad_pre[...])


def pair_sum_body(ids, mine, received, keep, send):
    rows = mine.shape[0] // 4

    def block(p):
        q = (0, 2, 1, 3)[p]
        left = mine[pl.ds(p * rows, rows), :].astype(f32)
        return (left + received[pl.ds(q * rows, rows), :].astype(f32)).astype(bf16)

    keep[pl.ds(0, rows), :] = block(0)
    keep[pl.ds(rows, rows), :] = block(2)
    send[pl.ds(0, rows), :] = block(1)
    send[pl.ds(rows, rows), :] = block(3)


def plane_sum_body(ids, keep, received, kept, send):
    rows = keep.shape[0] // 2
    total = keep[...].astype(f32) + received[...].astype(f32)
    kept[...] = total[:rows]
    send[...] = total[rows:].astype(bf16)


def last_sum_body(experts, stride, ids, kept, received, kept_back, received_back, *chunks):
    first = (kept[...] + received[...].astype(f32)).astype(bf16)
    second = (kept_back[...] + received_back[...].astype(f32)).astype(bf16)
    for s in range(experts):
        chunks[s][pl.ds(0, stride), :] = first[s * stride : (s + 1) * stride]
        chunks[s][pl.ds(stride, stride), :] = second[s * stride : (s + 1) * stride]


def combine_body(experts, stride, ids, *refs):
    chunks = refs[:experts]
    slots, routes, probs, cot, residual, packed = refs[experts:]
    t = ids[2]
    length = slots.shape[1]
    probs_all = probs[...]
    choice = iota(probs_all.shape, 1)
    cot_mine = halves(cot[...], t)[0].astype(f32)
    mixture = None
    back = None
    lanes = iota((length, LANES), 1)
    dots = jnp.zeros((length, LANES), f32)
    for k in range(TOP):
        slot = columns_of(slots[k : k + 1, :])
        route = columns_of(routes[k : k + 1, :])[:, : probs_all.shape[1]]
        gate = jnp.sum(
            jnp.where(choice.astype(f32) == route, probs_all, 0.0), axis=-1, keepdims=True
        )
        chosen = None
        for s in range(experts):
            place = (iota((length, stride), 1) + s * stride).astype(f32)
            pick = (place == slot[:, :1]).astype(bf16)
            value = nn(pick, chunks[s][pl.ds(0, stride), :])
            grad = nn(pick, chunks[s][pl.ds(stride, stride), :])
            chosen = value if chosen is None else chosen + value
            back = grad if back is None else back + grad
        mixture = gate * chosen if mixture is None else mixture + gate * chosen
        dots = jnp.where(lanes == k, jnp.sum(cot_mine * chosen, axis=-1, keepdims=True), dots)
    width = back.shape[1]
    packed[:, :width] = back
    packed[:, width : 2 * width] = halves(residual[...], t)[0] + mixture
    packed[:, 2 * width :] = dots


def norm_back_body(
    experts, ids, own, other, normed, probs, residual, routes, cot, gain, router, output, grad_out, att, small
):
    even = ids[2] == 0
    width = residual.shape[1] // 2
    first, last = slice(0, width), slice(width, 2 * width)
    low = jnp.where(even, own[:, first], other[:, first])
    high = jnp.where(even, other[:, first], own[:, first])
    back = jnp.concatenate([low, high], axis=1)
    output[:, first] = jnp.where(even, own[:, last], other[:, last]).astype(bf16)
    output[:, last] = jnp.where(even, other[:, last], own[:, last]).astype(bf16)
    dots = own[:, 2 * width :] + other[:, 2 * width :]
    probs_all = probs[...]
    choice = iota(probs_all.shape, 1).astype(f32)
    grad_probs = jnp.zeros_like(probs_all)
    for k in range(TOP):
        route = columns_of(routes[k : k + 1, :])[:, : probs_all.shape[1]]
        grad_probs = grad_probs + jnp.where(choice == route, dots[:, k : k + 1], 0.0)
    inner = jnp.sum(probs_all * grad_probs, axis=-1, keepdims=True)
    grad_logits = (probs_all * (grad_probs - inner)).astype(bf16)
    grad_normed = back + nn(grad_logits, router[...])
    wide = residual[...]
    inv = lax.rsqrt(jnp.mean(wide * wide, axis=-1, keepdims=True) + eps_norm)
    scaled = grad_normed * gain[...][None, :]
    grad = (
        cot[...].astype(f32)
        + inv * scaled
        - wide * (inv * inv * inv) * jnp.mean(scaled * wide, axis=-1, keepdims=True)
    )
    grad_out[...] = grad
    att[...] = grad.astype(bf16)
    small[0:1, :] = jnp.sum(grad_normed * wide * inv, axis=0, keepdims=True)
    small[pl.ds(1, experts), :] = tn(grad_logits, normed[...])


def attend_back_body(
    ids, att, wo, q_in, k_in, v_in, mixed_in, probs, wq, wk, wv, r0, r1, r2, r3, normed_part, bias, stack
):
    q_id, t = ids[1], ids[2]
    grad = att[...]
    rows = grad.shape[0]
    lane = iota((rows, LANES), 1)
    scale = HEAD_DIM ** (-0.5)
    for pair in range(q_in.shape[1] // LANES):
        span = slice(pair * LANES, (pair + 1) * LANES)
        grad_mixed = nt(grad, wo[span, :]).astype(bf16)
        q, k, v = q_in[:, span], k_in[:, span], v_in[:, span]
        mixed = mixed_in[pl.ds(rows, rows), span].astype(f32)
        dq, dk, dv = [], [], []
        for side in range(2):
            head = pair * 2 + side
            mine = (lane < HEAD_DIM) if side == 0 else (lane >= HEAD_DIM)
            part = jnp.where(mine, grad_mixed, jnp.zeros_like(grad_mixed))
            weight = probs[head]
            dv.append(tn(weight.astype(bf16), grad_mixed))
            delta = jnp.sum(part.astype(f32) * mixed, axis=-1, keepdims=True)
            scores = weight * (nt(part, v) - delta)
            bias[0:1, head * rows : (head + 1) * rows] = sums_by_distance(scores)
            scores = scores.astype(bf16)
            dq.append(nn(scores, k))
            dk.append(tn(scores, q))
        first = lane < HEAD_DIM
        stack[0, :, span] = (jnp.where(first, dq[0], dq[1]) * scale).astype(bf16)
        stack[1, :, span] = (jnp.where(first, dk[0], dk[1]) * scale).astype(bf16)
        stack[2, :, span] = jnp.where(first, dv[0], dv[1]).astype(bf16)
    stack[3] = halves(grad, t)[0]
    r0[...] = stack[q_id]
    r1[...] = stack[q_id ^ (1 + t)]
    r2[...] = stack[q_id ^ (2 - t)]
    r3[...] = stack[q_id ^ 3]
    total = nt(stack[0], wq[...]) + nt(stack[1], wk[...]) + nt(stack[2], wv[...])
    normed_part[...] = total.astype(bf16)


def tokens_back_body(experts, ids, own, other, tokens, gain, grad_res, small_ffn, bias, out, small):
    wide = tokens[...].astype(f32)
    inv = lax.rsqrt(jnp.mean(wide * wide, axis=-1, keepdims=True) + eps_norm)
    grad_normed = own[...].astype(f32) + other[...].astype(f32)
    scaled = grad_normed * gain[...][None, :]
    out[...] = (
        grad_res[...]
        + inv * scaled
        - wide * (inv * inv * inv) * jnp.mean(scaled * wide, axis=-1, keepdims=True)
    )
    small[...] = jnp.zeros_like(small)
    small[0:1, :] = jnp.sum(grad_normed * wide * inv, axis=0, keepdims=True)
    small[1:2, :] = bias[...]
    small[pl.ds(2, 1 + experts), :] = small_ffn[...]


def encode(value):
    width = value.shape[1] // 2
    tall = jnp.concatenate([value[:, :width], value[:, width:]], axis=0)
    lead = tall.astype(bf16)
    return lead, (tall - lead.astype(f32)).astype(bf16)


def decode(ref, start, rows):
    lead = ref[pl.ds(start, 2 * rows), :].astype(f32)
    return lead + ref[pl.ds(start + 2 * rows, 2 * rows), :].astype(f32)


def widen(tall):
    rows = tall.shape[0] // 2
    return jnp.concatenate([tall[:rows], tall[rows:]], axis=1)


def partial_body(groups, ids, *refs):
    early_own, early_other = refs[:4], refs[4:8]
    right, right_pair, small = refs[8:12], refs[12:16], refs[16]
    blocks, total = refs[17:-1], refs[-1]
    e, q, t = ids[0], ids[1], ids[2]
    even = t == 0
    is_last = q == 3
    tokens = right[0].shape[0]
    rows = early_own[0].shape[0]
    width = early_own[0].shape[1]
    low, high, rights = [], [], []
    normed, mixed = pl.ds(rows - 2 * tokens, tokens), pl.ds(rows - tokens, tokens)
    for p in range(4):
        mine = jnp.where(is_last, right[p][...], early_own[p][normed, :])
        other = jnp.where(is_last, right_pair[p][...], early_other[p][normed, :])
        low.append(jnp.where(even, mine, other))
        high.append(jnp.where(even, other, mine))
        rights.append(jnp.where(is_last, early_own[p][mixed, :], right[p][...]))
    rights = jnp.concatenate(rights, axis=0)
    total[:width, :] = tn(jnp.concatenate(low, axis=0), rights)
    total[width:, :] = tn(jnp.concatenate(high, axis=0), rights)
    depth = total.shape[0] // groups
    lead, rest = encode(small[...])
    for s in range(groups):
        start = pl.multiple_of((e ^ s) * depth, 8)
        blocks[s][pl.ds(0, depth), :] = total[pl.ds(start, depth), :].astype(bf16)
        blocks[s][pl.ds(depth, lead.shape[0]), :] = lead
        blocks[s][pl.ds(depth + lead.shape[0], lead.shape[0]), :] = rest


def reduce_body(groups, rows, ids, *refs):
    arrived, outs = refs[:groups], refs[groups:]
    depth = outs[0].shape[0]
    total = arrived[0][pl.ds(0, depth), :].astype(f32)
    for ref in arrived[1:]:
        total = total + ref[pl.ds(0, depth), :].astype(f32)
    outs[0][...] = total.astype(bf16)
    code, stack = outs[1:]
    for s in range(groups):
        stack[s] = decode(arrived[s], depth, rows)
    small = stack[ids[0]]
    for k in range(1, groups):
        small = small + stack[ids[0] ^ k]
    lead = small.astype(bf16)
    code[pl.ds(0, 2 * rows), :] = lead
    code[pl.ds(2 * rows, 2 * rows), :] = (small - lead.astype(f32)).astype(bf16)


def final_body(groups, experts, rows, ids, *refs):
    pieces, hot, outs = refs[:8], refs[8], refs[9:13]
    gain_attn, bias, gain_ffn, router = refs[13:17]
    square, small = refs[17:]
    e, q, t = ids[0], ids[1], ids[2]
    depth = square.shape[0] // groups
    per = groups - 1

    def place_of(chip):
        away = q ^ chip
        return jnp.where((t == 1) & ((away == 1) | (away == 2)), 3 - away, away)

    for p in range(4):
        small[p] = decode(pieces[p], per * depth, rows)
    for m in range(4):
        out = outs[m] if m < 3 else square
        place = place_of(m)
        for p in range(4):

            @pl.when(place == p)
            def _(p=p, out=out):
                for s in range(groups):
                    start = pl.multiple_of((s ^ e) * depth, 8)
                    piece = pieces[s // per * 4 + p]
                    out[pl.ds(start, depth), :] = piece[pl.ds(s % per * depth, depth), :].astype(f32)

    outs[3][...] = square[...].T
    total = widen(small[place_of(0)] + small[place_of(1)] + small[place_of(2)] + small[place_of(3)])
    gain_attn[...] = total[0]
    gain_ffn[...] = total[2]
    router[...] = total[3 : 3 + experts]
    length = hot.shape[1]
    for head in range(bias.shape[0]):
        line = jnp.broadcast_to(total[1:2, head * length : (head + 1) * length], (8, length))
        value = lax.dot_general(
            line,
            hot[...],
            (((1,), (1,)), ((), ())),
            precision=lax.Precision.HIGHEST,
            preferred_element_type=f32,
        )
        bias[head : head + 1, :] = value[0:1]


def on_device(
    n_dp,
    n_tensor,
    tokens,
    seq_ids,
    routes,
    gain_attn,
    w_query,
    w_key,
    w_value,
    w_attn_out,
    rel_bias,
    gain_ffn,
    w_router,
    expert_in,
    expert_out,
    cotangent,
):
    groups = n_dp // 4
    length, width = tokens.shape
    half = width // 2
    experts = w_router.shape[1]
    bucket_count = rel_bias.shape[1]
    heads = rel_bias.shape[0]
    local = w_query.shape[1]
    capacity = 4 * ((5 * TOP * length + 16 * experts - 1) // (16 * experts))
    stride = -(-capacity // 16) * 16
    slot_count = experts * stride
    dp_id = lax.axis_index("dp")
    t_id = lax.axis_index("tensor")
    ids = jnp.stack([dp_id // 4, dp_id % 4, t_id]).astype(jnp.int32)

    def send(array, target, only=None):
        pairs = []
        for dp in range(n_dp):
            for t in range(n_tensor):
                e_to, q_to, t_to = target(dp // 4, dp % 4, t)
                if only is None or q_to == only:
                    pairs.append((dp * n_tensor + t, (e_to * 4 + q_to) * n_tensor + t_to))
        return lax.ppermute(array, ("dp", "tensor"), pairs)

    def to_pair(e, q, t):
        return e, q, 1 - t

    def to_first(e, q, t):
        return e, q ^ (1 + t), t

    def to_second(e, q, t):
        return e, q ^ (2 - t), t

    def to_far(e, q, t):
        return e, q ^ 3, t

    def to_group(step):
        return lambda e, q, t: (e ^ step, q, t)

    def exchange(chunks):
        return [chunks[0]] + [send(chunks[s], to_group(s)) for s in range(1, len(chunks))]

    def join(arrays):
        rows = sum(a.shape[0] for a in arrays)
        return call(join_body, "join", ids, [((rows, arrays[0].shape[1]), arrays[0].dtype)], *arrays)[0]

    def spread_first(block):
        return block, send(block, to_first), send(block, to_second)

    def spread_rest(block, first, second):
        own = [block, first, second, send(first, to_second)]
        other = [send(piece, to_pair) for piece in own]
        return own, [other[0], other[2], other[1], other[3]]

    routes_t = routes.T
    gain_one, gain_two = gain_attn, gain_ffn
    router_t = w_router.T
    distance_bucket = bucket_of_distance(length, bucket_count, REACH)
    hot = (
        distance_bucket[(-np.arange(length)) % length][None, :] == np.arange(bucket_count)[:, None]
    ).astype(np.float32)
    hot = jnp.asarray(hot)

    chunk = ((stride, half), bf16)
    local_out = ((length, local), bf16)
    slots, *cot_chunks = call(
        functools.partial(route_body, experts, stride),
        "route",
        ids,
        [((TOP, length), jnp.int32)] + [chunk] * experts,
        routes_t,
        cotangent,
        scratch=[
            pltpu.VMEM((TOP, length), jnp.int32),
            pltpu.VMEM((length, width), bf16),
            pltpu.SemaphoreType.DMA((2,)),
        ],
        far=(0, 1),
    )
    cot_arrived = exchange(cot_chunks)
    early, att_part, queries, keys, values, probs = call(
        front_body,
        "front",
        ids,
        [((2 * length, half), bf16), ((length, width), f32)]
        + [local_out] * 3
        + [((heads, length, length), f32)],
        tokens,
        gain_one,
        w_query,
        w_key,
        w_value,
        rel_bias,
        hot,
        seq_ids.reshape(1, length),
        w_attn_out,
        scratch=[pltpu.VMEM((length, width), bf16), pltpu.VMEM((width,), f32)]
        + [pltpu.VMEM((width, local), bf16)] * 3
        + [
            pltpu.VMEM(rel_bias.shape, f32),
            pltpu.VMEM(hot.shape, f32),
            pltpu.VMEM((1, length), jnp.int32),
            pltpu.VMEM((local, width), bf16),
            pltpu.SemaphoreType.DMA((9,)),
        ],
        far=range(9),
    )
    att_part, *cot_arrived = lax.optimization_barrier((att_part, *cot_arrived))
    cot_near = spread_first(join(cot_arrived + [early]))
    att_other = send(att_part, to_pair)
    residual, normed_two, router_probs, *row_chunks = call(
        functools.partial(middle_body, experts, stride),
        "middle",
        ids,
        [((length, width), f32), ((length, width), bf16), ((length, experts), f32)]
        + [chunk] * experts,
        att_part,
        att_other,
        tokens,
        gain_two,
        router_t,
        slots,
    )
    *row_arrived, near, next_near = lax.optimization_barrier((*exchange(row_chunks), *cot_near[1:]))
    row_own, row_other = spread_rest(*spread_first(join(row_arrived)))
    cot_own, cot_other = spread_rest(cot_near[0], near, next_near)

    all_rows = 4 * slot_count
    rows_half = ((all_rows, half), bf16)
    units = expert_in.shape[2]
    act, slope, part_mine, part_other = call(
        functools.partial(expert_body, slot_count),
        "expert",
        ids,
        [((all_rows, units), bf16), ((all_rows, units), f32), rows_half, rows_half],
        *row_own,
        *row_other,
        expert_in,
        expert_out,
        limit=40,
    )
    two = ((2 * slot_count, half), bf16)
    one = ((slot_count, half), bf16)
    one_wide = ((slot_count, half), f32)

    keep, go = call(pair_sum_body, "pair_sum", ids, [two, two], part_mine, send(part_other, to_pair))
    part_kept, go = call(
        plane_sum_body, "plane_sum", ids, [one_wide, one], keep, send(go, to_first)
    )
    part_last = send(go, to_second)
    grad_pre, expert_cot, back_mine, back_other = call(
        functools.partial(expert_back_body, slot_count, experts),
        "expert_back",
        ids,
        [((all_rows, units), bf16), ((all_rows, width), bf16), rows_half, rows_half],
        *row_own,
        *row_other,
        *cot_own,
        *cot_other,
        expert_in,
        expert_out,
        router_t,
        slope,
        limit=40,
    )
    keep, go = call(pair_sum_body, "pair_sum", ids, [two, two], back_mine, send(back_other, to_pair))
    back_kept, go = call(
        plane_sum_body, "plane_sum", ids, [one_wide, one], keep, send(go, to_first)
    )
    back_last = send(go, to_second)
    grad_in, grad_out = call(
        functools.partial(expert_grads_body, slot_count),
        "expert_grads",
        ids,
        [(expert_in.shape, f32), (expert_out.shape, f32)],
        *row_own,
        *row_other,
        act,
        grad_pre,
        expert_cot,
        limit=40,
    )
    part_last, back_last, grad_in, grad_out = lax.optimization_barrier(
        (part_last, back_last, grad_in, grad_out)
    )
    chunks = call(
        functools.partial(last_sum_body, experts, stride),
        "last_sum",
        ids,
        [((2 * stride, half), bf16)] * experts,
        part_kept,
        part_last,
        back_kept,
        back_last,
    )
    returned = exchange(chunks)
    packed = call(
        functools.partial(combine_body, experts, stride),
        "combine",
        ids,
        [((length, width + LANES), f32)],
        *returned,
        slots,
        routes_t,
        router_probs,
        cotangent,
        residual,
    )[0]
    output, grad_residual, grad_att, small_ffn = call(
        functools.partial(norm_back_body, experts),
        "norm_back",
        ids,
        [
            ((length, width), bf16),
            ((length, width), f32),
            ((length, width), bf16),
            ((1 + experts, width), f32),
        ],
        packed,
        send(packed, to_pair),
        normed_two,
        router_probs,
        residual,
        routes_t,
        cotangent,
        gain_two,
        router_t,
    )
    right0, right1, right2, right3, normed_part, bias = call(
        attend_back_body,
        "attend_back",
        ids,
        [local_out] * 4 + [((length, width), bf16), ((1, heads * length), f32)],
        grad_att,
        w_attn_out,
        queries,
        keys,
        values,
        early,
        probs,
        w_query,
        w_key,
        w_value,
        scratch=[pltpu.VMEM((4, length, local), bf16)],
    )
    right_all = [right0, send(right1, to_first), send(right2, to_second), send(right3, to_far)]
    small_rows = -(-(3 + experts) // 8) * 8
    grad_tokens, small = call(
        functools.partial(tokens_back_body, experts),
        "tokens_back",
        ids,
        [((length, width), f32), ((small_rows, width), f32)],
        normed_part,
        send(normed_part, to_pair),
        tokens,
        gain_one,
        grad_residual,
        small_ffn,
        bias,
    )
    *right_all, small = lax.optimization_barrier((*right_all, small))
    right_pair = [send(right_all[p], to_pair) for p in (0, 2, 1, 3)]
    depth = width // groups
    blocks = call(
        functools.partial(partial_body, groups),
        "partial",
        ids,
        [((depth + 4 * small_rows, local), bf16)] * groups,
        *cot_own,
        *cot_other,
        *right_all,
        *right_pair,
        small,
        scratch=[pltpu.VMEM((width, local), f32)],
    )
    reduced, code = call(
        functools.partial(reduce_body, groups, small_rows),
        "reduce",
        ids,
        [((depth, local), bf16), ((4 * small_rows, local), bf16)],
        *exchange(blocks),
        scratch=[pltpu.VMEM((groups, 2 * small_rows, local), f32)],
    )
    spread = exchange([reduced] * groups)
    near, rest = spread[:-1], spread[-1:]
    matrix = join(near + [code])
    first, second = send(matrix, to_first), send(matrix, to_second)
    *rest, first, second = lax.optimization_barrier((*rest, first, second))
    far = send(first, to_second)
    matrix_two = rest[0]
    first_two, second_two = send(matrix_two, to_first), send(matrix_two, to_second)
    far_two = send(matrix_two, to_far)
    grads = call(
        functools.partial(final_body, groups, experts, small_rows),
        "final",
        ids,
        [((width, local), f32)] * 3
        + [((local, width), f32), ((width,), f32), ((heads, bucket_count), f32)]
        + [((width,), f32), ((experts, width), f32)],
        matrix,
        first,
        second,
        far,
        matrix_two,
        first_two,
        second_two,
        far_two,
        hot,
        scratch=[
            pltpu.VMEM((width, local), f32),
            pltpu.VMEM((4, 2 * small_rows, local), f32),
        ],
        limit=40,
    )
    return (
        output,
        grad_tokens,
        grads[4],
        grads[0],
        grads[1],
        grads[2],
        grads[3],
        grads[5],
        grads[6],
        grads[7].T,
        grad_in,
        grad_out,
    )


def solution(mesh):
    in_specs = (
        P("dp", None),
        P("dp"),
        P("dp", None),
        P(),
        P(None, "tensor"),
        P(None, "tensor"),
        P(None, "tensor"),
        P("tensor", None),
        P("tensor", None),
        P(),
        P(),
        P("dp", None, "tensor"),
        P("dp", "tensor", None),
        P("dp", None),
    )
    out_specs = (
        P("dp", None),
        P("dp", None),
        P(),
        P(None, "tensor"),
        P(None, "tensor"),
        P(None, "tensor"),
        P("tensor", None),
        P("tensor", None),
        P(),
        P(),
        P("dp", None, "tensor"),
        P("dp", "tensor", None),
    )
    return jax.shard_map(
        functools.partial(on_device, mesh.shape["dp"], mesh.shape["tensor"]),
        mesh=mesh,
        in_specs=in_specs,
        out_specs=out_specs,
        check_vma=False,
    )
```

```python
import functools

import jax
import jax.numpy as jnp
import numpy as np
from jax import lax
from jax.experimental import pallas as pl
from jax.experimental.pallas import tpu as pltpu
from jax.sharding import PartitionSpec as P

HEAD_DIM = 64
TOP = 2
REACH = 64
LANES = 128

eps_norm = 1e-06
gelu_scale = float(np.sqrt(2.0 / np.pi))
microseconds = {"front": 5, "route": 1.9, "expert": 4.4, "expert_back": 5.4, "expert_grads": 4.0, "combine": 1.9, "attend_back": 2.5, "partial": 1.2, "final": 3.9, "tokens_back": 1.5, "small": 1.4}
f32 = jnp.float32
bf16 = jnp.bfloat16


def bucket_of_distance(length, buckets, max_reach):
    exact_span = buckets // 2
    distance = np.arange(length)
    log_ratio = np.log(np.maximum(distance, exact_span) / exact_span) / np.log(
        max_reach / exact_span
    )
    coarse = exact_span + np.floor(log_ratio * (buckets - exact_span)).astype(np.int64)
    return np.where(distance < exact_span, distance, np.minimum(coarse, buckets - 1))


def nn(left, right, precision=None):
    return lax.dot_general(
        left, right, (((1,), (0,)), ((), ())), precision=precision, preferred_element_type=f32
    )


def nt(left, right):
    return lax.dot_general(left, right, (((1,), (1,)), ((), ())), preferred_element_type=f32)


def tn(left, right):
    return lax.dot_general(left, right, (((0,), (0,)), ((), ())), preferred_element_type=f32)


def iota(shape, axis):
    return lax.broadcasted_iota(jnp.int32, shape, axis)


def call(body, name, ids, outs, *args, scratch=(), limit=24, far=()):
    shapes = [jax.ShapeDtypeStruct(shape, dtype) for shape, dtype in outs]
    return pl.pallas_call(
        body,
        out_shape=shapes,
        in_specs=[pl.BlockSpec(memory_space=pltpu.SMEM)]
        + [
            pl.BlockSpec(memory_space=pltpu.HBM if i in far else pltpu.VMEM)
            for i in range(len(args))
        ],
        out_specs=[pl.BlockSpec(memory_space=pltpu.VMEM)] * len(outs),
        scratch_shapes=list(scratch),
        compiler_params=pltpu.CompilerParams(vmem_limit_bytes=limit << 20),
        cost_estimate=pl.CostEstimate(
            flops=0, transcendentals=0, bytes_accessed=int(microseconds.get(name, 0.8) * 3.6e6)
        ),
        name=name,
    )(
        ids,
        *[
            pltpu.with_memory_space_constraint(a, pltpu.HBM) if i in far else a
            for i, a in enumerate(args)
        ],
    )


def halves(value, t):
    width = value.shape[1] // 2
    low, high = value[:, :width], value[:, width:]
    even = t == 0
    return jnp.where(even, low, high), jnp.where(even, high, low)


def row_halves(value, t):
    width = value.shape[0] // 2
    low, high = value[:width], value[width:]
    even = t == 0
    return jnp.where(even, low, high), jnp.where(even, high, low)


def columns_of(row):
    length = row.shape[1]
    return jnp.broadcast_to(row.astype(f32), (length, length)).T


def sums_by_distance(square):
    length = square.shape[0]
    rows = length // 2
    while rows >= 1:
        square = square[:rows] + pltpu.roll(square[rows:], length - rows, 1)
        rows //= 2
    return square


def fetch(sources, targets, sems):
    copies = [
        pltpu.make_async_copy(source, target, sems.at[i])
        for i, (source, target) in enumerate(zip(sources, targets))
    ]
    for copy in copies:
        copy.start()
    return copies


def route_body(order, stride, ids, routes_far, cot_far, slots, *refs):
    experts = len(order)
    chunks, (routes, cot, sems) = refs[:experts], refs[experts:]
    copies = fetch((routes_far, cot_far), (routes, cot), sems)
    copies[0].wait()
    e, t = ids[0], ids[2]
    length = routes.shape[1]
    expert_row = iota((experts, length), 0)
    first = (expert_row == routes[0:1, :]).astype(f32)
    second = (expert_row == routes[1:2, :]).astype(f32)
    earlier = (iota((length, length), 0) < iota((length, length), 1)).astype(bf16)
    before = nn((first + second).astype(bf16), earlier)
    rank0 = jnp.sum(before * first, axis=0, keepdims=True).astype(jnp.int32)
    rank1 = jnp.sum(before * second, axis=0, keepdims=True).astype(jnp.int32)
    slot0 = (routes[0:1, :] ^ e) * stride + rank0
    slot1 = (routes[1:2, :] ^ e) * stride + rank1
    slots[0:1, :] = slot0
    slots[1:2, :] = slot1
    copies[1].wait()
    mine, _ = halves(cot[...], t)
    for s in range(experts):
        place = iota((stride, length), 0) + order[s] * stride
        pick = ((place == slot0) | (place == slot1)).astype(bf16)
        chunks[s][...] = nn(pick, mine).astype(bf16)


def front_body(ids, *refs):
    sources = refs[:9]
    early, part, q_out, k_out, v_out, probs = refs[9:15]
    targets, sems = refs[15:-1], refs[-1]
    tokens, gain, wq, wk, wv, rel, hot, seq, wo = targets
    copies = fetch(sources, targets, sems)
    t = ids[2]
    length = tokens.shape[0]
    mixed_out = early.at[pl.ds(length, length), :]
    copies[0].wait()
    copies[1].wait()
    wide = tokens[...].astype(f32)
    inv = lax.rsqrt(jnp.mean(wide * wide, axis=-1, keepdims=True) + eps_norm)
    value = (wide * inv * gain[...][None, :]).astype(bf16)
    early[pl.ds(0, length), :] = halves(value, t)[0]
    rows = length
    copies[2].wait()
    queries = nn(value, wq[...]).astype(bf16)
    copies[3].wait()
    keys = nn(value, wk[...]).astype(bf16)
    copies[4].wait()
    values = nn(value, wv[...]).astype(bf16)
    q_out[...] = queries
    k_out[...] = keys
    v_out[...] = values
    for copy in copies[5:8]:
        copy.wait()
    seq_cols = jnp.broadcast_to(seq[...].astype(f32), (rows, rows))
    allowed = (seq_cols == seq_cols.T) & (iota((rows, rows), 0) >= iota((rows, rows), 1))
    table = nn(rel[...], hot[...], lax.Precision.HIGHEST)
    lane = iota((rows, LANES), 1)
    pairs = [slice(i, i + LANES) for i in range(0, queries.shape[1], LANES)]
    heads = [(span, lane < HEAD_DIM if side == 0 else lane >= HEAD_DIM) for span in pairs for side in (0, 1)]
    raw = [
        nt(jnp.where(mine, queries[:, span], jnp.zeros((), bf16)), keys[:, span])
        for span, mine in heads
    ]
    biases = [
        pltpu.roll(
            jnp.broadcast_to(table[i : i + 1, :], (rows, rows)), 0, 1, stride=1, stride_axis=0
        )
        for i in range(len(heads))
    ]
    scores = [jnp.where(allowed, r * HEAD_DIM ** (-0.5) + b, -1e30) for r, b in zip(raw, biases)]
    tops = [jnp.max(x, axis=-1, keepdims=True) for x in scores]
    raised = [jnp.exp(x - top) for x, top in zip(scores, tops)]
    weights = [x / jnp.sum(x, axis=-1, keepdims=True) for x in raised]
    mixed = [nn(x.astype(bf16), values[:, span]) for x, (span, _) in zip(weights, heads)]
    for i, x in enumerate(weights):
        probs[i] = x
    for i, span in enumerate(pairs):
        mixed_out[:, span] = jnp.where(lane < HEAD_DIM, mixed[2 * i], mixed[2 * i + 1]).astype(bf16)
    copies[8].wait()
    part[...] = nn(mixed_out[...], wo[...])


def router_of(normed, weights_row):
    logits = nt(normed, weights_row)
    raised = jnp.exp(logits - jnp.max(logits, axis=-1, keepdims=True))
    return raised / jnp.sum(raised, axis=-1, keepdims=True)


def middle_body(order, stride, ids, own, other, tokens, gain, router, slots, residual, normed, probs, *chunks):
    t = ids[2]
    wide = tokens[...].astype(f32) + (own[...] + other[...])
    residual[...] = wide
    inv = lax.rsqrt(jnp.mean(wide * wide, axis=-1, keepdims=True) + eps_norm)
    value = (wide * inv * gain[...][None, :]).astype(bf16)
    normed[...] = value
    mine, _ = halves(value, t)
    length = slots.shape[1]
    for s in range(len(order)):
        place = iota((stride, length), 0) + order[s] * stride
        pick = ((place == slots[0:1, :]) | (place == slots[1:2, :])).astype(bf16)
        chunks[s][...] = nn(pick, mine).astype(bf16)
    probs[...] = router_of(value, router[...])


def join_body(ids, *refs):
    out = refs[-1]
    start = 0
    for ref in refs[:-1]:
        out[pl.ds(start, ref.shape[0]), :] = ref[...]
        start += ref.shape[0]


def in_order(own, other, even):
    return jnp.concatenate([jnp.where(even, own, other), jnp.where(even, other, own)], axis=1)


def expert_body(rows, ids, *refs):
    own, other = refs[:4], refs[4:8]
    w_in, w_out, act, slope, part_mine, part_other = refs[8:]
    t = ids[2]
    for p in range(4):
        span = pl.ds(p * rows, rows)
        pre = nn(in_order(own[p][...], other[p][...], t == 0), w_in[0])
        square = pre * pre
        bent = jnp.tanh(gelu_scale * (pre + 0.044715 * pre * square))
        half = 0.5 * (1.0 + bent)
        value = (pre * half).astype(bf16)
        act[span, :] = value
        slope[span, :] = half + 0.5 * pre * (1.0 - bent * bent) * (
            gelu_scale * (1.0 + 3 * 0.044715 * square)
        )
        mine, rest = halves(nn(value, w_out[0]).astype(bf16), t)
        part_mine[span, :] = mine
        part_other[span, :] = rest


def expert_back_body(rows, experts, ids, *refs):
    own, other, cot_own, cot_other = refs[:4], refs[4:8], refs[8:12], refs[12:16]
    w_in, w_out, router, slope, grad_pre, grads, back_mine, back_other = refs[16:]
    e, t = ids[0], ids[2]
    gates = []
    for p in range(4):
        logits = nt(in_order(own[p][...], other[p][...], t == 0), router[...])
        raised = jnp.exp(logits - jnp.max(logits, axis=-1, keepdims=True))
        chosen = jnp.where(iota(raised.shape, 1) == e, raised, 0.0)
        gates.append(
            jnp.sum(chosen, axis=-1, keepdims=True) / jnp.sum(raised, axis=-1, keepdims=True)
        )
    for p in range(4):
        span = pl.ds(p * rows, rows)
        cot_rows = pl.ds(0, rows)
        cot = in_order(cot_own[p][cot_rows, :], cot_other[p][cot_rows, :], t == 0)
        grad = (gates[p] * cot.astype(f32)).astype(bf16)
        grads[span, :] = grad
        value = (nt(grad, w_out[0]) * slope[span, :]).astype(bf16)
        grad_pre[span, :] = value
        mine, rest = halves(nt(value, w_in[0]).astype(bf16), t)
        back_mine[span, :] = mine
        back_other[span, :] = rest


def expert_grads_body(rows, ids, *refs):
    own, other = refs[:4], refs[4:8]
    act, grad_pre, grads, out_in, out_out = refs[8:]
    even = ids[2] == 0
    out_out[0] = tn(act[...], grads[...])
    sent = jnp.concatenate([in_order(own[p][...], other[p][...], even) for p in range(4)], axis=0)
    out_in[0] = tn(sent, grad_pre[...])


def pair_sum_body(ids, mine, received, keep, send):
    rows = mine.shape[0] // 4

    def block(p):
        q = (0, 2, 1, 3)[p]
        left = mine[pl.ds(p * rows, rows), :].astype(f32)
        return (left + received[pl.ds(q * rows, rows), :].astype(f32)).astype(bf16)

    keep[pl.ds(0, rows), :] = block(0)
    keep[pl.ds(rows, rows), :] = block(2)
    send[pl.ds(0, rows), :] = block(1)
    send[pl.ds(rows, rows), :] = block(3)


def plane_sum_body(ids, keep, received, kept, send):
    rows = keep.shape[0] // 2
    total = keep[...].astype(f32) + received[...].astype(f32)
    kept[...] = total[:rows]
    send[...] = total[rows:].astype(bf16)


def last_sum_body(experts, stride, ids, kept, received, kept_back, received_back, *chunks):
    first = (kept[...] + received[...].astype(f32)).astype(bf16)
    second = (kept_back[...] + received_back[...].astype(f32)).astype(bf16)
    for s in range(experts):
        chunks[s][pl.ds(0, stride), :] = first[s * stride : (s + 1) * stride]
        chunks[s][pl.ds(stride, stride), :] = second[s * stride : (s + 1) * stride]


def combine_body(order, stride, ids, *refs):
    experts = len(order)
    chunks = refs[:experts]
    slots, routes, probs, cot, residual, packed = refs[experts:]
    t = ids[2]
    length = slots.shape[1]
    probs_all = probs[...]
    choice = iota(probs_all.shape, 1)
    cot_mine = halves(cot[...], t)[0].astype(f32)
    mixture = None
    back = None
    lanes = iota((length, LANES), 1)
    dots = jnp.zeros((length, LANES), f32)
    for k in range(TOP):
        slot = columns_of(slots[k : k + 1, :])
        route = columns_of(routes[k : k + 1, :])[:, : probs_all.shape[1]]
        gate = jnp.sum(
            jnp.where(choice.astype(f32) == route, probs_all, 0.0), axis=-1, keepdims=True
        )
        chosen = None
        for s in range(experts):
            place = (iota((length, stride), 1) + order[s] * stride).astype(f32)
            pick = (place == slot[:, :1]).astype(bf16)
            value = nn(pick, chunks[s][pl.ds(0, stride), :])
            grad = nn(pick, chunks[s][pl.ds(stride, stride), :])
            chosen = value if chosen is None else chosen + value
            back = grad if back is None else back + grad
        mixture = gate * chosen if mixture is None else mixture + gate * chosen
        dots = jnp.where(lanes == k, jnp.sum(cot_mine * chosen, axis=-1, keepdims=True), dots)
    width = back.shape[1]
    packed[:, :width] = back
    packed[:, width : 2 * width] = halves(residual[...], t)[0] + mixture
    packed[:, 2 * width :] = dots


def norm_back_body(
    experts, ids, own, other, normed, probs, residual, routes, cot, gain, router, output, grad_out, att, small
):
    even = ids[2] == 0
    width = residual.shape[1] // 2
    first, last = slice(0, width), slice(width, 2 * width)
    low = jnp.where(even, own[:, first], other[:, first])
    high = jnp.where(even, other[:, first], own[:, first])
    back = jnp.concatenate([low, high], axis=1)
    output[:, first] = jnp.where(even, own[:, last], other[:, last]).astype(bf16)
    output[:, last] = jnp.where(even, other[:, last], own[:, last]).astype(bf16)
    dots = own[:, 2 * width :] + other[:, 2 * width :]
    probs_all = probs[...]
    choice = iota(probs_all.shape, 1).astype(f32)
    grad_probs = jnp.zeros_like(probs_all)
    for k in range(TOP):
        route = columns_of(routes[k : k + 1, :])[:, : probs_all.shape[1]]
        grad_probs = grad_probs + jnp.where(choice == route, dots[:, k : k + 1], 0.0)
    inner = jnp.sum(probs_all * grad_probs, axis=-1, keepdims=True)
    grad_logits = (probs_all * (grad_probs - inner)).astype(bf16)
    grad_normed = back + nn(grad_logits, router[...])
    wide = residual[...]
    inv = lax.rsqrt(jnp.mean(wide * wide, axis=-1, keepdims=True) + eps_norm)
    scaled = grad_normed * gain[...][None, :]
    grad = (
        cot[...].astype(f32)
        + inv * scaled
        - wide * (inv * inv * inv) * jnp.mean(scaled * wide, axis=-1, keepdims=True)
    )
    grad_out[...] = grad
    att[...] = grad.astype(bf16)
    small[0:1, :] = jnp.sum(grad_normed * wide * inv, axis=0, keepdims=True)
    small[pl.ds(1, experts), :] = tn(grad_logits, normed[...])


def attend_back_body(
    ids, att, wo, q_in, k_in, v_in, mixed_in, probs, wq, wk, wv, r0, r1, r2, r3, normed_part, bias, stack
):
    q_id, t = ids[1], ids[2]
    grad = att[...]
    rows = grad.shape[0]
    lane = iota((rows, LANES), 1)
    scale = HEAD_DIM ** (-0.5)
    pairs = [slice(i, i + LANES) for i in range(0, q_in.shape[1], LANES)]
    heads = [(i, lane < HEAD_DIM if side == 0 else lane >= HEAD_DIM) for i in range(len(pairs)) for side in (0, 1)]
    grad_mixed = [nt(grad, wo[span, :]).astype(bf16) for span in pairs]
    queries, keys, values = ([ref[:, span] for span in pairs] for ref in (q_in, k_in, v_in))
    mixed = [mixed_in[pl.ds(rows, rows), span].astype(f32) for span in pairs]
    weights = [probs[i] for i in range(len(heads))]
    parts = [jnp.where(mine, grad_mixed[i], jnp.zeros((), bf16)) for i, mine in heads]
    inner = [nt(part, values[i]) for part, (i, _) in zip(parts, heads)]
    deltas = [
        jnp.sum(part.astype(f32) * mixed[i], axis=-1, keepdims=True)
        for part, (i, _) in zip(parts, heads)
    ]
    scores = [w * (x - delta) for w, x, delta in zip(weights, inner, deltas)]
    half = [x.astype(bf16) for x in scores]
    dv = [tn(w.astype(bf16), grad_mixed[i]) for w, (i, _) in zip(weights, heads)]
    dq = [nn(x, keys[i]) for x, (i, _) in zip(half, heads)]
    dk = [tn(x, queries[i]) for x, (i, _) in zip(half, heads)]
    sums = [sums_by_distance(x) for x in scores]
    first = lane < HEAD_DIM
    for i, span in enumerate(pairs):
        stack[0, :, span] = (jnp.where(first, dq[2 * i], dq[2 * i + 1]) * scale).astype(bf16)
        stack[1, :, span] = (jnp.where(first, dk[2 * i], dk[2 * i + 1]) * scale).astype(bf16)
        stack[2, :, span] = jnp.where(first, dv[2 * i], dv[2 * i + 1]).astype(bf16)
    for i, row in enumerate(sums):
        bias[0:1, i * rows : (i + 1) * rows] = row
    stack[3] = halves(grad, t)[0]
    r0[...] = stack[q_id]
    r1[...] = stack[q_id ^ (1 + t)]
    r2[...] = stack[q_id ^ (2 - t)]
    r3[...] = stack[q_id ^ 3]
    total = nt(stack[0], wq[...]) + nt(stack[1], wk[...]) + nt(stack[2], wv[...])
    normed_part[...] = total.astype(bf16)


def tokens_back_body(experts, ids, own, other, tokens, gain, grad_res, small_ffn, bias, out, small):
    wide = tokens[...].astype(f32)
    inv = lax.rsqrt(jnp.mean(wide * wide, axis=-1, keepdims=True) + eps_norm)
    grad_normed = own[...].astype(f32) + other[...].astype(f32)
    scaled = grad_normed * gain[...][None, :]
    out[...] = (
        grad_res[...]
        + inv * scaled
        - wide * (inv * inv * inv) * jnp.mean(scaled * wide, axis=-1, keepdims=True)
    )
    small[...] = jnp.zeros_like(small)
    small[0:1, :] = jnp.sum(grad_normed * wide * inv, axis=0, keepdims=True)
    small[1:2, :] = bias[...]
    small[pl.ds(2, 1 + experts), :] = small_ffn[...]


def encode(value):
    width = value.shape[1] // 2
    tall = jnp.concatenate([value[:, :width], value[:, width:]], axis=0)
    lead = tall.astype(bf16)
    return lead, (tall - lead.astype(f32)).astype(bf16)


def decode(ref, start, rows):
    lead = ref[pl.ds(start, 2 * rows), :].astype(f32)
    return lead + ref[pl.ds(start + 2 * rows, 2 * rows), :].astype(f32)


def widen(tall):
    rows = tall.shape[0] // 2
    return jnp.concatenate([tall[:rows], tall[rows:]], axis=1)


def partial_body(order, ids, *refs):
    early_own, early_other = refs[:4], refs[4:8]
    right, right_pair, small = refs[8:12], refs[12:16], refs[16]
    blocks, total = refs[17:-1], refs[-1]
    e, q, t = ids[0], ids[1], ids[2]
    even = t == 0
    is_last = q == 3
    tokens = right[0].shape[0]
    rows = early_own[0].shape[0]
    width = early_own[0].shape[1]
    low, high, rights = [], [], []
    normed, mixed = pl.ds(rows - 2 * tokens, tokens), pl.ds(rows - tokens, tokens)
    for p in range(4):
        mine = jnp.where(is_last, right[p][...], early_own[p][normed, :])
        other = jnp.where(is_last, right_pair[p][...], early_other[p][normed, :])
        low.append(jnp.where(even, mine, other))
        high.append(jnp.where(even, other, mine))
        rights.append(jnp.where(is_last, early_own[p][mixed, :], right[p][...]))
    rights = jnp.concatenate(rights, axis=0)
    total[:width, :] = tn(jnp.concatenate(low, axis=0), rights)
    total[width:, :] = tn(jnp.concatenate(high, axis=0), rights)
    groups = len(order)
    depth = total.shape[0] // groups
    lead, rest = encode(small[...])
    for s in range(groups):
        start = pl.multiple_of((e ^ order[s]) * depth, 8)
        blocks[s][pl.ds(0, depth), :] = total[pl.ds(start, depth), :].astype(bf16)
        blocks[s][pl.ds(depth, lead.shape[0]), :] = lead
        blocks[s][pl.ds(depth + lead.shape[0], lead.shape[0]), :] = rest


def reduce_body(order, rows, ids, *refs):
    groups = len(order)
    arrived, outs = refs[:groups], refs[groups:]
    depth = outs[0].shape[0]
    total = arrived[0][pl.ds(0, depth), :].astype(f32)
    for ref in arrived[1:]:
        total = total + ref[pl.ds(0, depth), :].astype(f32)
    outs[0][...] = total.astype(bf16)
    code, stack = outs[1:]
    for s in range(groups):
        stack[order[s]] = decode(arrived[s], depth, rows)
    small = stack[ids[0]]
    for k in range(1, groups):
        small = small + stack[ids[0] ^ k]
    lead = small.astype(bf16)
    code[pl.ds(0, 2 * rows), :] = lead
    code[pl.ds(2 * rows, 2 * rows), :] = (small - lead.astype(f32)).astype(bf16)


def final_body(order, experts, rows, ids, *refs):
    groups = len(order)
    pieces, hot, outs = refs[:8], refs[8], refs[9:13]
    gain_attn, bias, gain_ffn, router = refs[13:17]
    square, small = refs[17:]
    e, q, t = ids[0], ids[1], ids[2]
    depth = square.shape[0] // groups
    per = groups - 1

    def place_of(chip):
        away = q ^ chip
        return jnp.where((t == 1) & ((away == 1) | (away == 2)), 3 - away, away)

    for p in range(4):
        small[p] = decode(pieces[p], per * depth, rows)
    for m in range(4):
        out = outs[m] if m < 3 else square
        place = place_of(m)
        for p in range(4):

            @pl.when(place == p)
            def _(p=p, out=out):
                for s in range(groups):
                    start = pl.multiple_of((order[s] ^ e) * depth, 8)
                    piece = pieces[s // per * 4 + p]
                    out[pl.ds(start, depth), :] = piece[pl.ds(s % per * depth, depth), :].astype(f32)

    outs[3][...] = square[...].T
    total = widen(small[place_of(0)] + small[place_of(1)] + small[place_of(2)] + small[place_of(3)])
    gain_attn[...] = total[0]
    gain_ffn[...] = total[2]
    router[...] = total[3 : 3 + experts]
    length = hot.shape[1]
    for head in range(bias.shape[0]):
        line = jnp.broadcast_to(total[1:2, head * length : (head + 1) * length], (8, length))
        value = lax.dot_general(
            line,
            hot[...],
            (((1,), (1,)), ((), ())),
            precision=lax.Precision.HIGHEST,
            preferred_element_type=f32,
        )
        bias[head : head + 1, :] = value[0:1]


def on_device(
    n_dp,
    n_tensor,
    tokens,
    seq_ids,
    routes,
    gain_attn,
    w_query,
    w_key,
    w_value,
    w_attn_out,
    rel_bias,
    gain_ffn,
    w_router,
    expert_in,
    expert_out,
    cotangent,
):
    groups = n_dp // 4
    length, width = tokens.shape
    half = width // 2
    experts = w_router.shape[1]
    bucket_count = rel_bias.shape[1]
    heads = rel_bias.shape[0]
    local = w_query.shape[1]
    capacity = 4 * ((5 * TOP * length + 16 * experts - 1) // (16 * experts))
    stride = -(-capacity // 16) * 16
    slot_count = experts * stride
    dp_id = lax.axis_index("dp")
    t_id = lax.axis_index("tensor")
    ids = jnp.stack([dp_id // 4, dp_id % 4, t_id]).astype(jnp.int32)

    def send(array, target, only=None):
        pairs = []
        for dp in range(n_dp):
            for t in range(n_tensor):
                e_to, q_to, t_to = target(dp // 4, dp % 4, t)
                if only is None or q_to == only:
                    pairs.append((dp * n_tensor + t, (e_to * 4 + q_to) * n_tensor + t_to))
        return lax.ppermute(array, ("dp", "tensor"), pairs)

    def to_pair(e, q, t):
        return e, q, 1 - t

    def to_first(e, q, t):
        return e, q ^ (1 + t), t

    def to_second(e, q, t):
        return e, q ^ (2 - t), t

    def to_far(e, q, t):
        return e, q ^ 3, t

    def to_group(step):
        return lambda e, q, t: (e ^ step, q, t)

    order = (0, *range(groups // 2, groups), *range(1, groups // 2))
    last_order = (0, *range(groups // 2, groups - 1), *range(1, groups // 2), groups - 1)

    def exchange(chunks, order=order):
        return [chunks[0]] + [
            send(chunk, to_group(step)) for chunk, step in zip(chunks[1:], order[1:])
        ]

    def join(arrays):
        rows = sum(a.shape[0] for a in arrays)
        return call(join_body, "join", ids, [((rows, arrays[0].shape[1]), arrays[0].dtype)], *arrays)[0]

    def spread_first(block):
        return block, send(block, to_first), send(block, to_second)

    def spread_rest(block, first, second):
        own = [block, first, second, send(first, to_second)]
        other = [send(piece, to_pair) for piece in own]
        return own, [other[0], other[2], other[1], other[3]]

    routes_t = routes.T
    gain_one, gain_two = gain_attn, gain_ffn
    router_t = w_router.T
    distance_bucket = bucket_of_distance(length, bucket_count, REACH)
    hot = (
        distance_bucket[(-np.arange(length)) % length][None, :] == np.arange(bucket_count)[:, None]
    ).astype(np.float32)
    hot = jnp.asarray(hot)

    chunk = ((stride, half), bf16)
    local_out = ((length, local), bf16)
    slots, *cot_chunks = call(
        functools.partial(route_body, order, stride),
        "route",
        ids,
        [((TOP, length), jnp.int32)] + [chunk] * experts,
        routes_t,
        cotangent,
        scratch=[
            pltpu.VMEM((TOP, length), jnp.int32),
            pltpu.VMEM((length, width), bf16),
            pltpu.SemaphoreType.DMA((2,)),
        ],
        far=(0, 1),
    )
    cot_arrived = exchange(cot_chunks)
    early, att_part, queries, keys, values, probs = call(
        front_body,
        "front",
        ids,
        [((2 * length, half), bf16), ((length, width), f32)]
        + [local_out] * 3
        + [((heads, length, length), f32)],
        tokens,
        gain_one,
        w_query,
        w_key,
        w_value,
        rel_bias,
        hot,
        seq_ids.reshape(1, length),
        w_attn_out,
        scratch=[pltpu.VMEM((length, width), bf16), pltpu.VMEM((width,), f32)]
        + [pltpu.VMEM((width, local), bf16)] * 3
        + [
            pltpu.VMEM(rel_bias.shape, f32),
            pltpu.VMEM(hot.shape, f32),
            pltpu.VMEM((1, length), jnp.int32),
            pltpu.VMEM((local, width), bf16),
            pltpu.SemaphoreType.DMA((9,)),
        ],
        far=range(9),
    )
    att_part, *cot_arrived = lax.optimization_barrier((att_part, *cot_arrived))
    cot_near = spread_first(join(cot_arrived + [early]))
    att_other = send(att_part, to_pair)
    residual, normed_two, router_probs, *row_chunks = call(
        functools.partial(middle_body, order, stride),
        "middle",
        ids,
        [((length, width), f32), ((length, width), bf16), ((length, experts), f32)]
        + [chunk] * experts,
        att_part,
        att_other,
        tokens,
        gain_two,
        router_t,
        slots,
    )
    *row_arrived, near, next_near = lax.optimization_barrier((*exchange(row_chunks), *cot_near[1:]))
    row_own, row_other = spread_rest(*spread_first(join(row_arrived)))
    cot_own, cot_other = spread_rest(cot_near[0], near, next_near)

    all_rows = 4 * slot_count
    rows_half = ((all_rows, half), bf16)
    units = expert_in.shape[2]
    act, slope, part_mine, part_other = call(
        functools.partial(expert_body, slot_count),
        "expert",
        ids,
        [((all_rows, units), bf16), ((all_rows, units), f32), rows_half, rows_half],
        *row_own,
        *row_other,
        expert_in,
        expert_out,
        limit=40,
    )
    two = ((2 * slot_count, half), bf16)
    one = ((slot_count, half), bf16)
    one_wide = ((slot_count, half), f32)

    keep, go = call(pair_sum_body, "pair_sum", ids, [two, two], part_mine, send(part_other, to_pair))
    part_kept, go = call(
        plane_sum_body, "plane_sum", ids, [one_wide, one], keep, send(go, to_first)
    )
    part_last = send(go, to_second)
    grad_pre, expert_cot, back_mine, back_other = call(
        functools.partial(expert_back_body, slot_count, experts),
        "expert_back",
        ids,
        [((all_rows, units), bf16), ((all_rows, width), bf16), rows_half, rows_half],
        *row_own,
        *row_other,
        *cot_own,
        *cot_other,
        expert_in,
        expert_out,
        router_t,
        slope,
        limit=40,
    )
    keep, go = call(pair_sum_body, "pair_sum", ids, [two, two], back_mine, send(back_other, to_pair))
    back_kept, go = call(
        plane_sum_body, "plane_sum", ids, [one_wide, one], keep, send(go, to_first)
    )
    back_last = send(go, to_second)
    grad_in, grad_out = call(
        functools.partial(expert_grads_body, slot_count),
        "expert_grads",
        ids,
        [(expert_in.shape, f32), (expert_out.shape, f32)],
        *row_own,
        *row_other,
        act,
        grad_pre,
        expert_cot,
        limit=40,
    )
    part_last, back_last, grad_in, grad_out = lax.optimization_barrier(
        (part_last, back_last, grad_in, grad_out)
    )
    chunks = call(
        functools.partial(last_sum_body, experts, stride),
        "last_sum",
        ids,
        [((2 * stride, half), bf16)] * experts,
        part_kept,
        part_last,
        back_kept,
        back_last,
    )
    returned = exchange(chunks)
    packed = call(
        functools.partial(combine_body, order, stride),
        "combine",
        ids,
        [((length, width + LANES), f32)],
        *returned,
        slots,
        routes_t,
        router_probs,
        cotangent,
        residual,
    )[0]
    output, grad_residual, grad_att, small_ffn = call(
        functools.partial(norm_back_body, experts),
        "norm_back",
        ids,
        [
            ((length, width), bf16),
            ((length, width), f32),
            ((length, width), bf16),
            ((1 + experts, width), f32),
        ],
        packed,
        send(packed, to_pair),
        normed_two,
        router_probs,
        residual,
        routes_t,
        cotangent,
        gain_two,
        router_t,
    )
    right0, right1, right2, right3, normed_part, bias = call(
        attend_back_body,
        "attend_back",
        ids,
        [local_out] * 4 + [((length, width), bf16), ((1, heads * length), f32)],
        grad_att,
        w_attn_out,
        queries,
        keys,
        values,
        early,
        probs,
        w_query,
        w_key,
        w_value,
        scratch=[pltpu.VMEM((4, length, local), bf16)],
    )
    right_all = [right0, send(right1, to_first), send(right2, to_second), send(right3, to_far)]
    small_rows = -(-(3 + experts) // 8) * 8
    grad_tokens, small = call(
        functools.partial(tokens_back_body, experts),
        "tokens_back",
        ids,
        [((length, width), f32), ((small_rows, width), f32)],
        normed_part,
        send(normed_part, to_pair),
        tokens,
        gain_one,
        grad_residual,
        small_ffn,
        bias,
    )
    *right_all, small = lax.optimization_barrier((*right_all, small))
    right_pair = [send(right_all[p], to_pair) for p in (0, 2, 1, 3)]
    depth = width // groups
    blocks = call(
        functools.partial(partial_body, order),
        "partial",
        ids,
        [((depth + 4 * small_rows, local), bf16)] * groups,
        *cot_own,
        *cot_other,
        *right_all,
        *right_pair,
        small,
        scratch=[pltpu.VMEM((width, local), f32)],
    )
    reduced, code = call(
        functools.partial(reduce_body, order, small_rows),
        "reduce",
        ids,
        [((depth, local), bf16), ((4 * small_rows, local), bf16)],
        *exchange(blocks),
        scratch=[pltpu.VMEM((groups, 2 * small_rows, local), f32)],
    )
    spread = exchange([reduced] * groups, last_order)
    near, rest = spread[:-1], spread[-1:]
    matrix = join(near + [code])
    first, second = send(matrix, to_first), send(matrix, to_second)
    *rest, first, second = lax.optimization_barrier((*rest, first, second))
    far = send(first, to_second)
    matrix_two = rest[0]
    first_two, second_two = send(matrix_two, to_first), send(matrix_two, to_second)
    far_two = send(matrix_two, to_far)
    grads = call(
        functools.partial(final_body, last_order, experts, small_rows),
        "final",
        ids,
        [((width, local), f32)] * 3
        + [((local, width), f32), ((width,), f32), ((heads, bucket_count), f32)]
        + [((width,), f32), ((experts, width), f32)],
        matrix,
        first,
        second,
        far,
        matrix_two,
        first_two,
        second_two,
        far_two,
        hot,
        scratch=[
            pltpu.VMEM((width, local), f32),
            pltpu.VMEM((4, 2 * small_rows, local), f32),
        ],
        limit=40,
    )
    return (
        output,
        grad_tokens,
        grads[4],
        grads[0],
        grads[1],
        grads[2],
        grads[3],
        grads[5],
        grads[6],
        grads[7].T,
        grad_in,
        grad_out,
    )


def solution(mesh):
    in_specs = (
        P("dp", None),
        P("dp"),
        P("dp", None),
        P(),
        P(None, "tensor"),
        P(None, "tensor"),
        P(None, "tensor"),
        P("tensor", None),
        P("tensor", None),
        P(),
        P(),
        P("dp", None, "tensor"),
        P("dp", "tensor", None),
        P("dp", None),
    )
    out_specs = (
        P("dp", None),
        P("dp", None),
        P(),
        P(None, "tensor"),
        P(None, "tensor"),
        P(None, "tensor"),
        P("tensor", None),
        P("tensor", None),
        P(),
        P(),
        P("dp", None, "tensor"),
        P("dp", "tensor", None),
    )
    return jax.shard_map(
        functools.partial(on_device, mesh.shape["dp"], mesh.shape["tensor"]),
        mesh=mesh,
        in_specs=in_specs,
        out_specs=out_specs,
        check_vma=False,
    )
```

```python
import functools

import jax
import jax.numpy as jnp
import numpy as np
from jax import lax
from jax.experimental import pallas as pl
from jax.experimental.pallas import tpu as pltpu
from jax.sharding import PartitionSpec as P

HEAD_DIM = 64
TOP = 2
REACH = 64
LANES = 128

eps_norm = 1e-06
gelu_scale = float(np.sqrt(2.0 / np.pi))
microseconds = {"front": 5, "route": 1.9, "expert": 4.4, "expert_back": 5.4, "expert_grads": 4.0, "combine": 1.9, "attend_back": 2.5, "partial": 1.2, "final": 3.9, "tokens_back": 1.5, "small": 1.4}
f32 = jnp.float32
bf16 = jnp.bfloat16


def bucket_of_distance(length, buckets, max_reach):
    exact_span = buckets // 2
    distance = np.arange(length)
    log_ratio = np.log(np.maximum(distance, exact_span) / exact_span) / np.log(
        max_reach / exact_span
    )
    coarse = exact_span + np.floor(log_ratio * (buckets - exact_span)).astype(np.int64)
    return np.where(distance < exact_span, distance, np.minimum(coarse, buckets - 1))


def nn(left, right, precision=None):
    return lax.dot_general(
        left, right, (((1,), (0,)), ((), ())), precision=precision, preferred_element_type=f32
    )


def nt(left, right):
    return lax.dot_general(left, right, (((1,), (1,)), ((), ())), preferred_element_type=f32)


def tn(left, right):
    return lax.dot_general(left, right, (((0,), (0,)), ((), ())), preferred_element_type=f32)


def iota(shape, axis):
    return lax.broadcasted_iota(jnp.int32, shape, axis)


def call(body, name, ids, outs, *args, scratch=(), limit=24, far=()):
    shapes = [jax.ShapeDtypeStruct(shape, dtype) for shape, dtype in outs]
    return pl.pallas_call(
        body,
        out_shape=shapes,
        in_specs=[pl.BlockSpec(memory_space=pltpu.SMEM)]
        + [
            pl.BlockSpec(memory_space=pltpu.HBM if i in far else pltpu.VMEM)
            for i in range(len(args))
        ],
        out_specs=[pl.BlockSpec(memory_space=pltpu.VMEM)] * len(outs),
        scratch_shapes=list(scratch),
        compiler_params=pltpu.CompilerParams(vmem_limit_bytes=limit << 20),
        cost_estimate=pl.CostEstimate(
            flops=0, transcendentals=0, bytes_accessed=int(microseconds.get(name, 0.8) * 3.6e6)
        ),
        name=name,
    )(
        ids,
        *[
            pltpu.with_memory_space_constraint(a, pltpu.HBM) if i in far else a
            for i, a in enumerate(args)
        ],
    )


def halves(value, t):
    width = value.shape[1] // 2
    low, high = value[:, :width], value[:, width:]
    even = t == 0
    return jnp.where(even, low, high), jnp.where(even, high, low)


def row_halves(value, t):
    width = value.shape[0] // 2
    low, high = value[:width], value[width:]
    even = t == 0
    return jnp.where(even, low, high), jnp.where(even, high, low)


def columns_of(row):
    length = row.shape[1]
    return jnp.broadcast_to(row.astype(f32), (length, length)).T


def sums_by_distance(square):
    length = square.shape[0]
    rows = length // 2
    while rows >= 1:
        square = square[:rows] + pltpu.roll(square[rows:], length - rows, 1)
        rows //= 2
    return square


def fetch(sources, targets, sems):
    copies = [
        pltpu.make_async_copy(source, target, sems.at[i])
        for i, (source, target) in enumerate(zip(sources, targets))
    ]
    for copy in copies:
        copy.start()
    return copies


def route_body(order, stride, ids, routes_far, cot_far, slots, *refs):
    experts = len(order)
    chunks, (routes, cot, sems) = refs[:experts], refs[experts:]
    copies = fetch((routes_far, cot_far), (routes, cot), sems)
    copies[0].wait()
    e, t = ids[0], ids[2]
    length = routes.shape[1]
    expert_row = iota((experts, length), 0)
    first = (expert_row == routes[0:1, :]).astype(f32)
    second = (expert_row == routes[1:2, :]).astype(f32)
    earlier = (iota((length, length), 0) < iota((length, length), 1)).astype(bf16)
    before = nn((first + second).astype(bf16), earlier)
    rank0 = jnp.sum(before * first, axis=0, keepdims=True).astype(jnp.int32)
    rank1 = jnp.sum(before * second, axis=0, keepdims=True).astype(jnp.int32)
    slot0 = (routes[0:1, :] ^ e) * stride + rank0
    slot1 = (routes[1:2, :] ^ e) * stride + rank1
    slots[0:1, :] = slot0
    slots[1:2, :] = slot1
    copies[1].wait()
    mine, _ = halves(cot[...], t)
    for s in range(experts):
        place = iota((stride, length), 0) + order[s] * stride
        pick = ((place == slot0) | (place == slot1)).astype(bf16)
        chunks[s][...] = nn(pick, mine).astype(bf16)


def front_body(ids, *refs):
    sources = refs[:9]
    early, part, q_out, k_out, v_out, probs = refs[9:15]
    targets, sems = refs[15:-1], refs[-1]
    tokens, gain, wq, wk, wv, rel, hot, seq, wo = targets
    copies = fetch(sources, targets, sems)
    t = ids[2]
    length = tokens.shape[0]
    mixed_out = early.at[pl.ds(length, length), :]
    copies[0].wait()
    copies[1].wait()
    wide = tokens[...].astype(f32)
    inv = lax.rsqrt(jnp.mean(wide * wide, axis=-1, keepdims=True) + eps_norm)
    value = (wide * inv * gain[...][None, :]).astype(bf16)
    early[pl.ds(0, length), :] = halves(value, t)[0]
    rows = length
    copies[2].wait()
    queries = nn(value, wq[...]).astype(bf16)
    copies[3].wait()
    keys = nn(value, wk[...]).astype(bf16)
    copies[4].wait()
    values = nn(value, wv[...]).astype(bf16)
    q_out[...] = queries
    k_out[...] = keys
    v_out[...] = values
    for copy in copies[5:8]:
        copy.wait()
    seq_cols = jnp.broadcast_to(seq[...].astype(f32), (rows, rows))
    allowed = (seq_cols == seq_cols.T) & (iota((rows, rows), 0) >= iota((rows, rows), 1))
    table = nn(rel[...], hot[...], lax.Precision.HIGHEST)
    lane = iota((rows, LANES), 1)
    pairs = [slice(i, i + LANES) for i in range(0, queries.shape[1], LANES)]
    heads = [(span, lane < HEAD_DIM if side == 0 else lane >= HEAD_DIM) for span in pairs for side in (0, 1)]
    raw = [
        nt(jnp.where(mine, queries[:, span], jnp.zeros((), bf16)), keys[:, span])
        for span, mine in heads
    ]
    biases = [
        pltpu.roll(
            jnp.broadcast_to(table[i : i + 1, :], (rows, rows)), 0, 1, stride=1, stride_axis=0
        )
        for i in range(len(heads))
    ]
    scores = [jnp.where(allowed, r * HEAD_DIM ** (-0.5) + b, -1e30) for r, b in zip(raw, biases)]
    tops = [jnp.max(x, axis=-1, keepdims=True) for x in scores]
    raised = [jnp.exp(x - top) for x, top in zip(scores, tops)]
    weights = [x / jnp.sum(x, axis=-1, keepdims=True) for x in raised]
    mixed = [nn(x.astype(bf16), values[:, span]) for x, (span, _) in zip(weights, heads)]
    for i, x in enumerate(weights):
        probs[i] = x
    for i, span in enumerate(pairs):
        mixed_out[:, span] = jnp.where(lane < HEAD_DIM, mixed[2 * i], mixed[2 * i + 1]).astype(bf16)
    copies[8].wait()
    part[...] = nn(mixed_out[...], wo[...])


def router_of(normed, weights_row):
    logits = nt(normed, weights_row)
    raised = jnp.exp(logits - jnp.max(logits, axis=-1, keepdims=True))
    return raised / jnp.sum(raised, axis=-1, keepdims=True)


def middle_body(order, stride, ids, own, other, tokens, gain, router, slots, residual, normed, probs, *chunks):
    t = ids[2]
    wide = tokens[...].astype(f32) + (own[...] + other[...])
    residual[...] = wide
    inv = lax.rsqrt(jnp.mean(wide * wide, axis=-1, keepdims=True) + eps_norm)
    value = (wide * inv * gain[...][None, :]).astype(bf16)
    normed[...] = value
    mine, _ = halves(value, t)
    length = slots.shape[1]
    for s in range(len(order)):
        place = iota((stride, length), 0) + order[s] * stride
        pick = ((place == slots[0:1, :]) | (place == slots[1:2, :])).astype(bf16)
        chunks[s][...] = nn(pick, mine).astype(bf16)
    probs[...] = router_of(value, router[...])


def join_body(ids, *refs):
    out = refs[-1]
    start = 0
    for ref in refs[:-1]:
        out[pl.ds(start, ref.shape[0]), :] = ref[...]
        start += ref.shape[0]


def in_order(own, other, even):
    return jnp.concatenate([jnp.where(even, own, other), jnp.where(even, other, own)], axis=1)


def expert_body(rows, ids, *refs):
    own, other = refs[:4], refs[4:8]
    w_in, w_out, act, slope, part_mine, part_other = refs[8:]
    t = ids[2]
    for p in range(4):
        span = pl.ds(p * rows, rows)
        pre = nn(in_order(own[p][...], other[p][...], t == 0), w_in[0])
        square = pre * pre
        bent = jnp.tanh(gelu_scale * (pre + 0.044715 * pre * square))
        half = 0.5 * (1.0 + bent)
        value = (pre * half).astype(bf16)
        act[span, :] = value
        slope[span, :] = half + 0.5 * pre * (1.0 - bent * bent) * (
            gelu_scale * (1.0 + 3 * 0.044715 * square)
        )
        mine, rest = halves(nn(value, w_out[0]).astype(bf16), t)
        part_mine[span, :] = mine
        part_other[span, :] = rest


def expert_back_body(rows, experts, ids, *refs):
    own, other, cot_own, cot_other = refs[:4], refs[4:8], refs[8:12], refs[12:16]
    w_in, w_out, router, slope, grad_pre, grads, back_mine, back_other = refs[16:]
    e, t = ids[0], ids[2]
    gates = []
    for p in range(4):
        logits = nt(in_order(own[p][...], other[p][...], t == 0), router[...])
        raised = jnp.exp(logits - jnp.max(logits, axis=-1, keepdims=True))
        chosen = jnp.where(iota(raised.shape, 1) == e, raised, 0.0)
        gates.append(
            jnp.sum(chosen, axis=-1, keepdims=True) / jnp.sum(raised, axis=-1, keepdims=True)
        )
    for p in range(4):
        span = pl.ds(p * rows, rows)
        cot_rows = pl.ds(0, rows)
        cot = in_order(cot_own[p][cot_rows, :], cot_other[p][cot_rows, :], t == 0)
        grad = (gates[p] * cot.astype(f32)).astype(bf16)
        grads[span, :] = grad
        value = (nt(grad, w_out[0]) * slope[span, :]).astype(bf16)
        grad_pre[span, :] = value
        mine, rest = halves(nt(value, w_in[0]).astype(bf16), t)
        back_mine[span, :] = mine
        back_other[span, :] = rest


def expert_grads_body(rows, ids, *refs):
    own, other = refs[:4], refs[4:8]
    act, grad_pre, grads, out_in, out_out = refs[8:]
    even = ids[2] == 0
    out_out[0] = tn(act[...], grads[...])
    sent = jnp.concatenate([in_order(own[p][...], other[p][...], even) for p in range(4)], axis=0)
    out_in[0] = tn(sent, grad_pre[...])


def pair_sum_body(ids, mine, received, keep, send):
    rows = mine.shape[0] // 4

    def block(p):
        q = (0, 2, 1, 3)[p]
        left = mine[pl.ds(p * rows, rows), :].astype(f32)
        return (left + received[pl.ds(q * rows, rows), :].astype(f32)).astype(bf16)

    keep[pl.ds(0, rows), :] = block(0)
    keep[pl.ds(rows, rows), :] = block(2)
    send[pl.ds(0, rows), :] = block(1)
    send[pl.ds(rows, rows), :] = block(3)


def plane_sum_body(ids, keep, received, kept, send):
    rows = keep.shape[0] // 2
    total = keep[...].astype(f32) + received[...].astype(f32)
    kept[...] = total[:rows]
    send[...] = total[rows:].astype(bf16)


def last_sum_body(experts, stride, ids, kept, received, kept_back, received_back, *chunks):
    first = (kept[...] + received[...].astype(f32)).astype(bf16)
    second = (kept_back[...] + received_back[...].astype(f32)).astype(bf16)
    for s in range(experts):
        chunks[s][pl.ds(0, stride), :] = first[s * stride : (s + 1) * stride]
        chunks[s][pl.ds(stride, stride), :] = second[s * stride : (s + 1) * stride]


def combine_body(order, stride, ids, *refs):
    experts = len(order)
    chunks = refs[:experts]
    slots, routes, probs, cot, residual, packed = refs[experts:]
    t = ids[2]
    length = slots.shape[1]
    probs_all = probs[...]
    choice = iota(probs_all.shape, 1)
    cot_mine = halves(cot[...], t)[0].astype(f32)
    mixture = None
    back = None
    lanes = iota((length, LANES), 1)
    dots = jnp.zeros((length, LANES), f32)
    for k in range(TOP):
        slot = columns_of(slots[k : k + 1, :])
        route = columns_of(routes[k : k + 1, :])[:, : probs_all.shape[1]]
        gate = jnp.sum(
            jnp.where(choice.astype(f32) == route, probs_all, 0.0), axis=-1, keepdims=True
        )
        chosen = None
        for s in range(experts):
            place = (iota((length, stride), 1) + order[s] * stride).astype(f32)
            pick = (place == slot[:, :1]).astype(bf16)
            value = nn(pick, chunks[s][pl.ds(0, stride), :])
            grad = nn(pick, chunks[s][pl.ds(stride, stride), :])
            chosen = value if chosen is None else chosen + value
            back = grad if back is None else back + grad
        mixture = gate * chosen if mixture is None else mixture + gate * chosen
        dots = jnp.where(lanes == k, jnp.sum(cot_mine * chosen, axis=-1, keepdims=True), dots)
    width = back.shape[1]
    packed[:, :width] = back
    packed[:, width : 2 * width] = halves(residual[...], t)[0] + mixture
    packed[:, 2 * width :] = dots


def norm_back_body(
    experts, ids, own, other, normed, probs, residual, routes, cot, gain, router, output, grad_out, att, small
):
    even = ids[2] == 0
    width = residual.shape[1] // 2
    first, last = slice(0, width), slice(width, 2 * width)
    low = jnp.where(even, own[:, first], other[:, first])
    high = jnp.where(even, other[:, first], own[:, first])
    back = jnp.concatenate([low, high], axis=1)
    output[:, first] = jnp.where(even, own[:, last], other[:, last]).astype(bf16)
    output[:, last] = jnp.where(even, other[:, last], own[:, last]).astype(bf16)
    dots = own[:, 2 * width :] + other[:, 2 * width :]
    probs_all = probs[...]
    choice = iota(probs_all.shape, 1).astype(f32)
    grad_probs = jnp.zeros_like(probs_all)
    for k in range(TOP):
        route = columns_of(routes[k : k + 1, :])[:, : probs_all.shape[1]]
        grad_probs = grad_probs + jnp.where(choice == route, dots[:, k : k + 1], 0.0)
    inner = jnp.sum(probs_all * grad_probs, axis=-1, keepdims=True)
    grad_logits = (probs_all * (grad_probs - inner)).astype(bf16)
    grad_normed = back + nn(grad_logits, router[...])
    wide = residual[...]
    inv = lax.rsqrt(jnp.mean(wide * wide, axis=-1, keepdims=True) + eps_norm)
    scaled = grad_normed * gain[...][None, :]
    grad = (
        cot[...].astype(f32)
        + inv * scaled
        - wide * (inv * inv * inv) * jnp.mean(scaled * wide, axis=-1, keepdims=True)
    )
    grad_out[...] = grad
    att[...] = grad.astype(bf16)
    small[0:1, :] = jnp.sum(grad_normed * wide * inv, axis=0, keepdims=True)
    small[pl.ds(1, experts), :] = tn(grad_logits, normed[...])


def attend_back_body(
    ids, att, wo, q_in, k_in, v_in, mixed_in, probs, wq, wk, wv, r0, r1, r2, r3, normed_part, bias, stack
):
    q_id, t = ids[1], ids[2]
    grad = att[...]
    rows = grad.shape[0]
    lane = iota((rows, LANES), 1)
    scale = HEAD_DIM ** (-0.5)
    pairs = [slice(i, i + LANES) for i in range(0, q_in.shape[1], LANES)]
    heads = [(i, lane < HEAD_DIM if side == 0 else lane >= HEAD_DIM) for i in range(len(pairs)) for side in (0, 1)]
    grad_mixed = [nt(grad, wo[span, :]).astype(bf16) for span in pairs]
    queries, keys, values = ([ref[:, span] for span in pairs] for ref in (q_in, k_in, v_in))
    mixed = [mixed_in[pl.ds(rows, rows), span].astype(f32) for span in pairs]
    weights = [probs[i] for i in range(len(heads))]
    parts = [jnp.where(mine, grad_mixed[i], jnp.zeros((), bf16)) for i, mine in heads]
    inner = [nt(part, values[i]) for part, (i, _) in zip(parts, heads)]
    deltas = [
        jnp.sum(part.astype(f32) * mixed[i], axis=-1, keepdims=True)
        for part, (i, _) in zip(parts, heads)
    ]
    scores = [w * (x - delta) for w, x, delta in zip(weights, inner, deltas)]
    half = [x.astype(bf16) for x in scores]
    dv = [tn(w.astype(bf16), grad_mixed[i]) for w, (i, _) in zip(weights, heads)]
    dq = [nn(x, keys[i]) for x, (i, _) in zip(half, heads)]
    dk = [tn(x, queries[i]) for x, (i, _) in zip(half, heads)]
    sums = [sums_by_distance(x) for x in scores]
    first = lane < HEAD_DIM
    for i, span in enumerate(pairs):
        stack[0, :, span] = (jnp.where(first, dq[2 * i], dq[2 * i + 1]) * scale).astype(bf16)
        stack[1, :, span] = (jnp.where(first, dk[2 * i], dk[2 * i + 1]) * scale).astype(bf16)
        stack[2, :, span] = jnp.where(first, dv[2 * i], dv[2 * i + 1]).astype(bf16)
    for i, row in enumerate(sums):
        bias[0:1, i * rows : (i + 1) * rows] = row
    stack[3] = halves(grad, t)[0]
    r0[...] = stack[q_id]
    r1[...] = stack[q_id ^ (1 + t)]
    r2[...] = stack[q_id ^ (2 - t)]
    r3[...] = stack[q_id ^ 3]
    total = nt(stack[0], wq[...]) + nt(stack[1], wk[...]) + nt(stack[2], wv[...])
    normed_part[...] = total.astype(bf16)


def tokens_back_body(experts, ids, own, other, tokens, gain, grad_res, small_ffn, bias, out, small):
    wide = tokens[...].astype(f32)
    inv = lax.rsqrt(jnp.mean(wide * wide, axis=-1, keepdims=True) + eps_norm)
    grad_normed = own[...].astype(f32) + other[...].astype(f32)
    scaled = grad_normed * gain[...][None, :]
    out[...] = (
        grad_res[...]
        + inv * scaled
        - wide * (inv * inv * inv) * jnp.mean(scaled * wide, axis=-1, keepdims=True)
    )
    small[...] = jnp.zeros_like(small)
    small[0:1, :] = jnp.sum(grad_normed * wide * inv, axis=0, keepdims=True)
    small[1:2, :] = bias[...]
    small[pl.ds(2, 1 + experts), :] = small_ffn[...]


def encode(value):
    width = value.shape[1] // 2
    tall = jnp.concatenate([value[:, :width], value[:, width:]], axis=0)
    lead = tall.astype(bf16)
    return lead, (tall - lead.astype(f32)).astype(bf16)


def decode(ref, start, rows):
    lead = ref[pl.ds(start, 2 * rows), :].astype(f32)
    return lead + ref[pl.ds(start + 2 * rows, 2 * rows), :].astype(f32)


def widen(tall):
    rows = tall.shape[0] // 2
    return jnp.concatenate([tall[:rows], tall[rows:]], axis=1)


def partial_body(order, ids, *refs):
    early_own, early_other = refs[:4], refs[4:8]
    right, right_pair, small = refs[8:12], refs[12:16], refs[16]
    blocks, total = refs[17:-1], refs[-1]
    e, q, t = ids[0], ids[1], ids[2]
    even = t == 0
    is_last = q == 3
    tokens = right[0].shape[0]
    rows = early_own[0].shape[0]
    width = early_own[0].shape[1]
    low, high, rights = [], [], []
    normed, mixed = pl.ds(rows - 2 * tokens, tokens), pl.ds(rows - tokens, tokens)
    for p in range(4):
        mine = jnp.where(is_last, right[p][...], early_own[p][normed, :])
        other = jnp.where(is_last, right_pair[p][...], early_other[p][normed, :])
        low.append(jnp.where(even, mine, other))
        high.append(jnp.where(even, other, mine))
        rights.append(jnp.where(is_last, early_own[p][mixed, :], right[p][...]))
    rights = jnp.concatenate(rights, axis=0)
    total[:width, :] = tn(jnp.concatenate(low, axis=0), rights)
    total[width:, :] = tn(jnp.concatenate(high, axis=0), rights)
    groups = len(order)
    depth = total.shape[0] // groups
    lead, rest = encode(small[...])
    for s in range(groups):
        start = pl.multiple_of((e ^ order[s]) * depth, 8)
        blocks[s][pl.ds(0, depth), :] = total[pl.ds(start, depth), :].astype(bf16)
        blocks[s][pl.ds(depth, lead.shape[0]), :] = lead
        blocks[s][pl.ds(depth + lead.shape[0], lead.shape[0]), :] = rest


def reduce_body(order, rows, ids, *refs):
    groups = len(order)
    arrived, outs = refs[:groups], refs[groups:]
    depth = outs[0].shape[0]
    total = arrived[0][pl.ds(0, depth), :].astype(f32)
    for ref in arrived[1:]:
        total = total + ref[pl.ds(0, depth), :].astype(f32)
    outs[0][...] = total.astype(bf16)
    code, stack = outs[1:]
    for s in range(groups):
        stack[order[s]] = decode(arrived[s], depth, rows)
    small = stack[ids[0]]
    for k in range(1, groups):
        small = small + stack[ids[0] ^ k]
    lead = small.astype(bf16)
    code[pl.ds(0, depth), :] = outs[0][...]
    code[pl.ds(depth, 2 * rows), :] = lead
    code[pl.ds(depth + 2 * rows, 2 * rows), :] = (small - lead.astype(f32)).astype(bf16)


def final_body(order, experts, rows, ids, *refs):
    groups = len(order)
    pieces, hot, outs = refs[:12], refs[12], refs[13:17]
    gain_attn, bias, gain_ffn, router = refs[17:21]
    square, small = refs[21:]
    e, q, t = ids[0], ids[1], ids[2]
    depth = square.shape[0] // groups

    def place_of(chip):
        away = q ^ chip
        return jnp.where((t == 1) & ((away == 1) | (away == 2)), 3 - away, away)

    for p in range(4):
        small[p] = decode(pieces[p], depth, rows)
    for m in range(4):
        out = outs[m] if m < 3 else square
        place = place_of(m)
        for p in range(4):

            @pl.when(place == p)
            def _(p=p, out=out):
                for s in range(groups):
                    start = pl.multiple_of((order[s] ^ e) * depth, 8)
                    step, at = (0, 0) if s == 0 else (2, 0) if s == groups - 1 else (1, s - 1)
                    piece = pieces[step * 4 + p]
                    out[pl.ds(start, depth), :] = piece[pl.ds(at * depth, depth), :].astype(f32)

    outs[3][...] = square[...].T
    total = widen(small[place_of(0)] + small[place_of(1)] + small[place_of(2)] + small[place_of(3)])
    gain_attn[...] = total[0]
    gain_ffn[...] = total[2]
    router[...] = total[3 : 3 + experts]
    length = hot.shape[1]
    for head in range(bias.shape[0]):
        line = jnp.broadcast_to(total[1:2, head * length : (head + 1) * length], (8, length))
        value = lax.dot_general(
            line,
            hot[...],
            (((1,), (1,)), ((), ())),
            precision=lax.Precision.HIGHEST,
            preferred_element_type=f32,
        )
        bias[head : head + 1, :] = value[0:1]


def on_device(
    n_dp,
    n_tensor,
    tokens,
    seq_ids,
    routes,
    gain_attn,
    w_query,
    w_key,
    w_value,
    w_attn_out,
    rel_bias,
    gain_ffn,
    w_router,
    expert_in,
    expert_out,
    cotangent,
):
    groups = n_dp // 4
    length, width = tokens.shape
    half = width // 2
    experts = w_router.shape[1]
    bucket_count = rel_bias.shape[1]
    heads = rel_bias.shape[0]
    local = w_query.shape[1]
    capacity = 4 * ((5 * TOP * length + 16 * experts - 1) // (16 * experts))
    stride = -(-capacity // 16) * 16
    slot_count = experts * stride
    dp_id = lax.axis_index("dp")
    t_id = lax.axis_index("tensor")
    ids = jnp.stack([dp_id // 4, dp_id % 4, t_id]).astype(jnp.int32)

    def send(array, target, only=None):
        pairs = []
        for dp in range(n_dp):
            for t in range(n_tensor):
                e_to, q_to, t_to = target(dp // 4, dp % 4, t)
                if only is None or q_to == only:
                    pairs.append((dp * n_tensor + t, (e_to * 4 + q_to) * n_tensor + t_to))
        return lax.ppermute(array, ("dp", "tensor"), pairs)

    def to_pair(e, q, t):
        return e, q, 1 - t

    def to_first(e, q, t):
        return e, q ^ (1 + t), t

    def to_second(e, q, t):
        return e, q ^ (2 - t), t

    def to_far(e, q, t):
        return e, q ^ 3, t

    def to_group(step):
        return lambda e, q, t: (e ^ step, q, t)

    order = (0, *range(groups // 2, groups), *range(1, groups // 2))
    last_order = (0, *range(groups // 2, groups - 1), *range(1, groups // 2), groups - 1)

    def exchange(chunks, order=order):
        return [chunks[0]] + [
            send(chunk, to_group(step)) for chunk, step in zip(chunks[1:], order[1:])
        ]

    def join(arrays):
        rows = sum(a.shape[0] for a in arrays)
        return call(join_body, "join", ids, [((rows, arrays[0].shape[1]), arrays[0].dtype)], *arrays)[0]

    def spread_first(block):
        return block, send(block, to_first), send(block, to_second)

    def spread_rest(block, first, second):
        own = [block, first, second, send(first, to_second)]
        other = [send(piece, to_pair) for piece in own]
        return own, [other[0], other[2], other[1], other[3]]

    routes_t = routes.T
    gain_one, gain_two = gain_attn, gain_ffn
    router_t = w_router.T
    distance_bucket = bucket_of_distance(length, bucket_count, REACH)
    hot = (
        distance_bucket[(-np.arange(length)) % length][None, :] == np.arange(bucket_count)[:, None]
    ).astype(np.float32)
    hot = jnp.asarray(hot)

    chunk = ((stride, half), bf16)
    local_out = ((length, local), bf16)
    slots, *cot_chunks = call(
        functools.partial(route_body, order, stride),
        "route",
        ids,
        [((TOP, length), jnp.int32)] + [chunk] * experts,
        routes_t,
        cotangent,
        scratch=[
            pltpu.VMEM((TOP, length), jnp.int32),
            pltpu.VMEM((length, width), bf16),
            pltpu.SemaphoreType.DMA((2,)),
        ],
        far=(0, 1),
    )
    cot_arrived = exchange(cot_chunks)
    early, att_part, queries, keys, values, probs = call(
        front_body,
        "front",
        ids,
        [((2 * length, half), bf16), ((length, width), f32)]
        + [local_out] * 3
        + [((heads, length, length), f32)],
        tokens,
        gain_one,
        w_query,
        w_key,
        w_value,
        rel_bias,
        hot,
        seq_ids.reshape(1, length),
        w_attn_out,
        scratch=[pltpu.VMEM((length, width), bf16), pltpu.VMEM((width,), f32)]
        + [pltpu.VMEM((width, local), bf16)] * 3
        + [
            pltpu.VMEM(rel_bias.shape, f32),
            pltpu.VMEM(hot.shape, f32),
            pltpu.VMEM((1, length), jnp.int32),
            pltpu.VMEM((local, width), bf16),
            pltpu.SemaphoreType.DMA((9,)),
        ],
        far=range(9),
    )
    att_part, *cot_arrived = lax.optimization_barrier((att_part, *cot_arrived))
    cot_near = spread_first(join(cot_arrived + [early]))
    att_other = send(att_part, to_pair)
    residual, normed_two, router_probs, *row_chunks = call(
        functools.partial(middle_body, order, stride),
        "middle",
        ids,
        [((length, width), f32), ((length, width), bf16), ((length, experts), f32)]
        + [chunk] * experts,
        att_part,
        att_other,
        tokens,
        gain_two,
        router_t,
        slots,
    )
    *row_arrived, near, next_near = lax.optimization_barrier((*exchange(row_chunks), *cot_near[1:]))
    row_own, row_other = spread_rest(*spread_first(join(row_arrived)))
    cot_own, cot_other = spread_rest(cot_near[0], near, next_near)

    all_rows = 4 * slot_count
    rows_half = ((all_rows, half), bf16)
    units = expert_in.shape[2]
    act, slope, part_mine, part_other = call(
        functools.partial(expert_body, slot_count),
        "expert",
        ids,
        [((all_rows, units), bf16), ((all_rows, units), f32), rows_half, rows_half],
        *row_own,
        *row_other,
        expert_in,
        expert_out,
        limit=40,
    )
    two = ((2 * slot_count, half), bf16)
    one = ((slot_count, half), bf16)
    one_wide = ((slot_count, half), f32)

    keep, go = call(pair_sum_body, "pair_sum", ids, [two, two], part_mine, send(part_other, to_pair))
    part_kept, go = call(
        plane_sum_body, "plane_sum", ids, [one_wide, one], keep, send(go, to_first)
    )
    part_last = send(go, to_second)
    grad_pre, expert_cot, back_mine, back_other = call(
        functools.partial(expert_back_body, slot_count, experts),
        "expert_back",
        ids,
        [((all_rows, units), bf16), ((all_rows, width), bf16), rows_half, rows_half],
        *row_own,
        *row_other,
        *cot_own,
        *cot_other,
        expert_in,
        expert_out,
        router_t,
        slope,
        limit=40,
    )
    keep, go = call(pair_sum_body, "pair_sum", ids, [two, two], back_mine, send(back_other, to_pair))
    back_kept, go = call(
        plane_sum_body, "plane_sum", ids, [one_wide, one], keep, send(go, to_first)
    )
    back_last = send(go, to_second)
    grad_in, grad_out = call(
        functools.partial(expert_grads_body, slot_count),
        "expert_grads",
        ids,
        [(expert_in.shape, f32), (expert_out.shape, f32)],
        *row_own,
        *row_other,
        act,
        grad_pre,
        expert_cot,
        limit=40,
    )
    part_last, back_last, grad_in, grad_out = lax.optimization_barrier(
        (part_last, back_last, grad_in, grad_out)
    )
    chunks = call(
        functools.partial(last_sum_body, experts, stride),
        "last_sum",
        ids,
        [((2 * stride, half), bf16)] * experts,
        part_kept,
        part_last,
        back_kept,
        back_last,
    )
    returned = exchange(chunks)
    packed = call(
        functools.partial(combine_body, order, stride),
        "combine",
        ids,
        [((length, width + LANES), f32)],
        *returned,
        slots,
        routes_t,
        router_probs,
        cotangent,
        residual,
    )[0]
    output, grad_residual, grad_att, small_ffn = call(
        functools.partial(norm_back_body, experts),
        "norm_back",
        ids,
        [
            ((length, width), bf16),
            ((length, width), f32),
            ((length, width), bf16),
            ((1 + experts, width), f32),
        ],
        packed,
        send(packed, to_pair),
        normed_two,
        router_probs,
        residual,
        routes_t,
        cotangent,
        gain_two,
        router_t,
    )
    right0, right1, right2, right3, normed_part, bias = call(
        attend_back_body,
        "attend_back",
        ids,
        [local_out] * 4 + [((length, width), bf16), ((1, heads * length), f32)],
        grad_att,
        w_attn_out,
        queries,
        keys,
        values,
        early,
        probs,
        w_query,
        w_key,
        w_value,
        scratch=[pltpu.VMEM((4, length, local), bf16)],
    )
    right_all = [right0, send(right1, to_first), send(right2, to_second), send(right3, to_far)]
    small_rows = -(-(3 + experts) // 8) * 8
    grad_tokens, small = call(
        functools.partial(tokens_back_body, experts),
        "tokens_back",
        ids,
        [((length, width), f32), ((small_rows, width), f32)],
        normed_part,
        send(normed_part, to_pair),
        tokens,
        gain_one,
        grad_residual,
        small_ffn,
        bias,
    )
    *right_all, small = lax.optimization_barrier((*right_all, small))
    right_pair = [send(right_all[p], to_pair) for p in (0, 2, 1, 3)]
    depth = width // groups
    blocks = call(
        functools.partial(partial_body, order),
        "partial",
        ids,
        [((depth + 4 * small_rows, local), bf16)] * groups,
        *cot_own,
        *cot_other,
        *right_all,
        *right_pair,
        small,
        scratch=[pltpu.VMEM((width, local), f32)],
    )
    reduced, code = call(
        functools.partial(reduce_body, order, small_rows),
        "reduce",
        ids,
        [((depth, local), bf16), ((depth + 4 * small_rows, local), bf16)],
        *exchange(blocks),
        scratch=[pltpu.VMEM((groups, 2 * small_rows, local), f32)],
    )
    spread = exchange([reduced] * groups, last_order)
    def near(matrix):
        return [matrix, send(matrix, to_first), send(matrix, to_second)]

    start = near(code)
    joint = lax.optimization_barrier((*spread[1:-1], *start[1:]))
    start[1:] = joint[-2:]
    start.append(send(start[1], to_second))
    inner = near(join(joint[:-2]))
    last, *inner[1:], start[3] = lax.optimization_barrier((spread[-1], *inner[1:], start[3]))
    inner.append(send(inner[1], to_second))
    final_pieces = start + inner + near(last) + [send(last, to_far)]
    grads = call(
        functools.partial(final_body, last_order, experts, small_rows),
        "final",
        ids,
        [((width, local), f32)] * 3
        + [((local, width), f32), ((width,), f32), ((heads, bucket_count), f32)]
        + [((width,), f32), ((experts, width), f32)],
        *final_pieces,
        hot,
        scratch=[
            pltpu.VMEM((width, local), f32),
            pltpu.VMEM((4, 2 * small_rows, local), f32),
        ],
        limit=40,
    )
    return (
        output,
        grad_tokens,
        grads[4],
        grads[0],
        grads[1],
        grads[2],
        grads[3],
        grads[5],
        grads[6],
        grads[7].T,
        grad_in,
        grad_out,
    )


def solution(mesh):
    in_specs = (
        P("dp", None),
        P("dp"),
        P("dp", None),
        P(),
        P(None, "tensor"),
        P(None, "tensor"),
        P(None, "tensor"),
        P("tensor", None),
        P("tensor", None),
        P(),
        P(),
        P("dp", None, "tensor"),
        P("dp", "tensor", None),
        P("dp", None),
    )
    out_specs = (
        P("dp", None),
        P("dp", None),
        P(),
        P(None, "tensor"),
        P(None, "tensor"),
        P(None, "tensor"),
        P("tensor", None),
        P("tensor", None),
        P(),
        P(),
        P("dp", None, "tensor"),
        P("dp", "tensor", None),
    )
    return jax.shard_map(
        functools.partial(on_device, mesh.shape["dp"], mesh.shape["tensor"]),
        mesh=mesh,
        in_specs=in_specs,
        out_specs=out_specs,
        check_vma=False,
    )
```

```python
import functools

import jax
import jax.numpy as jnp
import numpy as np
from jax import lax
from jax.experimental import pallas as pl
from jax.experimental.pallas import tpu as pltpu
from jax.sharding import PartitionSpec as P

HEAD_DIM = 64
TOP = 2
REACH = 64
LANES = 128

eps_norm = 1e-06
gelu_scale = float(np.sqrt(2.0 / np.pi))
microseconds = {"front": 5, "route": 1.9, "expert": 4.4, "expert_back": 5.4, "expert_grads": 4.0, "combine": 1.9, "attend_back": 2.5, "partial": 1.2, "final": 3.9, "tokens_back": 1.5, "small": 1.4}
f32 = jnp.float32
bf16 = jnp.bfloat16


def bucket_of_distance(length, buckets, max_reach):
    exact_span = buckets // 2
    distance = np.arange(length)
    log_ratio = np.log(np.maximum(distance, exact_span) / exact_span) / np.log(
        max_reach / exact_span
    )
    coarse = exact_span + np.floor(log_ratio * (buckets - exact_span)).astype(np.int64)
    return np.where(distance < exact_span, distance, np.minimum(coarse, buckets - 1))


def nn(left, right, precision=None):
    return lax.dot_general(
        left, right, (((1,), (0,)), ((), ())), precision=precision, preferred_element_type=f32
    )


def nt(left, right):
    return lax.dot_general(left, right, (((1,), (1,)), ((), ())), preferred_element_type=f32)


def tn(left, right):
    return lax.dot_general(left, right, (((0,), (0,)), ((), ())), preferred_element_type=f32)


def iota(shape, axis):
    return lax.broadcasted_iota(jnp.int32, shape, axis)


def call(body, name, ids, outs, *args, scratch=(), limit=24, far=()):
    shapes = [jax.ShapeDtypeStruct(shape, dtype) for shape, dtype in outs]
    return pl.pallas_call(
        body,
        out_shape=shapes,
        in_specs=[pl.BlockSpec(memory_space=pltpu.SMEM)]
        + [
            pl.BlockSpec(memory_space=pltpu.HBM if i in far else pltpu.VMEM)
            for i in range(len(args))
        ],
        out_specs=[pl.BlockSpec(memory_space=pltpu.VMEM)] * len(outs),
        scratch_shapes=list(scratch),
        compiler_params=pltpu.CompilerParams(vmem_limit_bytes=limit << 20),
        cost_estimate=pl.CostEstimate(
            flops=0, transcendentals=0, bytes_accessed=int(microseconds.get(name, 0.8) * 3.6e6)
        ),
        name=name,
    )(
        ids,
        *[
            pltpu.with_memory_space_constraint(a, pltpu.HBM) if i in far else a
            for i, a in enumerate(args)
        ],
    )


def halves(value, t):
    width = value.shape[1] // 2
    low, high = value[:, :width], value[:, width:]
    even = t == 0
    return jnp.where(even, low, high), jnp.where(even, high, low)


def row_halves(value, t):
    width = value.shape[0] // 2
    low, high = value[:width], value[width:]
    even = t == 0
    return jnp.where(even, low, high), jnp.where(even, high, low)


def columns_of(row):
    length = row.shape[1]
    return jnp.broadcast_to(row.astype(f32), (length, length)).T


def sums_by_distance(square):
    length = square.shape[0]
    rows = length // 2
    while rows >= 1:
        square = square[:rows] + pltpu.roll(square[rows:], length - rows, 1)
        rows //= 2
    return square


def fetch(sources, targets, sems):
    copies = [
        pltpu.make_async_copy(source, target, sems.at[i])
        for i, (source, target) in enumerate(zip(sources, targets))
    ]
    for copy in copies:
        copy.start()
    return copies


def route_body(order, stride, ids, routes_far, cot_far, slots, *refs):
    experts = len(order)
    chunks, (routes, cot, sems) = refs[:experts], refs[experts:]
    copies = fetch((routes_far, cot_far), (routes, cot), sems)
    copies[0].wait()
    e, t = ids[0], ids[2]
    length = routes.shape[1]
    expert_row = iota((experts, length), 0)
    first = (expert_row == routes[0:1, :]).astype(f32)
    second = (expert_row == routes[1:2, :]).astype(f32)
    earlier = (iota((length, length), 0) < iota((length, length), 1)).astype(bf16)
    before = nn((first + second).astype(bf16), earlier)
    rank0 = jnp.sum(before * first, axis=0, keepdims=True).astype(jnp.int32)
    rank1 = jnp.sum(before * second, axis=0, keepdims=True).astype(jnp.int32)
    slot0 = (routes[0:1, :] ^ e) * stride + rank0
    slot1 = (routes[1:2, :] ^ e) * stride + rank1
    slots[0:1, :] = slot0
    slots[1:2, :] = slot1
    copies[1].wait()
    mine, _ = halves(cot[...], t)
    for s in range(experts):
        place = iota((stride, length), 0) + order[s] * stride
        pick = ((place == slot0) | (place == slot1)).astype(bf16)
        chunks[s][...] = nn(pick, mine).astype(bf16)


def front_body(ids, *refs):
    sources = refs[:9]
    early, part, q_out, k_out, v_out, probs = refs[9:15]
    targets, sems = refs[15:-1], refs[-1]
    tokens, gain, wq, wk, wv, rel, hot, seq, wo = targets
    copies = fetch(sources, targets, sems)
    t = ids[2]
    length = tokens.shape[0]
    mixed_out = early.at[pl.ds(length, length), :]
    copies[0].wait()
    copies[1].wait()
    wide = tokens[...].astype(f32)
    inv = lax.rsqrt(jnp.mean(wide * wide, axis=-1, keepdims=True) + eps_norm)
    value = (wide * inv * gain[...][None, :]).astype(bf16)
    early[pl.ds(0, length), :] = halves(value, t)[0]
    rows = length
    copies[2].wait()
    queries = nn(value, wq[...]).astype(bf16)
    copies[3].wait()
    keys = nn(value, wk[...]).astype(bf16)
    copies[4].wait()
    values = nn(value, wv[...]).astype(bf16)
    q_out[...] = queries
    k_out[...] = keys
    v_out[...] = values
    for copy in copies[5:8]:
        copy.wait()
    seq_cols = jnp.broadcast_to(seq[...].astype(f32), (rows, rows))
    allowed = (seq_cols == seq_cols.T) & (iota((rows, rows), 0) >= iota((rows, rows), 1))
    table = nn(rel[...], hot[...], lax.Precision.HIGHEST)
    lane = iota((rows, LANES), 1)
    pairs = [slice(i, i + LANES) for i in range(0, queries.shape[1], LANES)]
    heads = [(span, lane < HEAD_DIM if side == 0 else lane >= HEAD_DIM) for span in pairs for side in (0, 1)]
    raw = [
        nt(jnp.where(mine, queries[:, span], jnp.zeros((), bf16)), keys[:, span])
        for span, mine in heads
    ]
    biases = [
        pltpu.roll(
            jnp.broadcast_to(table[i : i + 1, :], (rows, rows)), 0, 1, stride=1, stride_axis=0
        )
        for i in range(len(heads))
    ]
    scores = [jnp.where(allowed, r * HEAD_DIM ** (-0.5) + b, -1e30) for r, b in zip(raw, biases)]
    tops = [jnp.max(x, axis=-1, keepdims=True) for x in scores]
    raised = [jnp.exp(x - top) for x, top in zip(scores, tops)]
    weights = [x / jnp.sum(x, axis=-1, keepdims=True) for x in raised]
    mixed = [nn(x.astype(bf16), values[:, span]) for x, (span, _) in zip(weights, heads)]
    for i, x in enumerate(weights):
        probs[i] = x
    for i, span in enumerate(pairs):
        mixed_out[:, span] = jnp.where(lane < HEAD_DIM, mixed[2 * i], mixed[2 * i + 1]).astype(bf16)
    copies[8].wait()
    part[...] = nn(mixed_out[...], wo[...])


def router_of(normed, weights_row):
    logits = nt(normed, weights_row)
    raised = jnp.exp(logits - jnp.max(logits, axis=-1, keepdims=True))
    return raised / jnp.sum(raised, axis=-1, keepdims=True)


def middle_body(order, stride, ids, own, other, tokens, gain, router, slots, residual, normed, probs, *chunks):
    t = ids[2]
    wide = tokens[...].astype(f32) + (own[...] + other[...])
    residual[...] = wide
    inv = lax.rsqrt(jnp.mean(wide * wide, axis=-1, keepdims=True) + eps_norm)
    value = (wide * inv * gain[...][None, :]).astype(bf16)
    normed[...] = value
    mine, _ = halves(value, t)
    length = slots.shape[1]
    for s in range(len(order)):
        place = iota((stride, length), 0) + order[s] * stride
        pick = ((place == slots[0:1, :]) | (place == slots[1:2, :])).astype(bf16)
        chunks[s][...] = nn(pick, mine).astype(bf16)
    probs[...] = router_of(value, router[...])


def join_body(ids, *refs):
    out = refs[-1]
    start = 0
    for ref in refs[:-1]:
        out[pl.ds(start, ref.shape[0]), :] = ref[...]
        start += ref.shape[0]


def in_order(own, other, even):
    return jnp.concatenate([jnp.where(even, own, other), jnp.where(even, other, own)], axis=1)


def expert_body(rows, ids, *refs):
    own, other = refs[:4], refs[4:8]
    w_in, w_out, act, slope, part_mine, part_other = refs[8:]
    t = ids[2]
    for p in range(4):
        span = pl.ds(p * rows, rows)
        pre = nn(in_order(own[p][...], other[p][...], t == 0), w_in[0])
        square = pre * pre
        bent = jnp.tanh(gelu_scale * (pre + 0.044715 * pre * square))
        half = 0.5 * (1.0 + bent)
        value = (pre * half).astype(bf16)
        act[span, :] = value
        slope[span, :] = half + 0.5 * pre * (1.0 - bent * bent) * (
            gelu_scale * (1.0 + 3 * 0.044715 * square)
        )
        mine, rest = halves(nn(value, w_out[0]).astype(bf16), t)
        part_mine[span, :] = mine
        part_other[span, :] = rest


def expert_back_body(rows, experts, ids, *refs):
    own, other, cot_own, cot_other = refs[:4], refs[4:8], refs[8:12], refs[12:16]
    w_in, w_out, router, slope, grad_pre, grads, back_mine, back_other = refs[16:]
    e, t = ids[0], ids[2]
    gates = []
    for p in range(4):
        logits = nt(in_order(own[p][...], other[p][...], t == 0), router[...])
        raised = jnp.exp(logits - jnp.max(logits, axis=-1, keepdims=True))
        chosen = jnp.where(iota(raised.shape, 1) == e, raised, 0.0)
        gates.append(
            jnp.sum(chosen, axis=-1, keepdims=True) / jnp.sum(raised, axis=-1, keepdims=True)
        )
    for p in range(4):
        span = pl.ds(p * rows, rows)
        cot_rows = pl.ds(0, rows)
        cot = in_order(cot_own[p][cot_rows, :], cot_other[p][cot_rows, :], t == 0)
        grad = (gates[p] * cot.astype(f32)).astype(bf16)
        grads[span, :] = grad
        value = (nt(grad, w_out[0]) * slope[span, :]).astype(bf16)
        grad_pre[span, :] = value
        mine, rest = halves(nt(value, w_in[0]).astype(bf16), t)
        back_mine[span, :] = mine
        back_other[span, :] = rest


def expert_grads_body(rows, ids, *refs):
    own, other = refs[:4], refs[4:8]
    act, grad_pre, grads, out_in, out_out = refs[8:]
    even = ids[2] == 0
    out_out[0] = tn(act[...], grads[...])
    sent = jnp.concatenate([in_order(own[p][...], other[p][...], even) for p in range(4)], axis=0)
    out_in[0] = tn(sent, grad_pre[...])


def pair_sum_body(ids, mine, received, keep, send):
    rows = mine.shape[0] // 4

    def block(p):
        q = (0, 2, 1, 3)[p]
        left = mine[pl.ds(p * rows, rows), :].astype(f32)
        return (left + received[pl.ds(q * rows, rows), :].astype(f32)).astype(bf16)

    keep[pl.ds(0, rows), :] = block(0)
    keep[pl.ds(rows, rows), :] = block(2)
    send[pl.ds(0, rows), :] = block(1)
    send[pl.ds(rows, rows), :] = block(3)


def plane_sum_body(ids, keep, received, kept, send):
    rows = keep.shape[0] // 2
    total = keep[...].astype(f32) + received[...].astype(f32)
    kept[...] = total[:rows]
    send[...] = total[rows:].astype(bf16)


def last_sum_body(experts, stride, ids, kept, received, kept_back, received_back, *chunks):
    first = (kept[...] + received[...].astype(f32)).astype(bf16)
    second = (kept_back[...] + received_back[...].astype(f32)).astype(bf16)
    for s in range(experts):
        chunks[s][pl.ds(0, stride), :] = first[s * stride : (s + 1) * stride]
        chunks[s][pl.ds(stride, stride), :] = second[s * stride : (s + 1) * stride]


def combine_body(order, stride, ids, *refs):
    experts = len(order)
    chunks = refs[:experts]
    slots, routes, probs, cot, residual, packed = refs[experts:]
    t = ids[2]
    length = slots.shape[1]
    probs_all = probs[...]
    choice = iota(probs_all.shape, 1)
    cot_mine = halves(cot[...], t)[0].astype(f32)
    mixture = None
    back = None
    lanes = iota((length, LANES), 1)
    dots = jnp.zeros((length, LANES), f32)
    for k in range(TOP):
        slot = columns_of(slots[k : k + 1, :])
        route = columns_of(routes[k : k + 1, :])[:, : probs_all.shape[1]]
        gate = jnp.sum(
            jnp.where(choice.astype(f32) == route, probs_all, 0.0), axis=-1, keepdims=True
        )
        chosen = None
        for s in range(experts):
            place = (iota((length, stride), 1) + order[s] * stride).astype(f32)
            pick = (place == slot[:, :1]).astype(bf16)
            value = nn(pick, chunks[s][pl.ds(0, stride), :])
            grad = nn(pick, chunks[s][pl.ds(stride, stride), :])
            chosen = value if chosen is None else chosen + value
            back = grad if back is None else back + grad
        mixture = gate * chosen if mixture is None else mixture + gate * chosen
        dots = jnp.where(lanes == k, jnp.sum(cot_mine * chosen, axis=-1, keepdims=True), dots)
    width = back.shape[1]
    packed[:, :width] = back
    packed[:, width : 2 * width] = halves(residual[...], t)[0] + mixture
    packed[:, 2 * width :] = dots


def norm_back_body(
    experts, ids, own, other, normed, probs, residual, routes, cot, gain, router, output, grad_out, att, small
):
    even = ids[2] == 0
    width = residual.shape[1] // 2
    first, last = slice(0, width), slice(width, 2 * width)
    low = jnp.where(even, own[:, first], other[:, first])
    high = jnp.where(even, other[:, first], own[:, first])
    back = jnp.concatenate([low, high], axis=1)
    output[:, first] = jnp.where(even, own[:, last], other[:, last]).astype(bf16)
    output[:, last] = jnp.where(even, other[:, last], own[:, last]).astype(bf16)
    dots = own[:, 2 * width :] + other[:, 2 * width :]
    probs_all = probs[...]
    choice = iota(probs_all.shape, 1).astype(f32)
    grad_probs = jnp.zeros_like(probs_all)
    for k in range(TOP):
        route = columns_of(routes[k : k + 1, :])[:, : probs_all.shape[1]]
        grad_probs = grad_probs + jnp.where(choice == route, dots[:, k : k + 1], 0.0)
    inner = jnp.sum(probs_all * grad_probs, axis=-1, keepdims=True)
    grad_logits = (probs_all * (grad_probs - inner)).astype(bf16)
    grad_normed = back + nn(grad_logits, router[...])
    wide = residual[...]
    inv = lax.rsqrt(jnp.mean(wide * wide, axis=-1, keepdims=True) + eps_norm)
    scaled = grad_normed * gain[...][None, :]
    grad = (
        cot[...].astype(f32)
        + inv * scaled
        - wide * (inv * inv * inv) * jnp.mean(scaled * wide, axis=-1, keepdims=True)
    )
    grad_out[...] = grad
    att[...] = grad.astype(bf16)
    small[0:1, :] = jnp.sum(grad_normed * wide * inv, axis=0, keepdims=True)
    small[pl.ds(1, experts), :] = tn(grad_logits, normed[...])


def attend_back_body(
    ids, att, wo, q_in, k_in, v_in, mixed_in, probs, wq, wk, wv, r0, r1, r2, r3, normed_part, bias, stack
):
    q_id, t = ids[1], ids[2]
    grad = att[...]
    rows = grad.shape[0]
    lane = iota((rows, LANES), 1)
    scale = HEAD_DIM ** (-0.5)
    pairs = [slice(i, i + LANES) for i in range(0, q_in.shape[1], LANES)]
    heads = [(i, lane < HEAD_DIM if side == 0 else lane >= HEAD_DIM) for i in range(len(pairs)) for side in (0, 1)]
    grad_mixed = [nt(grad, wo[span, :]).astype(bf16) for span in pairs]
    queries, keys, values = ([ref[:, span] for span in pairs] for ref in (q_in, k_in, v_in))
    mixed = [mixed_in[pl.ds(rows, rows), span].astype(f32) for span in pairs]
    weights = [probs[i] for i in range(len(heads))]
    parts = [jnp.where(mine, grad_mixed[i], jnp.zeros((), bf16)) for i, mine in heads]
    inner = [nt(part, values[i]) for part, (i, _) in zip(parts, heads)]
    deltas = [
        jnp.sum(part.astype(f32) * mixed[i], axis=-1, keepdims=True)
        for part, (i, _) in zip(parts, heads)
    ]
    scores = [w * (x - delta) for w, x, delta in zip(weights, inner, deltas)]
    half = [x.astype(bf16) for x in scores]
    dv = [tn(w.astype(bf16), grad_mixed[i]) for w, (i, _) in zip(weights, heads)]
    dq = [nn(x, keys[i]) for x, (i, _) in zip(half, heads)]
    dk = [tn(x, queries[i]) for x, (i, _) in zip(half, heads)]
    sums = [sums_by_distance(x) for x in scores]
    first = lane < HEAD_DIM
    for i, span in enumerate(pairs):
        stack[0, :, span] = (jnp.where(first, dq[2 * i], dq[2 * i + 1]) * scale).astype(bf16)
        stack[1, :, span] = (jnp.where(first, dk[2 * i], dk[2 * i + 1]) * scale).astype(bf16)
        stack[2, :, span] = jnp.where(first, dv[2 * i], dv[2 * i + 1]).astype(bf16)
    for i, row in enumerate(sums):
        bias[0:1, i * rows : (i + 1) * rows] = row
    stack[3] = halves(grad, t)[0]
    r0[...] = stack[q_id]
    r1[...] = stack[q_id ^ (1 + t)]
    r2[...] = stack[q_id ^ (2 - t)]
    r3[...] = stack[q_id ^ 3]
    total = nt(stack[0], wq[...]) + nt(stack[1], wk[...]) + nt(stack[2], wv[...])
    normed_part[...] = total.astype(bf16)


def tokens_back_body(experts, ids, own, other, tokens, gain, grad_res, small_ffn, bias, out, small):
    wide = tokens[...].astype(f32)
    inv = lax.rsqrt(jnp.mean(wide * wide, axis=-1, keepdims=True) + eps_norm)
    grad_normed = own[...].astype(f32) + other[...].astype(f32)
    scaled = grad_normed * gain[...][None, :]
    out[...] = (
        grad_res[...]
        + inv * scaled
        - wide * (inv * inv * inv) * jnp.mean(scaled * wide, axis=-1, keepdims=True)
    )
    small[...] = jnp.zeros_like(small)
    small[0:1, :] = jnp.sum(grad_normed * wide * inv, axis=0, keepdims=True)
    small[1:2, :] = bias[...]
    small[pl.ds(2, 1 + experts), :] = small_ffn[...]


def encode(value):
    width = value.shape[1] // 2
    tall = jnp.concatenate([value[:, :width], value[:, width:]], axis=0)
    lead = tall.astype(bf16)
    return lead, (tall - lead.astype(f32)).astype(bf16)


def decode(ref, start, rows):
    lead = ref[pl.ds(start, 2 * rows), :].astype(f32)
    return lead + ref[pl.ds(start + 2 * rows, 2 * rows), :].astype(f32)


def widen(tall):
    rows = tall.shape[0] // 2
    return jnp.concatenate([tall[:rows], tall[rows:]], axis=1)


def partial_body(order, ids, *refs):
    early_own, early_other = refs[:4], refs[4:8]
    right, right_pair, small = refs[8:12], refs[12:16], refs[16]
    blocks, total = refs[17:-1], refs[-1]
    e, q, t = ids[0], ids[1], ids[2]
    even = t == 0
    is_last = q == 3
    tokens = right[0].shape[0]
    rows = early_own[0].shape[0]
    width = early_own[0].shape[1]
    low, high, rights = [], [], []
    normed, mixed = pl.ds(rows - 2 * tokens, tokens), pl.ds(rows - tokens, tokens)
    for p in range(4):
        mine = jnp.where(is_last, right[p][...], early_own[p][normed, :])
        other = jnp.where(is_last, right_pair[p][...], early_other[p][normed, :])
        low.append(jnp.where(even, mine, other))
        high.append(jnp.where(even, other, mine))
        rights.append(jnp.where(is_last, early_own[p][mixed, :], right[p][...]))
    rights = jnp.concatenate(rights, axis=0)
    total[:width, :] = tn(jnp.concatenate(low, axis=0), rights)
    total[width:, :] = tn(jnp.concatenate(high, axis=0), rights)
    groups = len(order)
    depth = total.shape[0] // groups
    lead, rest = encode(small[...])
    for s in range(groups):
        start = pl.multiple_of((e ^ order[s]) * depth, 8)
        blocks[s][pl.ds(0, depth), :] = total[pl.ds(start, depth), :].astype(bf16)
        blocks[s][pl.ds(depth, lead.shape[0]), :] = lead
        blocks[s][pl.ds(depth + lead.shape[0], lead.shape[0]), :] = rest


def reduce_body(order, rows, ids, *refs):
    groups = len(order)
    arrived, outs = refs[:groups], refs[groups:]
    depth = outs[0].shape[0]
    total = arrived[0][pl.ds(0, depth), :].astype(f32)
    for ref in arrived[1:]:
        total = total + ref[pl.ds(0, depth), :].astype(f32)
    outs[0][...] = total.astype(bf16)
    code, stack = outs[1:]
    for s in range(groups):
        stack[order[s]] = decode(arrived[s], depth, rows)
    small = stack[ids[0]]
    for k in range(1, groups):
        small = small + stack[ids[0] ^ k]
    lead = small.astype(bf16)
    code[pl.ds(0, depth), :] = outs[0][...]
    code[pl.ds(depth, 2 * rows), :] = lead
    code[pl.ds(depth + 2 * rows, 2 * rows), :] = (small - lead.astype(f32)).astype(bf16)


def final_body(order, experts, rows, ids, *refs):
    groups = len(order)
    pieces, hot, outs = refs[:12], refs[12], refs[13:17]
    gain_attn, bias, gain_ffn, router = refs[17:21]
    square, small = refs[21:]
    e, q, t = ids[0], ids[1], ids[2]
    depth = square.shape[0] // groups

    def place_of(chip):
        away = q ^ chip
        return jnp.where((t == 1) & ((away == 1) | (away == 2)), 3 - away, away)

    for p in range(4):
        small[p] = decode(pieces[p], depth, rows)
    for m in range(4):
        out = outs[m] if m < 3 else square
        place = place_of(m)
        for p in range(4):

            @pl.when(place == p)
            def _(p=p, out=out):
                for s in range(groups):
                    start = pl.multiple_of((order[s] ^ e) * depth, 8)
                    step, at = (0, 0) if s == 0 else (2, 0) if s == groups - 1 else (1, s - 1)
                    piece = pieces[step * 4 + p]
                    out[pl.ds(start, depth), :] = piece[pl.ds(at * depth, depth), :].astype(f32)

    outs[3][...] = square[...].T
    total = widen(small[place_of(0)] + small[place_of(1)] + small[place_of(2)] + small[place_of(3)])
    gain_attn[...] = total[0]
    gain_ffn[...] = total[2]
    router[...] = total[3 : 3 + experts]
    length = hot.shape[1]
    for head in range(bias.shape[0]):
        line = jnp.broadcast_to(total[1:2, head * length : (head + 1) * length], (8, length))
        value = lax.dot_general(
            line,
            hot[...],
            (((1,), (1,)), ((), ())),
            precision=lax.Precision.HIGHEST,
            preferred_element_type=f32,
        )
        bias[head : head + 1, :] = value[0:1]


def on_device(
    n_dp,
    n_tensor,
    tokens,
    seq_ids,
    routes,
    gain_attn,
    w_query,
    w_key,
    w_value,
    w_attn_out,
    rel_bias,
    gain_ffn,
    w_router,
    expert_in,
    expert_out,
    cotangent,
):
    groups = n_dp // 4
    length, width = tokens.shape
    half = width // 2
    experts = w_router.shape[1]
    bucket_count = rel_bias.shape[1]
    heads = rel_bias.shape[0]
    local = w_query.shape[1]
    capacity = 4 * ((5 * TOP * length + 16 * experts - 1) // (16 * experts))
    stride = -(-capacity // 16) * 16
    slot_count = experts * stride
    dp_id = lax.axis_index("dp")
    t_id = lax.axis_index("tensor")
    ids = jnp.stack([dp_id // 4, dp_id % 4, t_id]).astype(jnp.int32)

    def send(array, target, only=None):
        pairs = []
        for dp in range(n_dp):
            for t in range(n_tensor):
                e_to, q_to, t_to = target(dp // 4, dp % 4, t)
                if only is None or q_to == only:
                    pairs.append((dp * n_tensor + t, (e_to * 4 + q_to) * n_tensor + t_to))
        return lax.ppermute(array, ("dp", "tensor"), pairs)

    def to_pair(e, q, t):
        return e, q, 1 - t

    def to_first(e, q, t):
        return e, q ^ (1 + t), t

    def to_second(e, q, t):
        return e, q ^ (2 - t), t

    def to_far(e, q, t):
        return e, q ^ 3, t

    def to_group(step):
        return lambda e, q, t: (e ^ step, q, t)

    order = (0, *range(groups // 2, groups), *range(1, groups // 2))
    last_order = (0, *range(groups // 2, groups - 1), *range(1, groups // 2), groups - 1)

    def exchange(chunks, order=order):
        return [chunks[0]] + [
            send(chunk, to_group(step)) for chunk, step in zip(chunks[1:], order[1:])
        ]

    def join(arrays):
        rows = sum(a.shape[0] for a in arrays)
        return call(join_body, "join", ids, [((rows, arrays[0].shape[1]), arrays[0].dtype)], *arrays)[0]

    def spread_first(block):
        return block, send(block, to_first), send(block, to_second)

    def spread_rest(block, first, second):
        own = [block, first, second, send(first, to_second)]
        other = [send(piece, to_pair) for piece in own]
        return own, [other[0], other[2], other[1], other[3]]

    routes_t = routes.T
    gain_one, gain_two = gain_attn, gain_ffn
    router_t = w_router.T
    distance_bucket = bucket_of_distance(length, bucket_count, REACH)
    hot = (
        distance_bucket[(-np.arange(length)) % length][None, :] == np.arange(bucket_count)[:, None]
    ).astype(np.float32)
    hot = jnp.asarray(hot)

    chunk = ((stride, half), bf16)
    local_out = ((length, local), bf16)
    slots, *cot_chunks = call(
        functools.partial(route_body, order, stride),
        "route",
        ids,
        [((TOP, length), jnp.int32)] + [chunk] * experts,
        routes_t,
        cotangent,
        scratch=[
            pltpu.VMEM((TOP, length), jnp.int32),
            pltpu.VMEM((length, width), bf16),
            pltpu.SemaphoreType.DMA((2,)),
        ],
        far=(0, 1),
    )
    cot_arrived = exchange(cot_chunks)
    early, att_part, queries, keys, values, probs = call(
        front_body,
        "front",
        ids,
        [((2 * length, half), bf16), ((length, width), f32)]
        + [local_out] * 3
        + [((heads, length, length), f32)],
        tokens,
        gain_one,
        w_query,
        w_key,
        w_value,
        rel_bias,
        hot,
        seq_ids.reshape(1, length),
        w_attn_out,
        scratch=[pltpu.VMEM((length, width), bf16), pltpu.VMEM((width,), f32)]
        + [pltpu.VMEM((width, local), bf16)] * 3
        + [
            pltpu.VMEM(rel_bias.shape, f32),
            pltpu.VMEM(hot.shape, f32),
            pltpu.VMEM((1, length), jnp.int32),
            pltpu.VMEM((local, width), bf16),
            pltpu.SemaphoreType.DMA((9,)),
        ],
        far=range(9),
    )
    att_part, *cot_arrived = lax.optimization_barrier((att_part, *cot_arrived))
    cot_near = spread_first(join(cot_arrived + [early]))
    att_other = send(att_part, to_pair)
    residual, normed_two, router_probs, *row_chunks = call(
        functools.partial(middle_body, order, stride),
        "middle",
        ids,
        [((length, width), f32), ((length, width), bf16), ((length, experts), f32)]
        + [chunk] * experts,
        att_part,
        att_other,
        tokens,
        gain_two,
        router_t,
        slots,
    )
    *row_arrived, near, next_near = lax.optimization_barrier((*exchange(row_chunks), *cot_near[1:]))
    row_own, row_other = spread_rest(*spread_first(join(row_arrived)))
    cot_own, cot_other = spread_rest(cot_near[0], near, next_near)

    all_rows = 4 * slot_count
    rows_half = ((all_rows, half), bf16)
    units = expert_in.shape[2]
    act, slope, part_mine, part_other = call(
        functools.partial(expert_body, slot_count),
        "expert",
        ids,
        [((all_rows, units), bf16), ((all_rows, units), f32), rows_half, rows_half],
        *row_own,
        *row_other,
        expert_in,
        expert_out,
        limit=40,
    )
    two = ((2 * slot_count, half), bf16)
    one = ((slot_count, half), bf16)
    one_wide = ((slot_count, half), f32)

    keep, go = call(pair_sum_body, "pair_sum", ids, [two, two], part_mine, send(part_other, to_pair))
    part_kept, go = call(
        plane_sum_body, "plane_sum", ids, [one_wide, one], keep, send(go, to_first)
    )
    part_last = send(go, to_second)
    grad_pre, expert_cot, back_mine, back_other = call(
        functools.partial(expert_back_body, slot_count, experts),
        "expert_back",
        ids,
        [((all_rows, units), bf16), ((all_rows, width), bf16), rows_half, rows_half],
        *row_own,
        *row_other,
        *cot_own,
        *cot_other,
        expert_in,
        expert_out,
        router_t,
        slope,
        limit=40,
    )
    keep, go = call(pair_sum_body, "pair_sum", ids, [two, two], back_mine, send(back_other, to_pair))
    back_kept, go = call(
        plane_sum_body, "plane_sum", ids, [one_wide, one], keep, send(go, to_first)
    )
    back_last = send(go, to_second)
    grad_in, grad_out = call(
        functools.partial(expert_grads_body, slot_count),
        "expert_grads",
        ids,
        [(expert_in.shape, f32), (expert_out.shape, f32)],
        *row_own,
        *row_other,
        act,
        grad_pre,
        expert_cot,
        limit=40,
    )
    part_last, back_last, grad_in, grad_out = lax.optimization_barrier(
        (part_last, back_last, grad_in, grad_out)
    )
    chunks = call(
        functools.partial(last_sum_body, experts, stride),
        "last_sum",
        ids,
        [((2 * stride, half), bf16)] * experts,
        part_kept,
        part_last,
        back_kept,
        back_last,
    )
    returned = exchange(chunks)
    packed = call(
        functools.partial(combine_body, order, stride),
        "combine",
        ids,
        [((length, width + LANES), f32)],
        *returned,
        slots,
        routes_t,
        router_probs,
        cotangent,
        residual,
    )[0]
    output, grad_residual, grad_att, small_ffn = call(
        functools.partial(norm_back_body, experts),
        "norm_back",
        ids,
        [
            ((length, width), bf16),
            ((length, width), f32),
            ((length, width), bf16),
            ((1 + experts, width), f32),
        ],
        packed,
        send(packed, to_pair),
        normed_two,
        router_probs,
        residual,
        routes_t,
        cotangent,
        gain_two,
        router_t,
    )
    right0, right1, right2, right3, normed_part, bias = call(
        attend_back_body,
        "attend_back",
        ids,
        [local_out] * 4 + [((length, width), bf16), ((1, heads * length), f32)],
        grad_att,
        w_attn_out,
        queries,
        keys,
        values,
        early,
        probs,
        w_query,
        w_key,
        w_value,
        scratch=[pltpu.VMEM((4, length, local), bf16)],
    )
    right_all = [right0, send(right1, to_first), send(right2, to_second), send(right3, to_far)]
    small_rows = -(-(3 + experts) // 8) * 8
    grad_tokens, small = call(
        functools.partial(tokens_back_body, experts),
        "tokens_back",
        ids,
        [((length, width), f32), ((small_rows, width), f32)],
        normed_part,
        send(normed_part, to_pair),
        tokens,
        gain_one,
        grad_residual,
        small_ffn,
        bias,
    )
    *right_all, small = lax.optimization_barrier((*right_all, small))
    right_pair = [send(right_all[p], to_pair) for p in (0, 2, 1, 3)]
    depth = width // groups
    blocks = call(
        functools.partial(partial_body, order),
        "partial",
        ids,
        [((depth + 4 * small_rows, local), bf16)] * groups,
        *cot_own,
        *cot_other,
        *right_all,
        *right_pair,
        small,
        scratch=[pltpu.VMEM((width, local), f32)],
    )
    reduced, code = call(
        functools.partial(reduce_body, order, small_rows),
        "reduce",
        ids,
        [((depth, local), bf16), ((depth + 4 * small_rows, local), bf16)],
        *exchange(blocks),
        scratch=[pltpu.VMEM((groups, 2 * small_rows, local), f32)],
    )
    spread = exchange([reduced] * groups, last_order)
    def near(matrix):
        return [matrix, send(matrix, to_first), send(matrix, to_second)]

    start = near(code)
    joint = lax.optimization_barrier((*spread[1:-1], *start[1:]))
    start[1:] = joint[-2:]
    start.append(send(start[1], to_second))
    inner = near(join(joint[:-2]))
    last, start[3] = lax.optimization_barrier((spread[-1], start[3]))
    inner.append(send(inner[1], to_second))
    final_pieces = start + inner + near(last) + [send(last, to_far)]
    grads = call(
        functools.partial(final_body, last_order, experts, small_rows),
        "final",
        ids,
        [((width, local), f32)] * 3
        + [((local, width), f32), ((width,), f32), ((heads, bucket_count), f32)]
        + [((width,), f32), ((experts, width), f32)],
        *final_pieces,
        hot,
        scratch=[
            pltpu.VMEM((width, local), f32),
            pltpu.VMEM((4, 2 * small_rows, local), f32),
        ],
        limit=40,
    )
    return (
        output,
        grad_tokens,
        grads[4],
        grads[0],
        grads[1],
        grads[2],
        grads[3],
        grads[5],
        grads[6],
        grads[7].T,
        grad_in,
        grad_out,
    )


def solution(mesh):
    in_specs = (
        P("dp", None),
        P("dp"),
        P("dp", None),
        P(),
        P(None, "tensor"),
        P(None, "tensor"),
        P(None, "tensor"),
        P("tensor", None),
        P("tensor", None),
        P(),
        P(),
        P("dp", None, "tensor"),
        P("dp", "tensor", None),
        P("dp", None),
    )
    out_specs = (
        P("dp", None),
        P("dp", None),
        P(),
        P(None, "tensor"),
        P(None, "tensor"),
        P(None, "tensor"),
        P("tensor", None),
        P("tensor", None),
        P(),
        P(),
        P("dp", None, "tensor"),
        P("dp", "tensor", None),
    )
    return jax.shard_map(
        functools.partial(on_device, mesh.shape["dp"], mesh.shape["tensor"]),
        mesh=mesh,
        in_specs=in_specs,
        out_specs=out_specs,
        check_vma=False,
    )
```

```python
import functools

import jax
import jax.numpy as jnp
import numpy as np
from jax import lax
from jax.experimental import pallas as pl
from jax.experimental.pallas import tpu as pltpu
from jax.sharding import PartitionSpec as P

HEAD_DIM = 64
TOP = 2
REACH = 64
LANES = 128

eps_norm = 1e-06
gelu_scale = float(np.sqrt(2.0 / np.pi))
microseconds = {"front": 5, "route": 1.9, "expert": 4.4, "expert_back": 5.4, "expert_grads": 4.0, "combine": 1.9, "attend_back": 2.5, "partial": 1.2, "final": 3.9, "tokens_back": 1.5, "small": 1.4}
f32 = jnp.float32
bf16 = jnp.bfloat16


def bucket_of_distance(length, buckets, max_reach):
    exact_span = buckets // 2
    distance = np.arange(length)
    log_ratio = np.log(np.maximum(distance, exact_span) / exact_span) / np.log(
        max_reach / exact_span
    )
    coarse = exact_span + np.floor(log_ratio * (buckets - exact_span)).astype(np.int64)
    return np.where(distance < exact_span, distance, np.minimum(coarse, buckets - 1))


def nn(left, right, precision=None):
    return lax.dot_general(
        left, right, (((1,), (0,)), ((), ())), precision=precision, preferred_element_type=f32
    )


def nt(left, right):
    return lax.dot_general(left, right, (((1,), (1,)), ((), ())), preferred_element_type=f32)


def tn(left, right):
    return lax.dot_general(left, right, (((0,), (0,)), ((), ())), preferred_element_type=f32)


def iota(shape, axis):
    return lax.broadcasted_iota(jnp.int32, shape, axis)


def call(body, name, ids, outs, *args, scratch=(), limit=24, far=()):
    shapes = [jax.ShapeDtypeStruct(shape, dtype) for shape, dtype in outs]
    return pl.pallas_call(
        body,
        out_shape=shapes,
        in_specs=[pl.BlockSpec(memory_space=pltpu.SMEM)]
        + [
            pl.BlockSpec(memory_space=pltpu.HBM if i in far else pltpu.VMEM)
            for i in range(len(args))
        ],
        out_specs=[pl.BlockSpec(memory_space=pltpu.VMEM)] * len(outs),
        scratch_shapes=list(scratch),
        compiler_params=pltpu.CompilerParams(vmem_limit_bytes=limit << 20),
        cost_estimate=pl.CostEstimate(
            flops=0, transcendentals=0, bytes_accessed=int(microseconds.get(name, 0.8) * 3.6e6)
        ),
        name=name,
    )(
        ids,
        *[
            pltpu.with_memory_space_constraint(a, pltpu.HBM) if i in far else a
            for i, a in enumerate(args)
        ],
    )


def halves(value, t):
    width = value.shape[1] // 2
    low, high = value[:, :width], value[:, width:]
    even = t == 0
    return jnp.where(even, low, high), jnp.where(even, high, low)


def row_halves(value, t):
    width = value.shape[0] // 2
    low, high = value[:width], value[width:]
    even = t == 0
    return jnp.where(even, low, high), jnp.where(even, high, low)


def columns_of(row):
    length = row.shape[1]
    return jnp.broadcast_to(row.astype(f32), (length, length)).T


def sums_by_distance(square):
    length = square.shape[0]
    rows = length // 2
    while rows >= 1:
        square = square[:rows] + pltpu.roll(square[rows:], length - rows, 1)
        rows //= 2
    return square


def fetch(sources, targets, sems):
    copies = [
        pltpu.make_async_copy(source, target, sems.at[i])
        for i, (source, target) in enumerate(zip(sources, targets))
    ]
    for copy in copies:
        copy.start()
    return copies


def route_body(order, stride, ids, routes_far, cot_far, slots, *refs):
    experts = len(order)
    chunks, (routes, cot, sems) = refs[:experts], refs[experts:]
    copies = fetch((routes_far, cot_far), (routes, cot), sems)
    copies[0].wait()
    e, t = ids[0], ids[2]
    length = routes.shape[1]
    expert_row = iota((experts, length), 0)
    first = (expert_row == routes[0:1, :]).astype(f32)
    second = (expert_row == routes[1:2, :]).astype(f32)
    earlier = (iota((length, length), 0) < iota((length, length), 1)).astype(bf16)
    before = nn((first + second).astype(bf16), earlier)
    rank0 = jnp.sum(before * first, axis=0, keepdims=True).astype(jnp.int32)
    rank1 = jnp.sum(before * second, axis=0, keepdims=True).astype(jnp.int32)
    slot0 = (routes[0:1, :] ^ e) * stride + rank0
    slot1 = (routes[1:2, :] ^ e) * stride + rank1
    slots[0:1, :] = slot0
    slots[1:2, :] = slot1
    copies[1].wait()
    mine, _ = halves(cot[...], t)
    for s in range(experts):
        place = iota((stride, length), 0) + order[s] * stride
        pick = ((place == slot0) | (place == slot1)).astype(bf16)
        chunks[s][...] = nn(pick, mine).astype(bf16)


def front_body(ids, *refs):
    sources = refs[:9]
    early, part, q_out, k_out, v_out, probs = refs[9:15]
    targets, sems = refs[15:-1], refs[-1]
    tokens, gain, wq, wk, wv, rel, hot, seq, wo = targets
    copies = fetch(sources, targets, sems)
    t = ids[2]
    length = tokens.shape[0]
    mixed_out = early.at[pl.ds(length, length), :]
    copies[0].wait()
    copies[1].wait()
    wide = tokens[...].astype(f32)
    inv = lax.rsqrt(jnp.mean(wide * wide, axis=-1, keepdims=True) + eps_norm)
    value = (wide * inv * gain[...][None, :]).astype(bf16)
    early[pl.ds(0, length), :] = halves(value, t)[0]
    rows = length
    copies[2].wait()
    queries = nn(value, wq[...]).astype(bf16)
    copies[3].wait()
    keys = nn(value, wk[...]).astype(bf16)
    copies[4].wait()
    values = nn(value, wv[...]).astype(bf16)
    q_out[...] = queries
    k_out[...] = keys
    v_out[...] = values
    for copy in copies[5:8]:
        copy.wait()
    seq_cols = jnp.broadcast_to(seq[...].astype(f32), (rows, rows))
    allowed = (seq_cols == seq_cols.T) & (iota((rows, rows), 0) >= iota((rows, rows), 1))
    table = nn(rel[...], hot[...], lax.Precision.HIGHEST)
    lane = iota((rows, LANES), 1)
    pairs = [slice(i, i + LANES) for i in range(0, queries.shape[1], LANES)]
    heads = [(span, lane < HEAD_DIM if side == 0 else lane >= HEAD_DIM) for span in pairs for side in (0, 1)]
    raw = [
        nt(jnp.where(mine, queries[:, span], jnp.zeros((), bf16)), keys[:, span])
        for span, mine in heads
    ]
    biases = [
        pltpu.roll(
            jnp.broadcast_to(table[i : i + 1, :], (rows, rows)), 0, 1, stride=1, stride_axis=0
        )
        for i in range(len(heads))
    ]
    scores = [jnp.where(allowed, r * HEAD_DIM ** (-0.5) + b, -1e30) for r, b in zip(raw, biases)]
    tops = [jnp.max(x, axis=-1, keepdims=True) for x in scores]
    raised = [jnp.exp(x - top) for x, top in zip(scores, tops)]
    weights = [x / jnp.sum(x, axis=-1, keepdims=True) for x in raised]
    mixed = [nn(x.astype(bf16), values[:, span]) for x, (span, _) in zip(weights, heads)]
    for i, x in enumerate(weights):
        probs[i] = x
    for i, span in enumerate(pairs):
        mixed_out[:, span] = jnp.where(lane < HEAD_DIM, mixed[2 * i], mixed[2 * i + 1]).astype(bf16)
    copies[8].wait()
    part[...] = nn(mixed_out[...], wo[...])


def router_of(normed, weights_row):
    logits = nt(normed, weights_row)
    raised = jnp.exp(logits - jnp.max(logits, axis=-1, keepdims=True))
    return raised / jnp.sum(raised, axis=-1, keepdims=True)


def middle_body(order, stride, ids, own, other, tokens, gain, router, slots, residual, normed, probs, *chunks):
    t = ids[2]
    wide = tokens[...].astype(f32) + (own[...] + other[...])
    residual[...] = wide
    inv = lax.rsqrt(jnp.mean(wide * wide, axis=-1, keepdims=True) + eps_norm)
    value = (wide * inv * gain[...][None, :]).astype(bf16)
    normed[...] = value
    mine, _ = halves(value, t)
    length = slots.shape[1]
    for s in range(len(order)):
        place = iota((stride, length), 0) + order[s] * stride
        pick = ((place == slots[0:1, :]) | (place == slots[1:2, :])).astype(bf16)
        chunks[s][...] = nn(pick, mine).astype(bf16)
    probs[...] = router_of(value, router[...])


def join_body(ids, *refs):
    out = refs[-1]
    start = 0
    for ref in refs[:-1]:
        out[pl.ds(start, ref.shape[0]), :] = ref[...]
        start += ref.shape[0]


def in_order(own, other, even):
    return jnp.concatenate([jnp.where(even, own, other), jnp.where(even, other, own)], axis=1)


def expert_body(rows, ids, *refs):
    own, other = refs[:4], refs[4:8]
    w_in, w_out, act, slope, part_mine, part_other = refs[8:]
    t = ids[2]
    for p in range(4):
        span = pl.ds(p * rows, rows)
        pre = nn(in_order(own[p][...], other[p][...], t == 0), w_in[0])
        square = pre * pre
        bent = jnp.tanh(gelu_scale * (pre + 0.044715 * pre * square))
        half = 0.5 * (1.0 + bent)
        value = (pre * half).astype(bf16)
        act[span, :] = value
        slope[span, :] = half + 0.5 * pre * (1.0 - bent * bent) * (
            gelu_scale * (1.0 + 3 * 0.044715 * square)
        )
        mine, rest = halves(nn(value, w_out[0]).astype(bf16), t)
        part_mine[span, :] = mine
        part_other[span, :] = rest


def expert_back_body(rows, experts, ids, *refs):
    own, other, cot_own, cot_other = refs[:4], refs[4:8], refs[8:12], refs[12:16]
    w_in, w_out, router, slope, grad_pre, grads, back_mine, back_other = refs[16:]
    e, t = ids[0], ids[2]
    gates = []
    for p in range(4):
        logits = nt(in_order(own[p][...], other[p][...], t == 0), router[...])
        raised = jnp.exp(logits - jnp.max(logits, axis=-1, keepdims=True))
        chosen = jnp.where(iota(raised.shape, 1) == e, raised, 0.0)
        gates.append(
            jnp.sum(chosen, axis=-1, keepdims=True) / jnp.sum(raised, axis=-1, keepdims=True)
        )
    for p in range(4):
        span = pl.ds(p * rows, rows)
        cot_rows = pl.ds(0, rows)
        cot = in_order(cot_own[p][cot_rows, :], cot_other[p][cot_rows, :], t == 0)
        grad = (gates[p] * cot.astype(f32)).astype(bf16)
        grads[span, :] = grad
        value = (nt(grad, w_out[0]) * slope[span, :]).astype(bf16)
        grad_pre[span, :] = value
        mine, rest = halves(nt(value, w_in[0]).astype(bf16), t)
        back_mine[span, :] = mine
        back_other[span, :] = rest


def expert_grads_body(rows, ids, *refs):
    own, other = refs[:4], refs[4:8]
    act, grad_pre, grads, out_in, out_out = refs[8:]
    even = ids[2] == 0
    out_out[0] = tn(act[...], grads[...])
    sent = jnp.concatenate([in_order(own[p][...], other[p][...], even) for p in range(4)], axis=0)
    out_in[0] = tn(sent, grad_pre[...])


def pair_sum_body(ids, mine, received, keep, send):
    rows = mine.shape[0] // 4

    def block(p):
        q = (0, 2, 1, 3)[p]
        left = mine[pl.ds(p * rows, rows), :].astype(f32)
        return (left + received[pl.ds(q * rows, rows), :].astype(f32)).astype(bf16)

    keep[pl.ds(0, rows), :] = block(0)
    keep[pl.ds(rows, rows), :] = block(2)
    send[pl.ds(0, rows), :] = block(1)
    send[pl.ds(rows, rows), :] = block(3)


def plane_sum_body(ids, keep, received, kept, send):
    rows = keep.shape[0] // 2
    total = keep[...].astype(f32) + received[...].astype(f32)
    kept[...] = total[:rows]
    send[...] = total[rows:].astype(bf16)


def last_sum_body(experts, stride, ids, kept, received, kept_back, received_back, *chunks):
    first = (kept[...] + received[...].astype(f32)).astype(bf16)
    second = (kept_back[...] + received_back[...].astype(f32)).astype(bf16)
    for s in range(experts):
        chunks[s][pl.ds(0, stride), :] = first[s * stride : (s + 1) * stride]
        chunks[s][pl.ds(stride, stride), :] = second[s * stride : (s + 1) * stride]


def combine_body(order, stride, ids, *refs):
    experts = len(order)
    chunks = refs[:experts]
    slots, routes, probs, cot, residual, packed = refs[experts:]
    t = ids[2]
    length = slots.shape[1]
    probs_all = probs[...]
    choice = iota(probs_all.shape, 1)
    cot_mine = halves(cot[...], t)[0].astype(f32)
    mixture = None
    back = None
    lanes = iota((length, LANES), 1)
    dots = jnp.zeros((length, LANES), f32)
    for k in range(TOP):
        slot = columns_of(slots[k : k + 1, :])
        route = columns_of(routes[k : k + 1, :])[:, : probs_all.shape[1]]
        gate = jnp.sum(
            jnp.where(choice.astype(f32) == route, probs_all, 0.0), axis=-1, keepdims=True
        )
        chosen = None
        for s in range(experts):
            place = (iota((length, stride), 1) + order[s] * stride).astype(f32)
            pick = (place == slot[:, :1]).astype(bf16)
            value = nn(pick, chunks[s][pl.ds(0, stride), :])
            grad = nn(pick, chunks[s][pl.ds(stride, stride), :])
            chosen = value if chosen is None else chosen + value
            back = grad if back is None else back + grad
        mixture = gate * chosen if mixture is None else mixture + gate * chosen
        dots = jnp.where(lanes == k, jnp.sum(cot_mine * chosen, axis=-1, keepdims=True), dots)
    width = back.shape[1]
    packed[:, :width] = back
    packed[:, width : 2 * width] = halves(residual[...], t)[0] + mixture
    packed[:, 2 * width :] = dots


def norm_back_body(
    experts, ids, own, other, normed, probs, residual, routes, cot, gain, router, output, grad_out, att, small
):
    even = ids[2] == 0
    width = residual.shape[1] // 2
    first, last = slice(0, width), slice(width, 2 * width)
    low = jnp.where(even, own[:, first], other[:, first])
    high = jnp.where(even, other[:, first], own[:, first])
    back = jnp.concatenate([low, high], axis=1)
    output[:, first] = jnp.where(even, own[:, last], other[:, last]).astype(bf16)
    output[:, last] = jnp.where(even, other[:, last], own[:, last]).astype(bf16)
    dots = own[:, 2 * width :] + other[:, 2 * width :]
    probs_all = probs[...]
    choice = iota(probs_all.shape, 1).astype(f32)
    grad_probs = jnp.zeros_like(probs_all)
    for k in range(TOP):
        route = columns_of(routes[k : k + 1, :])[:, : probs_all.shape[1]]
        grad_probs = grad_probs + jnp.where(choice == route, dots[:, k : k + 1], 0.0)
    inner = jnp.sum(probs_all * grad_probs, axis=-1, keepdims=True)
    grad_logits = (probs_all * (grad_probs - inner)).astype(bf16)
    grad_normed = back + nn(grad_logits, router[...])
    wide = residual[...]
    inv = lax.rsqrt(jnp.mean(wide * wide, axis=-1, keepdims=True) + eps_norm)
    scaled = grad_normed * gain[...][None, :]
    grad = (
        cot[...].astype(f32)
        + inv * scaled
        - wide * (inv * inv * inv) * jnp.mean(scaled * wide, axis=-1, keepdims=True)
    )
    grad_out[...] = grad
    att[...] = grad.astype(bf16)
    small[0:1, :] = jnp.sum(grad_normed * wide * inv, axis=0, keepdims=True)
    small[pl.ds(1, experts), :] = tn(grad_logits, normed[...])


def attend_back_body(
    ids, att, wo, q_in, k_in, v_in, mixed_in, probs, wq, wk, wv, r0, r1, r2, r3, normed_part, bias, stack
):
    q_id, t = ids[1], ids[2]
    grad = att[...]
    rows = grad.shape[0]
    lane = iota((rows, LANES), 1)
    scale = HEAD_DIM ** (-0.5)
    pairs = [slice(i, i + LANES) for i in range(0, q_in.shape[1], LANES)]
    heads = [(i, lane < HEAD_DIM if side == 0 else lane >= HEAD_DIM) for i in range(len(pairs)) for side in (0, 1)]
    grad_mixed = [nt(grad, wo[span, :]).astype(bf16) for span in pairs]
    queries, keys, values = ([ref[:, span] for span in pairs] for ref in (q_in, k_in, v_in))
    mixed = [mixed_in[pl.ds(rows, rows), span].astype(f32) for span in pairs]
    weights = [probs[i] for i in range(len(heads))]
    parts = [jnp.where(mine, grad_mixed[i], jnp.zeros((), bf16)) for i, mine in heads]
    inner = [nt(part, values[i]) for part, (i, _) in zip(parts, heads)]
    deltas = [
        jnp.sum(part.astype(f32) * mixed[i], axis=-1, keepdims=True)
        for part, (i, _) in zip(parts, heads)
    ]
    scores = [w * (x - delta) for w, x, delta in zip(weights, inner, deltas)]
    half = [x.astype(bf16) for x in scores]
    dv = [tn(w.astype(bf16), grad_mixed[i]) for w, (i, _) in zip(weights, heads)]
    dq = [nn(x, keys[i]) for x, (i, _) in zip(half, heads)]
    dk = [tn(x, queries[i]) for x, (i, _) in zip(half, heads)]
    sums = [sums_by_distance(x) for x in scores]
    first = lane < HEAD_DIM
    for i, span in enumerate(pairs):
        stack[0, :, span] = (jnp.where(first, dq[2 * i], dq[2 * i + 1]) * scale).astype(bf16)
        stack[1, :, span] = (jnp.where(first, dk[2 * i], dk[2 * i + 1]) * scale).astype(bf16)
        stack[2, :, span] = jnp.where(first, dv[2 * i], dv[2 * i + 1]).astype(bf16)
    for i, row in enumerate(sums):
        bias[0:1, i * rows : (i + 1) * rows] = row
    stack[3] = halves(grad, t)[0]
    r0[...] = stack[q_id]
    r1[...] = stack[q_id ^ (1 + t)]
    r2[...] = stack[q_id ^ (2 - t)]
    r3[...] = stack[q_id ^ 3]
    total = nt(stack[0], wq[...]) + nt(stack[1], wk[...]) + nt(stack[2], wv[...])
    normed_part[...] = total.astype(bf16)


def tokens_back_body(experts, ids, own, other, tokens, gain, grad_res, small_ffn, bias, out, small):
    wide = tokens[...].astype(f32)
    inv = lax.rsqrt(jnp.mean(wide * wide, axis=-1, keepdims=True) + eps_norm)
    grad_normed = own[...].astype(f32) + other[...].astype(f32)
    scaled = grad_normed * gain[...][None, :]
    out[...] = (
        grad_res[...]
        + inv * scaled
        - wide * (inv * inv * inv) * jnp.mean(scaled * wide, axis=-1, keepdims=True)
    )
    small[...] = jnp.zeros_like(small)
    small[0:1, :] = jnp.sum(grad_normed * wide * inv, axis=0, keepdims=True)
    small[1:2, :] = bias[...]
    small[pl.ds(2, 1 + experts), :] = small_ffn[...]


def encode(value):
    width = value.shape[1] // 2
    tall = jnp.concatenate([value[:, :width], value[:, width:]], axis=0)
    lead = tall.astype(bf16)
    return lead, (tall - lead.astype(f32)).astype(bf16)


def decode(ref, start, rows):
    lead = ref[pl.ds(start, 2 * rows), :].astype(f32)
    return lead + ref[pl.ds(start + 2 * rows, 2 * rows), :].astype(f32)


def widen(tall):
    rows = tall.shape[0] // 2
    return jnp.concatenate([tall[:rows], tall[rows:]], axis=1)


def partial_body(order, ids, *refs):
    early_own, early_other = refs[:4], refs[4:8]
    right, right_pair, small = refs[8:12], refs[12:16], refs[16]
    blocks, total = refs[17:-1], refs[-1]
    e, q, t = ids[0], ids[1], ids[2]
    even = t == 0
    is_last = q == 3
    tokens = right[0].shape[0]
    rows = early_own[0].shape[0]
    width = early_own[0].shape[1]
    low, high, rights = [], [], []
    normed, mixed = pl.ds(rows - 2 * tokens, tokens), pl.ds(rows - tokens, tokens)
    for p in range(4):
        mine = jnp.where(is_last, right[p][...], early_own[p][normed, :])
        other = jnp.where(is_last, right_pair[p][...], early_other[p][normed, :])
        low.append(jnp.where(even, mine, other))
        high.append(jnp.where(even, other, mine))
        rights.append(jnp.where(is_last, early_own[p][mixed, :], right[p][...]))
    rights = jnp.concatenate(rights, axis=0)
    total[:width, :] = tn(jnp.concatenate(low, axis=0), rights)
    total[width:, :] = tn(jnp.concatenate(high, axis=0), rights)
    groups = len(order)
    depth = total.shape[0] // groups
    lead, rest = encode(small[...])
    for s in range(groups):
        start = pl.multiple_of((e ^ order[s]) * depth, 8)
        blocks[s][pl.ds(0, depth), :] = total[pl.ds(start, depth), :].astype(bf16)
        blocks[s][pl.ds(depth, lead.shape[0]), :] = lead
        blocks[s][pl.ds(depth + lead.shape[0], lead.shape[0]), :] = rest


def reduce_body(order, rows, ids, *refs):
    groups = len(order)
    arrived, outs = refs[:groups], refs[groups:]
    depth = outs[0].shape[0]
    total = arrived[0][pl.ds(0, depth), :].astype(f32)
    for ref in arrived[1:]:
        total = total + ref[pl.ds(0, depth), :].astype(f32)
    outs[0][...] = total.astype(bf16)
    code, stack = outs[1:]
    for s in range(groups):
        stack[order[s]] = decode(arrived[s], depth, rows)
    small = stack[ids[0]]
    for k in range(1, groups):
        small = small + stack[ids[0] ^ k]
    lead = small.astype(bf16)
    code[pl.ds(0, depth), :] = outs[0][...]
    code[pl.ds(depth, 2 * rows), :] = lead
    code[pl.ds(depth + 2 * rows, 2 * rows), :] = (small - lead.astype(f32)).astype(bf16)


def final_body(order, experts, rows, ids, *refs):
    groups = len(order)
    pieces, hot, outs = refs[:12], refs[12], refs[13:17]
    gain_attn, bias, gain_ffn, router = refs[17:21]
    square, small = refs[21:]
    e, q, t = ids[0], ids[1], ids[2]
    depth = square.shape[0] // groups

    def place_of(chip):
        away = q ^ chip
        return jnp.where((t == 1) & ((away == 1) | (away == 2)), 3 - away, away)

    for p in range(4):
        small[p] = decode(pieces[p], depth, rows)
    for m in range(4):
        out = outs[m] if m < 3 else square
        place = place_of(m)
        for p in range(4):

            @pl.when(place == p)
            def _(p=p, out=out):
                for s in range(groups):
                    start = pl.multiple_of((order[s] ^ e) * depth, 8)
                    step, at = (0, 0) if s == 0 else (2, 0) if s == groups - 1 else (1, s - 1)
                    piece = pieces[step * 4 + p]
                    out[pl.ds(start, depth), :] = piece[pl.ds(at * depth, depth), :].astype(f32)

    outs[3][...] = square[...].T
    total = widen(small[place_of(0)] + small[place_of(1)] + small[place_of(2)] + small[place_of(3)])
    gain_attn[...] = total[0]
    gain_ffn[...] = total[2]
    router[...] = total[3 : 3 + experts]
    length = hot.shape[1]
    for head in range(bias.shape[0]):
        line = jnp.broadcast_to(total[1:2, head * length : (head + 1) * length], (8, length))
        value = lax.dot_general(
            line,
            hot[...],
            (((1,), (1,)), ((), ())),
            precision=lax.Precision.HIGHEST,
            preferred_element_type=f32,
        )
        bias[head : head + 1, :] = value[0:1]


def on_device(
    n_dp,
    n_tensor,
    tokens,
    seq_ids,
    routes,
    gain_attn,
    w_query,
    w_key,
    w_value,
    w_attn_out,
    rel_bias,
    gain_ffn,
    w_router,
    expert_in,
    expert_out,
    cotangent,
):
    groups = n_dp // 4
    length, width = tokens.shape
    half = width // 2
    experts = w_router.shape[1]
    bucket_count = rel_bias.shape[1]
    heads = rel_bias.shape[0]
    local = w_query.shape[1]
    capacity = 4 * ((5 * TOP * length + 16 * experts - 1) // (16 * experts))
    stride = -(-capacity // 16) * 16
    slot_count = experts * stride
    dp_id = lax.axis_index("dp")
    t_id = lax.axis_index("tensor")
    ids = jnp.stack([dp_id // 4, dp_id % 4, t_id]).astype(jnp.int32)

    def send(array, target, only=None):
        pairs = []
        for dp in range(n_dp):
            for t in range(n_tensor):
                e_to, q_to, t_to = target(dp // 4, dp % 4, t)
                if only is None or q_to == only:
                    pairs.append((dp * n_tensor + t, (e_to * 4 + q_to) * n_tensor + t_to))
        return lax.ppermute(array, ("dp", "tensor"), pairs)

    def to_pair(e, q, t):
        return e, q, 1 - t

    def to_first(e, q, t):
        return e, q ^ (1 + t), t

    def to_second(e, q, t):
        return e, q ^ (2 - t), t

    def to_far(e, q, t):
        return e, q ^ 3, t

    def to_group(step):
        return lambda e, q, t: (e ^ step, q, t)

    order = (0, *range(groups // 2, groups), *range(1, groups // 2))
    last_order = (0, *range(groups // 2, groups - 1), *range(1, groups // 2), groups - 1)

    def exchange(chunks, order=order):
        return [chunks[0]] + [
            send(chunk, to_group(step)) for chunk, step in zip(chunks[1:], order[1:])
        ]

    def join(arrays):
        rows = sum(a.shape[0] for a in arrays)
        return call(join_body, "join", ids, [((rows, arrays[0].shape[1]), arrays[0].dtype)], *arrays)[0]

    def spread_first(block):
        return block, send(block, to_first), send(block, to_second)

    def spread_rest(block, first, second):
        own = [block, first, second, send(first, to_second)]
        other = [send(piece, to_pair) for piece in own]
        return own, [other[0], other[2], other[1], other[3]]

    routes_t = routes.T
    gain_one, gain_two = gain_attn, gain_ffn
    router_t = w_router.T
    distance_bucket = bucket_of_distance(length, bucket_count, REACH)
    hot = (
        distance_bucket[(-np.arange(length)) % length][None, :] == np.arange(bucket_count)[:, None]
    ).astype(np.float32)
    hot = jnp.asarray(hot)

    chunk = ((stride, half), bf16)
    local_out = ((length, local), bf16)
    slots, *cot_chunks = call(
        functools.partial(route_body, order, stride),
        "route",
        ids,
        [((TOP, length), jnp.int32)] + [chunk] * experts,
        routes_t,
        cotangent,
        scratch=[
            pltpu.VMEM((TOP, length), jnp.int32),
            pltpu.VMEM((length, width), bf16),
            pltpu.SemaphoreType.DMA((2,)),
        ],
        far=(0, 1),
    )
    cot_arrived = exchange(cot_chunks)
    early, att_part, queries, keys, values, probs = call(
        front_body,
        "front",
        ids,
        [((2 * length, half), bf16), ((length, width), f32)]
        + [local_out] * 3
        + [((heads, length, length), f32)],
        tokens,
        gain_one,
        w_query,
        w_key,
        w_value,
        rel_bias,
        hot,
        seq_ids.reshape(1, length),
        w_attn_out,
        scratch=[pltpu.VMEM((length, width), bf16), pltpu.VMEM((width,), f32)]
        + [pltpu.VMEM((width, local), bf16)] * 3
        + [
            pltpu.VMEM(rel_bias.shape, f32),
            pltpu.VMEM(hot.shape, f32),
            pltpu.VMEM((1, length), jnp.int32),
            pltpu.VMEM((local, width), bf16),
            pltpu.SemaphoreType.DMA((9,)),
        ],
        far=range(9),
    )
    att_part, *cot_arrived = lax.optimization_barrier((att_part, *cot_arrived))
    cot_near = spread_first(join(cot_arrived + [early]))
    att_other = send(att_part, to_pair)
    residual, normed_two, router_probs, *row_chunks = call(
        functools.partial(middle_body, order, stride),
        "middle",
        ids,
        [((length, width), f32), ((length, width), bf16), ((length, experts), f32)]
        + [chunk] * experts,
        att_part,
        att_other,
        tokens,
        gain_two,
        router_t,
        slots,
    )
    *row_arrived, near, next_near = lax.optimization_barrier((*exchange(row_chunks), *cot_near[1:]))
    row_own, row_other = spread_rest(*spread_first(join(row_arrived)))
    cot_own, cot_other = spread_rest(cot_near[0], near, next_near)

    all_rows = 4 * slot_count
    rows_half = ((all_rows, half), bf16)
    units = expert_in.shape[2]
    act, slope, part_mine, part_other = call(
        functools.partial(expert_body, slot_count),
        "expert",
        ids,
        [((all_rows, units), bf16), ((all_rows, units), f32), rows_half, rows_half],
        *row_own,
        *row_other,
        expert_in,
        expert_out,
        limit=40,
    )
    two = ((2 * slot_count, half), bf16)
    one = ((slot_count, half), bf16)
    one_wide = ((slot_count, half), f32)

    keep, go = call(pair_sum_body, "pair_sum", ids, [two, two], part_mine, send(part_other, to_pair))
    part_kept, go = call(
        plane_sum_body, "plane_sum", ids, [one_wide, one], keep, send(go, to_first)
    )
    part_last = send(go, to_second)
    grad_pre, expert_cot, back_mine, back_other = call(
        functools.partial(expert_back_body, slot_count, experts),
        "expert_back",
        ids,
        [((all_rows, units), bf16), ((all_rows, width), bf16), rows_half, rows_half],
        *row_own,
        *row_other,
        *cot_own,
        *cot_other,
        expert_in,
        expert_out,
        router_t,
        slope,
        limit=40,
    )
    keep, go = call(pair_sum_body, "pair_sum", ids, [two, two], back_mine, send(back_other, to_pair))
    back_kept, go = call(
        plane_sum_body, "plane_sum", ids, [one_wide, one], keep, send(go, to_first)
    )
    back_last = send(go, to_second)
    grad_in, grad_out = call(
        functools.partial(expert_grads_body, slot_count),
        "expert_grads",
        ids,
        [(expert_in.shape, f32), (expert_out.shape, f32)],
        *row_own,
        *row_other,
        act,
        grad_pre,
        expert_cot,
        limit=40,
    )
    part_last, back_last, grad_in, grad_out = lax.optimization_barrier(
        (part_last, back_last, grad_in, grad_out)
    )
    chunks = call(
        functools.partial(last_sum_body, experts, stride),
        "last_sum",
        ids,
        [((2 * stride, half), bf16)] * experts,
        part_kept,
        part_last,
        back_kept,
        back_last,
    )
    returned = exchange(chunks)
    packed = call(
        functools.partial(combine_body, order, stride),
        "combine",
        ids,
        [((length, width + LANES), f32)],
        *returned,
        slots,
        routes_t,
        router_probs,
        cotangent,
        residual,
    )[0]
    output, grad_residual, grad_att, small_ffn = call(
        functools.partial(norm_back_body, experts),
        "norm_back",
        ids,
        [
            ((length, width), bf16),
            ((length, width), f32),
            ((length, width), bf16),
            ((1 + experts, width), f32),
        ],
        packed,
        send(packed, to_pair),
        normed_two,
        router_probs,
        residual,
        routes_t,
        cotangent,
        gain_two,
        router_t,
    )
    right0, right1, right2, right3, normed_part, bias = call(
        attend_back_body,
        "attend_back",
        ids,
        [local_out] * 4 + [((length, width), bf16), ((1, heads * length), f32)],
        grad_att,
        w_attn_out,
        queries,
        keys,
        values,
        early,
        probs,
        w_query,
        w_key,
        w_value,
        scratch=[pltpu.VMEM((4, length, local), bf16)],
    )
    right_all = [right0, send(right1, to_first), send(right2, to_second), send(right3, to_far)]
    small_rows = -(-(3 + experts) // 8) * 8
    grad_tokens, small = call(
        functools.partial(tokens_back_body, experts),
        "tokens_back",
        ids,
        [((length, width), f32), ((small_rows, width), f32)],
        normed_part,
        send(normed_part, to_pair),
        tokens,
        gain_one,
        grad_residual,
        small_ffn,
        bias,
    )
    *right_all, small = lax.optimization_barrier((*right_all, small))
    right_pair = [send(right_all[p], to_pair) for p in (0, 2, 1, 3)]
    depth = width // groups
    blocks = call(
        functools.partial(partial_body, order),
        "partial",
        ids,
        [((depth + 4 * small_rows, local), bf16)] * groups,
        *cot_own,
        *cot_other,
        *right_all,
        *right_pair,
        small,
        scratch=[pltpu.VMEM((width, local), f32)],
    )
    reduced, code = call(
        functools.partial(reduce_body, order, small_rows),
        "reduce",
        ids,
        [((depth, local), bf16), ((depth + 4 * small_rows, local), bf16)],
        *exchange(blocks),
        scratch=[pltpu.VMEM((groups, 2 * small_rows, local), f32)],
    )
    spread = exchange([reduced] * groups, last_order)
    def near(matrix):
        return [matrix, send(matrix, to_first), send(matrix, to_second)]

    start = near(code)
    *joint, start[1] = lax.optimization_barrier((*spread[1:-1], start[1]))
    start.append(send(start[1], to_second))
    inner = near(join(joint))
    last, start[3] = lax.optimization_barrier((spread[-1], start[3]))
    inner.append(send(inner[1], to_second))
    final_pieces = start + inner + near(last) + [send(last, to_far)]
    grads = call(
        functools.partial(final_body, last_order, experts, small_rows),
        "final",
        ids,
        [((width, local), f32)] * 3
        + [((local, width), f32), ((width,), f32), ((heads, bucket_count), f32)]
        + [((width,), f32), ((experts, width), f32)],
        *final_pieces,
        hot,
        scratch=[
            pltpu.VMEM((width, local), f32),
            pltpu.VMEM((4, 2 * small_rows, local), f32),
        ],
        limit=40,
    )
    return (
        output,
        grad_tokens,
        grads[4],
        grads[0],
        grads[1],
        grads[2],
        grads[3],
        grads[5],
        grads[6],
        grads[7].T,
        grad_in,
        grad_out,
    )


def solution(mesh):
    in_specs = (
        P("dp", None),
        P("dp"),
        P("dp", None),
        P(),
        P(None, "tensor"),
        P(None, "tensor"),
        P(None, "tensor"),
        P("tensor", None),
        P("tensor", None),
        P(),
        P(),
        P("dp", None, "tensor"),
        P("dp", "tensor", None),
        P("dp", None),
    )
    out_specs = (
        P("dp", None),
        P("dp", None),
        P(),
        P(None, "tensor"),
        P(None, "tensor"),
        P(None, "tensor"),
        P("tensor", None),
        P("tensor", None),
        P(),
        P(),
        P("dp", None, "tensor"),
        P("dp", "tensor", None),
    )
    return jax.shard_map(
        functools.partial(on_device, mesh.shape["dp"], mesh.shape["tensor"]),
        mesh=mesh,
        in_specs=in_specs,
        out_specs=out_specs,
        check_vma=False,
    )
```
